128 devices in a mesh: gx: 16 (over y, z_hi, core), gy: 8 (over x, z_lo).
Axes of the slice: x: 4, y: 4, z: 4 (z_hi: 2, z_lo: 2; z = z_hi * 2 + z_lo), core: 2. Of those that a mesh axis runs over, the one named last changes fastest.
Arguments:
- saved_mid: bfloat16 [768, 256, 256], P('gx', 'gy'), may hold values from -6 to 6
- out_grad: bfloat16 [768, 256, 256], P('gx', 'gy'), may hold values from -6 to 6
- expert_weight: bfloat16 [10, 9, 256, 256], replicated, may hold values from -0.125 to 0.125
- routes: int32 [48, 16, 4], P('gx', 'gy'), may hold values from 0 to 7, all different within a row
- gates: float32 [48, 16, 6], P('gx', 'gy'), may hold values from 0.5 to 1.5
- band_matrix: bfloat16 [16, 256, 256], replicated, may hold values from -0.375 to 0.375
- band_ids: int32 [64, 32], replicated, may hold values from 0 to 15
Outputs:
- field_grad: bfloat16 [768, 256, 256], P('gx', 'gy')
The draws below stay inside these ranges and needn't reach their ends.
Inputs may be any that keep to these rules, and one draw needn't show every extreme that they name: `routes`: each tile names 4 different routed experts.
All inputs are finite; a program needn't handle non-finite values.
Results may differ from the reference program's by a relative error of at most 0.0095.
Values may be sent and summed in bfloat16 or wider, within the bound.
A program may use at most 128 MiB of HBM per device.

```python
import math
import jax
import jax.numpy as jnp
from jax import lax

CH = 256
ROUTED = 8
TOP = 4
SHARED = 2
TILE = 16
KH = 64
KW = 32
BANDS = 16
H = 768
W = 256
TR = 48
TC = 16
SLOTS = 6
EXPERTS = 10


def with_ends(array, key, smallest, largest):
    dims = array.shape
    place = [jax.random.randint(jax.random.fold_in(key, axis), (), 0, dims[axis]) for axis in range(len(dims))]
    array = array.at[tuple(place)].set(smallest)
    longest = dims.index(max(dims))
    place[longest] = (place[longest] + 1) % dims[longest]
    return array.at[tuple(place)].set(largest)


def block_levels(stream_key, dims, pieces, low, largest):
    factor_of = 1.0
    for position, blocks in pieces:
        heights = jax.random.uniform(jax.random.fold_in(jax.random.fold_in(stream_key, 6), position), (blocks,), jnp.float32, low / len(pieces), largest / len(pieces))
        factor_of = factor_of * jnp.repeat(jnp.exp(heights), dims[position] // blocks).reshape((-1,) + (1,) * (len(dims) - 1 - position))
    return factor_of


def picks_of(rng, rows, count, top, lift):
    order = jax.random.permutation(jax.random.fold_in(rng, 1), count)
    favour = order
    for power in range(3):
        favour = favour * favour // count
    favour = favour * lift // count
    tickets = jax.random.randint(jax.random.fold_in(rng, 2), (rows, count), 0, 4096) + favour
    fixed_rows = jax.random.permutation(jax.random.fold_in(rng, 3), rows)[jnp.arange(count) % rows]
    tickets = jnp.where(jnp.arange(rows)[:, None] == fixed_rows[None, :], 1 << 14, tickets)
    merit = tickets * count + jnp.arange(count)
    return lax.top_k(merit.astype(jnp.int32), top)[1].astype(jnp.int32)


def scatter_about(rng, shape, deviation, bound, cuts=(), kind=jnp.bfloat16):
    drawn = deviation * jax.random.normal(rng, shape, jnp.float32)
    if cuts:
        drawn = drawn * block_levels(rng, shape, cuts, -0.22, 0.18)
    return jnp.clip(drawn, -bound, bound).astype(kind)


def setup_inputs(seed: int = 0) -> dict:
    splits = jax.random.split(jax.random.key(seed), 8)
    return {
        "saved_mid": scatter_about(splits[0], (H, W, CH), 1.0, 6.0, ((0, 16), (1, 8))),
        "out_grad": scatter_about(splits[1], (H, W, CH), 1.0, 6.0, ((0, 16), (1, 8))),
        "expert_weight": scatter_about(splits[2], (EXPERTS, 9, CH, CH), (9 * CH) ** -0.5, 0.125),
        "routes": picks_of(splits[3], TR * TC, ROUTED, TOP, 8192).reshape((TR, TC, TOP)),
        "gates": jnp.clip(0.5 + 1.0 * jax.random.uniform(splits[4], (TR, TC, SLOTS), jnp.float32) ** block_levels(splits[4], (TR, TC, SLOTS), ((0, 16), (1, 8)), -0.2, 0.2), 0.5, 1.5),
        "band_matrix": scatter_about(splits[5], (BANDS, CH, CH), CH ** -0.5, 0.375),
        "band_ids": with_ends(jax.random.randint(splits[6], (KH, KW), 0, BANDS), jax.random.fold_in(splits[6], 1), 0, BANDS - 1).astype(jnp.int32),
    }


tap_offsets = ((-1, -1), (-1, 0), (-1, 1), (0, -1), (0, 0), (0, 1), (1, -1), (1, 0), (1, 1))

def gelu_slope(values):
    normal_cdf = 0.5 * (1.0 + lax.erf(values * 0.7071067811865476))
    density = jnp.exp(-0.5 * values * values) * 0.3989422804014327
    return normal_cdf + values * density

def angle_table(index, freq, period):
    product = index[:, None] * freq[None, :] % period
    theta = product.astype(jnp.float32) * (2.0 * math.pi / period)
    return (jnp.cos(theta), jnp.sin(theta))

def reference(saved_mid, out_grad, expert_weight, routes, gates, band_matrix, band_ids):
    highest = lax.Precision.HIGHEST
    padded_mid = jnp.pad(saved_mid, ((1, 1), (1, 1), (0, 0)))
    flat_weight = expert_weight.reshape(EXPERTS, 9 * CH, CH)
    zero = jnp.int32(0)

    def one_tile(tile_id):
        tile_row = tile_id // TC
        tile_col = tile_id % TC
        window = lax.dynamic_slice(padded_mid, (tile_row * TILE, tile_col * TILE, zero), (TILE + 2, TILE + 2, CH))
        gradient = lax.dynamic_slice(out_grad, (tile_row * TILE, tile_col * TILE, zero), (TILE, TILE, CH))
        gradient = gradient.reshape(TILE * TILE, CH).astype(jnp.float32)
        patches = jnp.stack([window[1 + row_off:1 + row_off + TILE, 1 + col_off:1 + col_off + TILE] for row_off, col_off in tap_offsets], axis=2)
        patches = patches.reshape(TILE * TILE, 9 * CH).astype(jnp.float32)
        chosen_ids = jnp.concatenate([jnp.arange(SHARED, dtype=jnp.int32), routes[tile_row, tile_col].astype(jnp.int32) + SHARED])
        chosen = jnp.take(flat_weight, chosen_ids, axis=0).astype(jnp.float32)
        preact = jnp.einsum('pk,sko->spo', patches, chosen, precision=highest)
        deltas = (gates[tile_row, tile_col][:, None, None] * gelu_slope(preact) * gradient[None]).astype(jnp.bfloat16)
        tap_tile = jnp.einsum('spo,sko->pk', deltas.astype(jnp.float32), chosen, precision=highest)
        return tap_tile.astype(jnp.bfloat16)
    tap_tiles = lax.map(one_tile, jnp.arange(TR * TC, dtype=jnp.int32))
    tap_field = tap_tiles.reshape(TR, TC, TILE, TILE, 9, CH).transpose(0, 2, 1, 3, 4, 5).reshape(H, W, 9, CH)
    grad_mid = out_grad.astype(jnp.float32)
    for tap_index, (row_off, col_off) in enumerate(tap_offsets):
        shifted = jnp.pad(tap_field[:, :, tap_index, :], ((1, 1), (1, 1), (0, 0)))
        grad_mid = grad_mid + shifted[1 - row_off:1 - row_off + H, 1 - col_off:1 - col_off + W].astype(jnp.float32)
    row_modes = jnp.arange(KH, dtype=jnp.int32)
    row_freq = jnp.where(row_modes < KH // 2, row_modes, H - KH + row_modes).astype(jnp.int32)
    row_cos, row_sin = angle_table(jnp.arange(H, dtype=jnp.int32), row_freq, H)
    col_cos, col_sin = angle_table(jnp.arange(W, dtype=jnp.int32), jnp.arange(KW, dtype=jnp.int32), W)
    half_cos = jnp.einsum('hwc,wn->hnc', grad_mid, col_cos, precision=highest)
    half_sin = jnp.einsum('hwc,wn->hnc', grad_mid, col_sin, precision=highest)
    analysis_scale = 1.0 / math.sqrt(H * W)
    coef_cos = (jnp.einsum('hm,hnc->mnc', row_cos, half_cos, precision=highest) - jnp.einsum('hm,hnc->mnc', row_sin, half_sin, precision=highest)) * analysis_scale
    coef_sin = (jnp.einsum('hm,hnc->mnc', row_sin, half_cos, precision=highest) + jnp.einsum('hm,hnc->mnc', row_cos, half_sin, precision=highest)) * analysis_scale
    coef_cos = coef_cos.astype(jnp.bfloat16).astype(jnp.float32)
    coef_sin = coef_sin.astype(jnp.bfloat16).astype(jnp.float32)
    one_hot = (band_ids[:, :, None] == jnp.arange(BANDS, dtype=jnp.int32)[None, None, :]).astype(jnp.float32)
    bands_f = band_matrix.astype(jnp.float32)
    spec_cos = lax.optimization_barrier(jnp.sum(jnp.einsum('mno,bio->mnbi', coef_cos, bands_f, precision=highest) * one_hot[:, :, :, None], axis=2))
    spec_sin = lax.optimization_barrier(jnp.sum(jnp.einsum('mno,bio->mnbi', coef_sin, bands_f, precision=highest) * one_hot[:, :, :, None], axis=2))
    spec_cos = spec_cos.astype(jnp.bfloat16).astype(jnp.float32)
    spec_sin = spec_sin.astype(jnp.bfloat16).astype(jnp.float32)
    z_cos = jnp.einsum('mnc,hm->hnc', spec_cos, row_cos, precision=highest) + jnp.einsum('mnc,hm->hnc', spec_sin, row_sin, precision=highest)
    z_sin = jnp.einsum('mnc,hm->hnc', spec_sin, row_cos, precision=highest) - jnp.einsum('mnc,hm->hnc', spec_cos, row_sin, precision=highest)
    spectral = jnp.einsum('hnc,wn->hwc', z_cos, col_cos, precision=highest) + jnp.einsum('hnc,wn->hwc', z_sin, col_sin, precision=highest)
    spectral = spectral / math.sqrt(2 * KH * KW)
    return (grad_mid + spectral).astype(jnp.bfloat16)
```

```python
import math

import jax
import jax.numpy as jnp
import numpy as np
from jax import lax
from jax.experimental import pallas as pl
from jax.experimental.pallas import tpu as pltpu
from jax.sharding import PartitionSpec as P

F32 = jnp.float32
BF = jnp.bfloat16
MESH = pl.DeviceIdType.MESH
GX, GY = 16, 8
ROWS, COLS, CH = 48, 32, 256
KH, KW = 64, 32
H, W = 768, 256
EXPERTS, SLOTS, TILES = 10, 6, 6

DIRS = ((1, 0), (-1, 0), (0, 1), (0, -1), (1, 1), (1, -1), (-1, 1), (-1, -1))


def mod(value, count):
    return lax.rem(value + count, count)


def tables():
    n = 4 * np.arange(8)[None, :] + np.arange(4)[:, None]
    theta = 2 * np.pi * ((n.reshape(-1)[:, None] * np.arange(W)[None, :]) % W) / W
    col = np.concatenate([np.cos(theta), np.sin(theta)])
    m = np.arange(KH)
    freq = np.where(m < KH // 2, m, H - KH + m)
    phase = 2 * np.pi * ((freq[:, None] * np.arange(H)[None, :]) % H) / H
    rc = np.cos(phase).reshape(2, 32, GX, ROWS)
    rs = np.sin(phase).reshape(2, 32, GX, ROWS)
    top = np.stack([rc, -rs], axis=3)
    bottom = np.stack([rs, rc], axis=3)
    row = np.stack([top, bottom], axis=1)
    row = row.transpose(3, 0, 1, 2, 4, 5).reshape(GX, 128, 2 * ROWS)
    return col, row


COL_TABLE, ROW_TABLE = tables()


def gelu_slope(values):
    normal_cdf = 0.5 * (1.0 + lax.erf(values * 0.7071067811865476))
    density = jnp.exp(-0.5 * values * values) * 0.3989422804014327
    return normal_cdf + values * density


def transpose_blocks(parts):
    lane = lax.broadcasted_iota(jnp.int32, parts[0].shape, parts[0].ndim - 1)
    axis = parts[0].ndim - 1
    low = lane < 64
    a, b, c, d = parts
    a, c = (
        jnp.where(low, a, pltpu.roll(c, 64, axis)),
        jnp.where(low, pltpu.roll(a, 64, axis), c),
    )
    b, d = (
        jnp.where(low, b, pltpu.roll(d, 64, axis)),
        jnp.where(low, pltpu.roll(b, 64, axis), d),
    )
    even = (lane & 32) == 0
    a, b = (
        jnp.where(even, a, pltpu.roll(b, 32, axis)),
        jnp.where(even, pltpu.roll(a, 96, axis), b),
    )
    c, d = (
        jnp.where(even, c, pltpu.roll(d, 32, axis)),
        jnp.where(even, pltpu.roll(c, 96, axis), d),
    )
    return a, b, c, d


def border_copies(gx, gy, sources, targets, send_sem, recv_sem):
    copies = []
    for k, (dr, dc) in enumerate(DIRS):
        copies.append(
            pltpu.make_async_remote_copy(
                src_ref=sources[k],
                dst_ref=targets[k],
                send_sem=send_sem.at[k],
                recv_sem=recv_sem.at[k],
                device_id=(mod(gx + dr, GX), mod(gy + dc, GY)),
                device_id_type=MESH,
            )
        )
    return copies


def greet(devices):
    barrier = pltpu.get_barrier_semaphore()
    for device in devices:
        pl.semaphore_signal(barrier, inc=1, device_id=device, device_id_type=MESH)
    pl.semaphore_wait(barrier, len(devices))


def neighbours(gx, gy):
    return [(mod(gx + dr, GX), mod(gy + dc, GY)) for dr, dc in DIRS]


def halo_body(mid, shifted, ext, ecol, ecor, rrow, rcol, rcor, side, ssem, rsem):
    gx, gy = lax.axis_index("gx"), lax.axis_index("gy")
    ext[1 : ROWS + 1] = mid[...].astype(F32)
    ecol[0] = ext[1 : ROWS + 1, COLS - 1, :].astype(BF)
    ecol[1] = ext[1 : ROWS + 1, 0, :].astype(BF)
    for k, (r, c) in enumerate(((ROWS, COLS - 1), (ROWS, 0), (1, COLS - 1), (1, 0))):
        ecor[k] = jnp.broadcast_to(ext[r, c : c + 1, :], (16, CH)).astype(BF)
    greet(neighbours(gx, gy))
    sources = [mid.at[ROWS - 1], mid.at[0], ecol.at[0], ecol.at[1]]
    sources += [ecor.at[k] for k in range(4)]
    targets = [rrow.at[0], rrow.at[1], rcol.at[0], rcol.at[1]]
    targets += [rcor.at[k] for k in range(4)]
    copies = border_copies(gx, gy, sources, targets, ssem, rsem)
    for copy in copies:
        copy.start()
    for copy in copies:
        copy.wait()
    above = jnp.where(gx > 0, 1.0, 0.0)
    below = jnp.where(gx < GX - 1, 1.0, 0.0)
    left = jnp.where(gy > 0, 1.0, 0.0)
    right = jnp.where(gy < GY - 1, 1.0, 0.0)
    ext[0] = rrow[0].astype(F32) * above
    ext[ROWS + 1] = rrow[1].astype(F32) * below
    side[0, 8 : 8 + ROWS] = rcol[0].astype(F32) * left
    side[1, 8 : 8 + ROWS] = rcol[1].astype(F32) * right
    side[0, 7:8] = rcor[0][0:1].astype(F32) * (above * left)
    side[1, 7:8] = rcor[1][0:1].astype(F32) * (above * right)
    side[0, 8 + ROWS : 9 + ROWS] = rcor[2][0:1].astype(F32) * (below * left)
    side[1, 8 + ROWS : 9 + ROWS] = rcor[3][0:1].astype(F32) * (below * right)
    place = lax.broadcasted_iota(jnp.int32, (COLS, CH), 0)

    def one_row(r, _):
        row = ext[r]
        before = side[0, pl.ds(r + 7, 1), :]
        after = side[1, pl.ds(r + 7, 1), :]
        shifted[1, r] = row.astype(BF)
        shifted[0, r] = jnp.where(place == 0, before, pltpu.roll(row, 1, 0)).astype(BF)
        shifted[2, r] = jnp.where(place == COLS - 1, after, pltpu.roll(row, COLS - 1, 0)).astype(BF)
        return 0

    lax.fori_loop(0, ROWS + 2, one_row, 0, unroll=5)


def tile_body(routes, gates, shifted, grad, w_hbm, spread, w, deltas, pre_a, pre_b, wsem):
    copies = [pltpu.make_async_copy(w_hbm.at[e], w.at[e], wsem.at[e]) for e in range(EXPERTS)]
    for copy in copies:
        copy.start()

    def expert(t, s):
        route = routes[t // 2, t % 2, jnp.maximum(s - 2, 0)]
        return jnp.where(s < 2, s, route + 2)

    def window(t):
        return t // 2, pl.ds(pl.multiple_of((t % 2) * 16, 16), 16)

    def forward(i, out):
        s, t = i // TILES, i % TILES
        rt, cols = window(t)
        pieces = [
            shifted[b, pl.ds(rt * 16 + a, 16), cols, :].reshape(256, CH)
            for a in range(3)
            for b in range(3)
        ]
        out[...] = jnp.dot(
            jnp.concatenate(pieces, axis=1), w[expert(t, s)], preferred_element_type=F32
        )

    def slope(i, src):
        s, t = i // TILES, i % TILES
        rt, cols = window(t)
        g = grad[pl.ds(rt * 16, 16), cols, :].reshape(256, CH).astype(F32)
        deltas[t, s] = (gates[rt, t % 2, s] * gelu_slope(src[...]) * g).astype(BF)

    copies[0].wait()
    copies[1].wait()
    forward(0, pre_a)

    def step(k, _):
        i = 2 * k
        forward(i + 1, pre_b)
        slope(i, pre_a)
        forward(i + 2, pre_a)
        slope(i + 1, pre_b)
        return 0

    lax.fori_loop(0, 5, step, 0)
    forward(11, pre_b)
    slope(10, pre_a)
    for copy in copies[2:]:
        copy.wait()
    forward(12, pre_a)
    slope(11, pre_b)
    lax.fori_loop(6, 17, step, 0)
    forward(35, pre_b)
    slope(34, pre_a)
    slope(35, pre_b)
    spread[...] = jnp.zeros_like(spread)

    def backward(t, _):
        rt, cols = window(t)
        d = jnp.concatenate([deltas[t, s] for s in range(SLOTS)], axis=1)
        chosen = [expert(t, s) for s in range(SLOTS)]
        for a in range(3):
            for b in range(3):
                tap = 3 * a + b
                kernels = jnp.concatenate(
                    [w[e, tap * CH : (tap + 1) * CH, :] for e in chosen], axis=1
                )
                r = lax.dot_general(
                    d, kernels, (((1,), (1,)), ((), ())), preferred_element_type=F32
                )
                spread[b, pl.ds(rt * 16 + a, 16), cols, :] += r.reshape(16, 16, CH)
        return 0

    lax.fori_loop(0, TILES, backward, 0)


def spectral_body(
    spread, grad, col, col_t, row, row_t, band_hbm, band_ids, out,
    total, erow, ecol, ecor, rrow, rcol, rcor,
    xs, xr, half, cs, cr, cg, sp, zs, fs, fr, band,
    border_s, border_r, x_s, x_r, c_s, c_r, g_s, g_r, p_s, p_r, f_s, f_r, band_sem,
):
    gx, gy = lax.axis_index("gx"), lax.axis_index("gy")
    band_copy = pltpu.make_async_copy(
        band_hbm.at[:, pl.ds(pl.multiple_of(gy * 32, 32), 32), :], band, band_sem
    )
    band_copy.start()
    place = lax.broadcasted_iota(jnp.int32, (COLS, CH), 0)

    def joined(r):
        ahead = jnp.where(place > 0, pltpu.roll(spread[2, r], 1, 0), 0.0)
        behind = jnp.where(place < COLS - 1, pltpu.roll(spread[0, r], COLS - 1, 0), 0.0)
        return spread[1, r] + ahead + behind

    erow[0] = joined(ROWS + 1).astype(BF)
    erow[1] = joined(0).astype(BF)
    ecol[0] = spread[2, 1 : ROWS + 1, COLS - 1, :].astype(BF)
    ecol[1] = spread[0, 1 : ROWS + 1, 0, :].astype(BF)
    for k, (b, r, c) in enumerate(
        ((2, ROWS + 1, COLS - 1), (0, ROWS + 1, 0), (2, 0, COLS - 1), (0, 0, 0))
    ):
        ecor[k] = jnp.broadcast_to(spread[b, r, c : c + 1, :], (16, CH)).astype(BF)
    others_y = [(gx, mod(gy + d, GY)) for d in range(1, GY)]
    others_x = [(mod(gx + d, GX), gy) for d in range(1, GX)]
    greet(others_y + others_x + neighbours(gx, gy)[4:])
    sources = [erow.at[0], erow.at[1], ecol.at[0], ecol.at[1]]
    sources += [ecor.at[k] for k in range(4)]
    targets = [rrow.at[0], rrow.at[1], rcol.at[0], rcol.at[1]]
    targets += [rcor.at[k] for k in range(4)]
    copies = border_copies(gx, gy, sources, targets, border_s, border_r)
    for copy in copies:
        copy.start()

    def own_row(r, _):
        total[r] = joined(r + 1) + grad[r].astype(F32)
        return 0

    lax.fori_loop(0, ROWS, own_row, 0, unroll=4)
    for copy in copies:
        copy.wait()
    above = jnp.where(gx > 0, 1.0, 0.0)
    below = jnp.where(gx < GX - 1, 1.0, 0.0)
    left = jnp.where(gy > 0, 1.0, 0.0)
    right = jnp.where(gy < GY - 1, 1.0, 0.0)
    total[0] += rrow[0].astype(F32) * above
    total[ROWS - 1] += rrow[1].astype(F32) * below
    total[:, 0, :] += rcol[0].astype(F32) * left
    total[:, COLS - 1, :] += rcol[1].astype(F32) * right
    total[0, 0:1, :] += rcor[0][0:1].astype(F32) * (above * left)
    total[0, COLS - 1 : COLS, :] += rcor[1][0:1].astype(F32) * (above * right)
    total[ROWS - 1, 0:1, :] += rcor[2][0:1].astype(F32) * (below * left)
    total[ROWS - 1, COLS - 1 : COLS, :] += rcor[3][0:1].astype(F32) * (below * right)

    def along_y(source, target, d, send, recv):
        return pltpu.make_async_remote_copy(
            src_ref=source,
            dst_ref=target,
            send_sem=send.at[d],
            recv_sem=recv.at[d],
            device_id=(gx, mod(gy + d, GY)),
            device_id_type=MESH,
        )

    def along_x(source, target, d, send, recv):
        return pltpu.make_async_remote_copy(
            src_ref=source,
            dst_ref=target,
            send_sem=send.at[d],
            recv_sem=recv.at[d],
            device_id=(mod(gx + d, GX), gy),
            device_id_type=MESH,
        )

    def split_rows(g, _):
        for jt in range(2):
            lanes = slice(jt * 128, jt * 128 + 128)
            parts = [total[4 * g + q, :, lanes] for q in range(4)]
            for s, part in enumerate(transpose_blocks(parts)):
                xs[jt * 4 + s, g] = part.astype(BF)
        return 0

    lax.fori_loop(0, 12, split_rows, 0, unroll=2)
    for d in range(1, GY):
        along_y(xs.at[mod(gy + d, GY)], xr.at[gy], d, x_s, x_r).start()
    xr[gy] = xs[gy]
    for d in range(1, GY):
        along_y(xs.at[mod(gy + d, GY)], xr.at[mod(gy - d, GY)], d, x_s, x_r).wait()

    for pair in range(6):
        data = jnp.concatenate(
            [xr[:, 2 * pair + k].reshape(256, 128) for k in range(2)], axis=1
        )
        c = jnp.dot(col[...], data, preferred_element_type=F32)
        for k in range(2):
            g = 2 * pair + k
            for part in range(2):
                parts = [
                    c[part * 32 + 8 * p : part * 32 + 8 * p + 8, k * 128 : k * 128 + 128]
                    for p in range(4)
                ]
                for q, block in enumerate(transpose_blocks(parts)):
                    half[pl.ds(part * ROWS + 4 * g + q, 8, stride=2 * ROWS), :] = block
    forward_scale = 1.0 / math.sqrt(H * W)
    for pair in range(4):
        data = jnp.concatenate(
            [half[(2 * pair + k) * 96 : (2 * pair + k + 1) * 96].astype(BF) for k in range(2)],
            axis=1,
        )
        c = jnp.dot(row[gx], data, preferred_element_type=F32) * forward_scale
        for k in range(2):
            for mh in range(2):
                cs[mh * 8 + 2 * pair + k] = c[
                    mh * 64 : mh * 64 + 64, k * 128 : k * 128 + 128
                ].astype(BF)
    for d in range(1, GX):
        along_x(cs.at[mod(gx + d, GX)], cr.at[gx], d, c_s, c_r).start()
    cr[gx] = cs[gx]
    for d in range(1, GX):
        along_x(cs.at[mod(gx + d, GX)], cr.at[mod(gx - d, GX)], d, c_s, c_r).wait()
    coef = cr[0].astype(F32)
    for k in range(1, GX):
        coef = coef + cr[k].astype(F32)
    cg[gy] = coef.astype(BF)
    for d in range(1, GY):
        along_y(cg.at[gy], cg.at[gy], d, g_s, g_r).start()
    band_copy.wait()
    for d in range(1, GY):
        along_y(cg.at[gy], cg.at[mod(gy - d, GY)], d, g_s, g_r).wait()

    inputs = []
    for jt in range(2):
        parts = [cg[jt * 4 + p].astype(F32) for p in range(4)]
        inputs.append(transpose_blocks(parts))
    n8 = lax.rem(gx, 8)
    mh = gx // 8
    ids = band_ids[pl.ds(pl.multiple_of(mh * 32, 32), 32), :]
    column = lax.broadcasted_iota(jnp.int32, (32, KW), 1)
    block_of_lane = lax.broadcasted_iota(jnp.int32, (64, 512), 1) >> 5
    lane_block = lax.broadcasted_iota(jnp.int32, (64, 128), 1) >> 5
    mixer = band[...].reshape(512, CH)
    spec = jnp.zeros((64, 128), F32)
    for n4 in range(4):
        modes = jnp.concatenate([inputs[0][n4], inputs[1][n4]], axis=1).astype(BF)
        z = lax.dot_general(
            modes, mixer, (((1,), (1,)), ((), ())), preferred_element_type=F32
        )
        mine = jnp.sum(jnp.where(column == 4 * n8 + n4, ids, 0), axis=1, keepdims=True)
        mine = jnp.concatenate([mine, mine], axis=0)
        z = jnp.where(block_of_lane == mine, z, 0.0)
        y = z[:, 0:128] + z[:, 128:256] + z[:, 256:384] + z[:, 384:512]
        y = y + pltpu.roll(y, 64, 1)
        y = y + pltpu.roll(y, 32, 1)
        spec = jnp.where(lane_block == n4, y, spec)
    sp[gx] = spec.astype(BF)
    for d in range(1, GX):
        along_x(sp.at[gx], sp.at[gx], d, p_s, p_r).start()
    for d in range(1, GX):
        along_x(sp.at[gx], sp.at[mod(gx - d, GX)], d, p_s, p_r).wait()

    inverse_scale = 1.0 / math.sqrt(2 * KH * KW)
    for pair in range(4):
        data = jnp.concatenate(
            [
                jnp.concatenate([sp[2 * pair + k], sp[8 + 2 * pair + k]], axis=0)
                for k in range(2)
            ],
            axis=1,
        )
        z = jnp.dot(row_t[gx], data, preferred_element_type=F32) * inverse_scale
        for k in range(2):
            zs[(2 * pair + k) * 96 : (2 * pair + k + 1) * 96, :] = z[:, k * 128 : k * 128 + 128]
    for pair in range(6):
        columns = []
        for k in range(2):
            g = 2 * pair + k
            pieces = []
            for part in range(2):
                parts = [
                    zs[pl.ds(part * ROWS + 4 * g + q, 8, stride=2 * ROWS), :] for q in range(4)
                ]
                pieces += list(transpose_blocks(parts))
            columns.append(jnp.concatenate(pieces, axis=0))
        data = jnp.concatenate(columns, axis=1).astype(BF)
        f = jnp.dot(col_t[...], data, preferred_element_type=F32)
        for k in range(2):
            for j in range(8):
                fs[j, 2 * pair + k] = f[j * 32 : j * 32 + 32, k * 128 : k * 128 + 128].astype(BF)
    for d in range(1, GY):
        along_y(fs.at[mod(gy + d, GY)], fr.at[gy], d, f_s, f_r).start()
    fr[gy] = fs[gy]
    for d in range(1, GY):
        along_y(fs.at[mod(gy + d, GY)], fr.at[mod(gy - d, GY)], d, f_s, f_r).wait()

    def join_rows(g, _):
        for jt in range(2):
            lanes = slice(jt * 128, jt * 128 + 128)
            parts = [fr[jt * 4 + s, g].astype(F32) for s in range(4)]
            for q, part in enumerate(transpose_blocks(parts)):
                out[4 * g + q, :, lanes] = (total[4 * g + q, :, lanes] + part).astype(BF)
        return 0

    lax.fori_loop(0, 12, join_rows, 0, unroll=2)


VMEM = pl.BlockSpec(memory_space=pltpu.VMEM)
SMEM = pl.BlockSpec(memory_space=pltpu.SMEM)
ANY = pl.BlockSpec(memory_space=pl.ANY)


def dma(count):
    return pltpu.SemaphoreType.DMA((count,))


BORDER_SCRATCH = [
    pltpu.VMEM((2, COLS, CH), BF),
    pltpu.VMEM((2, ROWS, CH), BF),
    pltpu.VMEM((4, 16, CH), BF),
]


def body(saved_mid, out_grad, expert_weight, routes, gates, band_matrix, band_ids):
    shifted = pl.pallas_call(
        halo_body,
        name="halo",
        out_shape=jax.ShapeDtypeStruct((3, ROWS + 2, COLS, CH), BF),
        in_specs=[VMEM],
        out_specs=VMEM,
        scratch_shapes=[
            pltpu.VMEM((ROWS + 2, COLS, CH), F32),
            pltpu.VMEM((2, ROWS, CH), BF),
            pltpu.VMEM((4, 16, CH), BF),
            *BORDER_SCRATCH,
            pltpu.VMEM((2, 64, CH), F32),
            dma(8),
            dma(8),
        ],
        compiler_params=pltpu.CompilerParams(collective_id=0, has_side_effects=True),
    )(saved_mid)
    spread = pl.pallas_call(
        tile_body,
        name="tiles",
        out_shape=jax.ShapeDtypeStruct((3, ROWS + 2, COLS, CH), F32),
        in_specs=[SMEM, SMEM, VMEM, VMEM, ANY],
        out_specs=VMEM,
        scratch_shapes=[
            pltpu.VMEM((EXPERTS, 9 * CH, CH), BF),
            pltpu.VMEM((TILES, SLOTS, 256, CH), BF),
            pltpu.VMEM((256, CH), F32),
            pltpu.VMEM((256, CH), F32),
            dma(EXPERTS),
        ],
        compiler_params=pltpu.CompilerParams(vmem_limit_bytes=56 * 2**20),
    )(routes, gates, shifted, out_grad, expert_weight.reshape(EXPERTS, 9 * CH, CH))
    col = jnp.asarray(COL_TABLE, BF)
    row = jnp.asarray(ROW_TABLE, BF)
    return pl.pallas_call(
        spectral_body,
        name="spectral",
        out_shape=jax.ShapeDtypeStruct((ROWS, COLS, CH), BF),
        in_specs=[VMEM] * 6 + [ANY, VMEM],
        out_specs=VMEM,
        scratch_shapes=[
            pltpu.VMEM((ROWS, COLS, CH), F32),
            pltpu.VMEM((2, COLS, CH), BF),
            pltpu.VMEM((2, ROWS, CH), BF),
            pltpu.VMEM((4, 16, CH), BF),
            *BORDER_SCRATCH,
            pltpu.VMEM((GY, 12, 32, 128), BF),
            pltpu.VMEM((GY, 12, 32, 128), BF),
            pltpu.VMEM((8 * 96, 128), F32),
            pltpu.VMEM((GX, 64, 128), BF),
            pltpu.VMEM((GX, 64, 128), BF),
            pltpu.VMEM((GY, 64, 128), BF),
            pltpu.VMEM((GX, 64, 128), BF),
            pltpu.VMEM((8 * 96, 128), F32),
            pltpu.VMEM((GY, 12, 32, 128), BF),
            pltpu.VMEM((GY, 12, 32, 128), BF),
            pltpu.VMEM((16, 32, CH), BF),
            dma(8), dma(8), dma(GY), dma(GY), dma(GX), dma(GX), dma(GY), dma(GY),
            dma(GX), dma(GX), dma(GY), dma(GY), pltpu.SemaphoreType.DMA,
        ],
        compiler_params=pltpu.CompilerParams(
            collective_id=1, has_side_effects=True, vmem_limit_bytes=56 * 2**20
        ),
    )(
        spread, out_grad, col, jnp.asarray(COL_TABLE.T, BF), row,
        jnp.asarray(ROW_TABLE.transpose(0, 2, 1), BF), band_matrix, band_ids,
    )


def solution(mesh):
    placed = (
        P("gx", "gy", None),
        P("gx", "gy", None),
        P(),
        P("gx", "gy", None),
        P("gx", "gy", None),
        P(),
        P(),
    )
    return jax.shard_map(
        body, mesh=mesh, in_specs=placed, out_specs=P("gx", "gy", None), check_vma=False
    )
```

```python
import math

import jax
import jax.numpy as jnp
import numpy as np
from jax import lax
from jax.experimental import pallas as pl
from jax.experimental.pallas import tpu as pltpu
from jax.sharding import PartitionSpec as P

F32 = jnp.float32
BF = jnp.bfloat16
MESH = pl.DeviceIdType.MESH
GX, GY = 16, 8
ROWS, COLS, CH = 48, 32, 256
KH, KW = 64, 32
H, W = 768, 256
EXPERTS, SLOTS, TILES = 10, 6, 6
OPEN = ROWS + 4
CHUNKS = ((0, 4, 0), (4, 4, 144), (8, 5, 288))

DIRS = ((1, 0), (-1, 0), (0, 1), (0, -1), (1, 1), (1, -1), (-1, 1), (-1, -1))


def mod(value, count):
    return lax.rem(value + count, count)


def tables():
    n = (4 * np.arange(8)[None, :] + np.arange(4)[:, None]).reshape(-1)

    def wave(columns):
        theta = 2 * np.pi * ((n[:, None] * columns[None, :]) % W) / W
        return np.concatenate([np.cos(theta), np.sin(theta)])

    col = wave(np.arange(W))
    edge = np.zeros((5, 64, GY, 16))
    for j in range(GY):
        for side, column in enumerate((COLS * j - 1, COLS * j + COLS)):
            if 0 <= column < W:
                for g in range(5):
                    edge[g, :, j, side * 8 + g] = wave(np.array([column]))[:, 0]
    m = np.arange(KH)
    freq = np.where(m < KH // 2, m, H - KH + m)
    row = np.zeros((GX, 2, 2, 32, 2, OPEN))
    for gx in range(GX):
        h = ROWS * gx - 1 + np.arange(OPEN)
        phase = 2 * np.pi * ((freq[:, None] * h[None, :]) % H) / H
        keep = (h >= 0) & (h < H) & (np.arange(OPEN) < ROWS + 2)
        rc = (np.cos(phase) * keep).reshape(2, 32, OPEN)
        rs = (np.sin(phase) * keep).reshape(2, 32, OPEN)
        row[gx, :, 0, :, 0], row[gx, :, 0, :, 1] = rc, -rs
        row[gx, :, 1, :, 0], row[gx, :, 1, :, 1] = rs, rc
    back = row[..., 1 : ROWS + 1].reshape(GX, 128, 2 * ROWS).transpose(0, 2, 1)
    return col, edge.reshape(320, 128), row.reshape(GX, 128, 2 * OPEN), back


COL_TABLE, EDGE_TABLE, ROW_TABLE, BACK_TABLE = tables()


def gelu_slope_twice(values):
    density = jnp.exp2((values * values) * (-0.5 * math.log2(math.e)))
    return (1.0 + lax.erf(values * math.sqrt(0.5))) + (values * math.sqrt(2.0 / math.pi)) * density


def transpose_blocks(parts):
    lane = lax.broadcasted_iota(jnp.int32, parts[0].shape, parts[0].ndim - 1)
    axis = parts[0].ndim - 1
    low = lane < 64
    a, b, c, d = parts
    a, c = (
        jnp.where(low, a, pltpu.roll(c, 64, axis)),
        jnp.where(low, pltpu.roll(a, 64, axis), c),
    )
    b, d = (
        jnp.where(low, b, pltpu.roll(d, 64, axis)),
        jnp.where(low, pltpu.roll(b, 64, axis), d),
    )
    even = (lane & 32) == 0
    a, b = (
        jnp.where(even, a, pltpu.roll(b, 32, axis)),
        jnp.where(even, pltpu.roll(a, 96, axis), b),
    )
    c, d = (
        jnp.where(even, c, pltpu.roll(d, 32, axis)),
        jnp.where(even, pltpu.roll(c, 96, axis), d),
    )
    return a, b, c, d


def border_copies(gx, gy, sources, targets, send_sem, recv_sem):
    copies = []
    for k, (dr, dc) in enumerate(DIRS):
        copies.append(
            pltpu.make_async_remote_copy(
                src_ref=sources[k],
                dst_ref=targets[k],
                send_sem=send_sem.at[k],
                recv_sem=recv_sem.at[k],
                device_id=(mod(gx + dr, GX), mod(gy + dc, GY)),
                device_id_type=MESH,
            )
        )
    return copies


def fused_body(
    mid, grad_hbm, w_hbm, routes, gates, band_hbm, band_ids, col, col_t, edge_table, row_hbm, back_hbm,
    out,
    grad, w, row, back, band, ext, shifted, side, deltas, spread, total, edge, edges,
    erow, ecol, ecor, rrow, rcol, rcor, brow, bcol, bcor, hrow, hcol, hcor,
    xs, xr, half, cs, cr, cg, sp, zs, fs, fr,
    w_sem, in_sem, halo_s, halo_r, border_s, border_r,
    x_s, x_r, c_s, c_r, g_s, g_r, p_s, p_r, f_s, f_r,
):
    gx, gy = lax.axis_index("gx"), lax.axis_index("gy")
    w_copies = [pltpu.make_async_copy(w_hbm.at[e], w.at[e], w_sem.at[e]) for e in range(EXPERTS)]
    in_copies = [
        pltpu.make_async_copy(grad_hbm, grad, in_sem.at[0]),
        pltpu.make_async_copy(row_hbm.at[gx], row, in_sem.at[1]),
        pltpu.make_async_copy(back_hbm.at[gx], back, in_sem.at[2]),
        pltpu.make_async_copy(
            band_hbm.at[:, pl.ds(pl.multiple_of(gy * 32, 32), 32), :], band, in_sem.at[3]
        ),
    ]
    w_copies[0].start()
    in_copies[0].start()
    for copy in w_copies[1:] + in_copies[1:]:
        copy.start()
    barrier = pltpu.get_barrier_semaphore()
    partners = [(gx, mod(gy + d, GY)) for d in range(1, GY)]
    partners += [(mod(gx + d, GX), gy) for d in range(1, GX)]
    partners += [(mod(gx + dr, GX), mod(gy + dc, GY)) for dr, dc in DIRS[4:]]
    for device in partners:
        pl.semaphore_signal(barrier, inc=1, device_id=device, device_id_type=MESH)

    above = jnp.where(gx > 0, 1.0, 0.0)
    below = jnp.where(gx < GX - 1, 1.0, 0.0)
    left = jnp.where(gy > 0, 1.0, 0.0)
    right = jnp.where(gy < GY - 1, 1.0, 0.0)

    ext[1 : ROWS + 1] = mid[...].astype(F32)
    hcol[0] = ext[1 : ROWS + 1, COLS - 1, :].astype(BF)
    hcol[1] = ext[1 : ROWS + 1, 0, :].astype(BF)
    for k, (r, c) in enumerate(((ROWS, COLS - 1), (ROWS, 0), (1, COLS - 1), (1, 0))):
        hcor[k] = jnp.broadcast_to(ext[r, c : c + 1, :], (16, CH)).astype(BF)
    pl.semaphore_wait(barrier, len(partners))
    halo = border_copies(
        gx, gy,
        [mid.at[ROWS - 1], mid.at[0], hcol.at[0], hcol.at[1]] + [hcor.at[k] for k in range(4)],
        [rrow.at[0], rrow.at[1], rcol.at[0], rcol.at[1]] + [rcor.at[k] for k in range(4)],
        halo_s, halo_r,
    )
    for copy in halo:
        copy.start()
    spread[...] = jnp.zeros_like(spread)
    edges[...] = jnp.zeros_like(edges)
    for copy in halo:
        copy.wait()
    ext[0] = rrow[0].astype(F32) * above
    ext[ROWS + 1] = rrow[1].astype(F32) * below
    side[0, 8 : 8 + ROWS] = rcol[0].astype(F32) * left
    side[1, 8 : 8 + ROWS] = rcol[1].astype(F32) * right
    side[0, 7:8] = rcor[0][0:1].astype(F32) * (above * left)
    side[1, 7:8] = rcor[1][0:1].astype(F32) * (above * right)
    side[0, 8 + ROWS : 9 + ROWS] = rcor[2][0:1].astype(F32) * (below * left)
    side[1, 8 + ROWS : 9 + ROWS] = rcor[3][0:1].astype(F32) * (below * right)
    place = lax.broadcasted_iota(jnp.int32, (COLS, CH), 0)

    def shift_row(r, _):
        line = ext[r]
        before = side[0, pl.ds(r + 7, 1), :]
        after = side[1, pl.ds(r + 7, 1), :]
        shifted[1, r] = line.astype(BF)
        shifted[0, r] = jnp.where(place == 0, before, pltpu.roll(line, 1, 0)).astype(BF)
        shifted[2, r] = jnp.where(place == COLS - 1, after, pltpu.roll(line, COLS - 1, 0)).astype(BF)
        return 0

    lax.fori_loop(0, ROWS + 2, shift_row, 0, unroll=5)

    def expert(t, s):
        return routes[t // 2, t % 2, s - 2] + 2

    def forward(s, kernel_of):
        for t in range(TILES):
            rt, cols = t // 2, slice((t % 2) * 16, (t % 2) * 16 + 16)
            pieces = [
                shifted[b, rt * 16 + a : rt * 16 + a + 16, cols, :].reshape(256, CH)
                for a in range(3)
                for b in range(3)
            ]
            pre = jnp.dot(
                jnp.concatenate(pieces, axis=1), w[kernel_of(t, s)], preferred_element_type=F32
            )
            g = grad[rt * 16 : rt * 16 + 16, cols, :].reshape(256, CH).astype(F32)
            gate = gates[rt, t % 2, s] * 0.5
            deltas[t, s] = (gelu_slope_twice(pre) * (g * gate)).astype(BF)

    def forward_shared(s, _):
        forward(s, lambda t, s: s)
        return 0

    def forward_routed(s, _):
        forward(s, expert)
        return 0

    in_copies[0].wait()
    w_copies[0].wait()
    w_copies[1].wait()
    lax.fori_loop(0, 2, forward_shared, 0)
    for copy in w_copies[2:]:
        copy.wait()
    lax.fori_loop(2, SLOTS, forward_routed, 0)

    def along_y(source, target, d, send, recv):
        return pltpu.make_async_remote_copy(
            src_ref=source, dst_ref=target, send_sem=send, recv_sem=recv,
            device_id=(gx, mod(gy + d, GY)), device_id_type=MESH,
        )

    def along_x(source, target, d, send, recv):
        return pltpu.make_async_remote_copy(
            src_ref=source, dst_ref=target, send_sem=send, recv_sem=recv,
            device_id=(mod(gx + d, GX), gy), device_id_type=MESH,
        )

    def backward(t, _):
        rt, cols = t // 2, pl.ds(pl.multiple_of((t % 2) * 16, 16), 16)
        d = jnp.concatenate([deltas[t, s] for s in range(SLOTS)], axis=1)
        chosen = [0, 1] + [expert(t, s) for s in range(2, SLOTS)]
        for a in range(3):
            for b in range(3):
                tap = 3 * a + b
                kernels = jnp.concatenate(
                    [w[e, tap * CH : (tap + 1) * CH, :] for e in chosen], axis=1
                )
                r = lax.dot_general(
                    d, kernels, (((1,), (1,)), ((), ())), preferred_element_type=F32
                )
                spread[b, pl.ds(rt * 16 + a, 16), cols, :] += r.reshape(16, 16, CH)
        return 0

    def joined(r):
        ahead = jnp.where(place > 0, pltpu.roll(spread[2, r], 1, 0), 0.0)
        behind = jnp.where(place < COLS - 1, pltpu.roll(spread[0, r], COLS - 1, 0), 0.0)
        return spread[1, r] + ahead + behind

    def x_copies(chunk, target):
        _, groups, start = CHUNKS[chunk]
        rows = slice(start, start + groups * 32 + 16)
        return [
            along_y(
                xs.at[mod(gy + d, GY), rows], xr.at[target(d), rows], d,
                x_s.at[chunk, d], x_r.at[chunk, d],
            )
            for d in range(1, GY)
        ]

    for chunk, (first, groups, start) in enumerate(CHUNKS):
        lax.fori_loop(2 * chunk, 2 * chunk + 2, backward, 0)

        def split_group(k, _):
            g = first + k
            for q in range(4):
                r = 4 * g + q
                keep = jnp.where((r >= 1) & (r <= ROWS), 1.0, 0.0)
                field = grad[jnp.clip(r - 1, 0, ROWS - 1)].astype(F32)
                total[r] = joined(r) + field * keep
            for jt in range(2):
                lanes = slice(jt * 128, jt * 128 + 128)
                parts = [total[4 * g + q, :, lanes] for q in range(4)]
                for s, part in enumerate(transpose_blocks(parts)):
                    rows = pl.ds(pl.multiple_of(start + 32 * k, 16), 32)
                    xs[jt * 4 + s, rows, :] = part.astype(BF)
            return 0

        lax.fori_loop(0, groups, split_group, 0)
        rows = slice(4 * first, 4 * first + 4 * groups)
        for jt in range(2):
            lanes = slice(jt * 128, jt * 128 + 128)
            edge[0, jt, rows] = spread[0, rows, 0, lanes]
            edge[1, jt, rows] = spread[2, rows, COLS - 1, lanes]
            for q in range(4):
                for s in range(2):
                    edges[q, jt, s * 8 : s * 8 + groups] = edge[
                        s, jt, pl.ds(4 * first + q, groups, stride=4), :
                    ]
            for s, part in enumerate(transpose_blocks([edges[q, jt] for q in range(4)])):
                last = start + groups * 32
                xs[jt * 4 + s, last : last + 16, :] = part.astype(BF)
        for copy in x_copies(chunk, lambda d: gy):
            copy.start()

    erow[0] = total[ROWS + 1].astype(BF)
    erow[1] = total[0].astype(BF)
    for jt in range(2):
        lanes = slice(jt * 128, jt * 128 + 128)
        ecol[0, :, lanes] = edge[1, jt, 1 : ROWS + 1].astype(BF)
        ecol[1, :, lanes] = edge[0, jt, 1 : ROWS + 1].astype(BF)
        for k, (s, r) in enumerate(((1, ROWS + 1), (0, ROWS + 1), (1, 0), (0, 0))):
            ecor[k, :, lanes] = jnp.broadcast_to(edge[s, jt, r : r + 1, :], (16, 128)).astype(BF)
    border = border_copies(
        gx, gy,
        [erow.at[0], erow.at[1], ecol.at[0], ecol.at[1]] + [ecor.at[k] for k in range(4)],
        [brow.at[0], brow.at[1], bcol.at[0], bcol.at[1]] + [bcor.at[k] for k in range(4)],
        border_s, border_r,
    )
    for copy in border:
        copy.start()
    xr[gy] = xs[gy]

    for chunk, (first, groups, start) in enumerate(CHUNKS):
        for copy in x_copies(chunk, lambda d: mod(gy - d, GY)):
            copy.wait()
        last = start + groups * 32
        rim = jnp.dot(
            edge_table[0 : groups * 64],
            xr[:, last : last + 16].reshape(128, 128),
            preferred_element_type=F32,
        )
        for pair in range(0, groups, 2):
            width = min(2, groups - pair)
            data = [
                xr[:, start + 32 * (pair + k) : start + 32 * (pair + k) + 32].reshape(256, 128)
                for k in range(width)
            ]
            c = jnp.dot(col[...], jnp.concatenate(data, axis=1), preferred_element_type=F32)
            for k in range(width):
                one = c[:, k * 128 : k * 128 + 128] + rim[(pair + k) * 64 : (pair + k) * 64 + 64]
                for part in range(2):
                    parts = [one[part * 32 + 8 * p : part * 32 + 8 * p + 8] for p in range(4)]
                    for q, block in enumerate(transpose_blocks(parts)):
                        r = part * OPEN + 4 * (first + pair + k) + q
                        half[pl.ds(r, 8, stride=2 * OPEN), :] = block
    forward_scale = 1.0 / math.sqrt(H * W)
    in_copies[1].wait()
    for pair in range(4):
        data = [
            half[(2 * pair + k) * 2 * OPEN : (2 * pair + k + 1) * 2 * OPEN].astype(BF)
            for k in range(2)
        ]
        c = jnp.dot(row[...], jnp.concatenate(data, axis=1), preferred_element_type=F32)
        c = (c * forward_scale).astype(BF)
        for k in range(2):
            for mh in range(2):
                cs[mh * 8 + 2 * pair + k] = c[mh * 64 : mh * 64 + 64, k * 128 : k * 128 + 128]
    for d in range(1, GX):
        along_x(cs.at[mod(gx + d, GX)], cr.at[gx], d, c_s.at[d], c_r.at[d]).start()
    cr[gx] = cs[gx]

    for copy in border:
        copy.wait()
    total[1] += brow[0].astype(F32) * above
    total[ROWS] += brow[1].astype(F32) * below
    own = slice(1, ROWS + 1)
    total[own, 0, :] += bcol[0].astype(F32) * left
    total[own, COLS - 1, :] += bcol[1].astype(F32) * right
    total[1, 0:1, :] += bcor[0][0:1].astype(F32) * (above * left)
    total[1, COLS - 1 : COLS, :] += bcor[1][0:1].astype(F32) * (above * right)
    total[ROWS, 0:1, :] += bcor[2][0:1].astype(F32) * (below * left)
    total[ROWS, COLS - 1 : COLS, :] += bcor[3][0:1].astype(F32) * (below * right)

    for d in range(1, GX):
        along_x(
            cs.at[mod(gx + d, GX)], cr.at[mod(gx - d, GX)], d, c_s.at[d], c_r.at[d]
        ).wait()
    coef = cr[0].astype(F32)
    for k in range(1, GX):
        coef = coef + cr[k].astype(F32)
    cg[gy] = coef.astype(BF)
    for d in range(1, GY):
        along_y(cg.at[gy], cg.at[gy], d, g_s.at[d], g_r.at[d]).start()
    in_copies[2].wait()
    in_copies[3].wait()
    for d in range(1, GY):
        along_y(cg.at[gy], cg.at[mod(gy - d, GY)], d, g_s.at[d], g_r.at[d]).wait()

    inputs = [
        transpose_blocks([cg[jt * 4 + p].astype(F32) for p in range(4)]) for jt in range(2)
    ]
    n8 = lax.rem(gx, 8)
    mh = gx // 8
    lane64 = lax.broadcasted_iota(jnp.int32, (32, KH), 1)
    row64 = lax.broadcasted_iota(jnp.int32, (32, KH), 0)
    block_of_lane = lax.broadcasted_iota(jnp.int32, (64, 512), 1) >> 5
    lane_block = lax.broadcasted_iota(jnp.int32, (64, 128), 1) >> 5
    mixer = band[...].reshape(512, CH)
    spec = jnp.zeros((64, 128), F32)
    for n4 in range(4):
        modes = jnp.concatenate([inputs[0][n4], inputs[1][n4]], axis=1).astype(BF)
        z = lax.dot_general(
            modes, mixer, (((1,), (1,)), ((), ())), preferred_element_type=F32
        )
        ids = jnp.broadcast_to(band_ids[pl.ds(4 * n8 + n4, 1), :], (32, KH))
        mine = jnp.sum(jnp.where(lane64 == row64 + 32 * mh, ids, 0), axis=1, keepdims=True)
        mine = jnp.concatenate([mine, mine], axis=0)
        z = jnp.where(block_of_lane == mine, z, 0.0)
        y = z[:, 0:128] + z[:, 128:256] + z[:, 256:384] + z[:, 384:512]
        y = y + pltpu.roll(y, 64, 1)
        y = y + pltpu.roll(y, 32, 1)
        spec = jnp.where(lane_block == n4, y, spec)
    sp[gx] = spec.astype(BF)
    for d in range(1, GX):
        along_x(sp.at[gx], sp.at[gx], d, p_s.at[d], p_r.at[d]).start()
    for d in range(1, GX):
        along_x(sp.at[gx], sp.at[mod(gx - d, GX)], d, p_s.at[d], p_r.at[d]).wait()

    inverse_scale = 1.0 / math.sqrt(2 * KH * KW)
    for pair in range(4):
        data = [
            jnp.concatenate([sp[2 * pair + k], sp[8 + 2 * pair + k]], axis=0) for k in range(2)
        ]
        z = jnp.dot(back[...], jnp.concatenate(data, axis=1), preferred_element_type=F32)
        z = z * inverse_scale
        for k in range(2):
            zs[(2 * pair + k) * 96 : (2 * pair + k + 1) * 96, :] = z[:, k * 128 : k * 128 + 128]

    def f_copies(third, target):
        rows = slice(4 * third, 4 * third + 4)
        return [
            along_y(
                fs.at[mod(gy + d, GY), rows], fr.at[target(d), rows], d,
                f_s.at[third, d], f_r.at[third, d],
            )
            for d in range(1, GY)
        ]

    for third in range(3):
        for pair in range(2 * third, 2 * third + 2):
            columns = []
            for k in range(2):
                pieces = []
                for part in range(2):
                    r = part * ROWS + 4 * (2 * pair + k)
                    parts = [zs[pl.ds(r + q, 8, stride=2 * ROWS), :] for q in range(4)]
                    pieces += list(transpose_blocks(parts))
                columns.append(jnp.concatenate(pieces, axis=0))
            data = jnp.concatenate(columns, axis=1).astype(BF)
            f = jnp.dot(col_t[...], data, preferred_element_type=F32).astype(BF)
            for k in range(2):
                for j in range(GY):
                    fs[j, 2 * pair + k] = f[j * 32 : j * 32 + 32, k * 128 : k * 128 + 128]
        for copy in f_copies(third, lambda d: gy):
            copy.start()
    fr[gy] = fs[gy]

    def join_group(g, _):
        for jt in range(2):
            lanes = slice(jt * 128, jt * 128 + 128)
            parts = [fr[jt * 4 + s, g].astype(F32) for s in range(4)]
            for q, part in enumerate(transpose_blocks(parts)):
                out[4 * g + q, :, lanes] = (total[4 * g + q + 1, :, lanes] + part).astype(BF)
        return 0

    for third in range(3):
        for copy in f_copies(third, lambda d: mod(gy - d, GY)):
            copy.wait()
        lax.fori_loop(4 * third, 4 * third + 4, join_group, 0, unroll=2)


VMEM = pl.BlockSpec(memory_space=pltpu.VMEM)
SMEM = pl.BlockSpec(memory_space=pltpu.SMEM)
ANY = pl.BlockSpec(memory_space=pl.ANY)


def dma(*shape):
    return pltpu.SemaphoreType.DMA(shape)


def border(count=1):
    one = [
        pltpu.VMEM((2, COLS, CH), BF),
        pltpu.VMEM((2, ROWS, CH), BF),
        pltpu.VMEM((4, 16, CH), BF),
    ]
    return one * count


def body(saved_mid, out_grad, expert_weight, routes, gates, band_matrix, band_ids):
    return pl.pallas_call(
        fused_body,
        name="fused",
        out_shape=jax.ShapeDtypeStruct((ROWS, COLS, CH), BF),
        in_specs=[VMEM, ANY, ANY, SMEM, SMEM, ANY, VMEM, VMEM, VMEM, VMEM, ANY, ANY],
        out_specs=VMEM,
        scratch_shapes=[
            pltpu.VMEM((ROWS, COLS, CH), BF),
            pltpu.VMEM((EXPERTS, 9 * CH, CH), BF),
            pltpu.VMEM((128, 2 * OPEN), BF),
            pltpu.VMEM((2 * ROWS, 128), BF),
            pltpu.VMEM((16, 32, CH), BF),
            pltpu.VMEM((ROWS + 2, COLS, CH), F32),
            pltpu.VMEM((3, ROWS + 2, COLS, CH), BF),
            pltpu.VMEM((2, 64, CH), F32),
            pltpu.VMEM((TILES, SLOTS, 256, CH), BF),
            pltpu.VMEM((3, OPEN, COLS, CH), F32),
            pltpu.VMEM((OPEN, COLS, CH), F32),
            pltpu.VMEM((2, 2, OPEN + 4, 128), F32),
            pltpu.VMEM((4, 2, 16, 128), F32),
            *border(4),
            pltpu.VMEM((GY, 464, 128), BF),
            pltpu.VMEM((GY, 464, 128), BF),
            pltpu.VMEM((8 * 2 * OPEN, 128), F32),
            pltpu.VMEM((GX, 64, 128), BF),
            pltpu.VMEM((GX, 64, 128), BF),
            pltpu.VMEM((GY, 64, 128), BF),
            pltpu.VMEM((GX, 64, 128), BF),
            pltpu.VMEM((8 * 2 * ROWS, 128), F32),
            pltpu.VMEM((GY, 12, 32, 128), BF),
            pltpu.VMEM((GY, 12, 32, 128), BF),
            dma(EXPERTS), dma(4), dma(8), dma(8), dma(8), dma(8),
            dma(3, GY), dma(3, GY), dma(GX), dma(GX), dma(GY), dma(GY),
            dma(GX), dma(GX), dma(3, GY), dma(3, GY),
        ],
        compiler_params=pltpu.CompilerParams(
            collective_id=0, has_side_effects=True, vmem_limit_bytes=60 * 2**20
        ),
    )(
        saved_mid, out_grad, expert_weight.reshape(EXPERTS, 9 * CH, CH), routes, gates,
        band_matrix, band_ids.T, jnp.asarray(COL_TABLE, BF), jnp.asarray(COL_TABLE.T, BF),
        jnp.asarray(EDGE_TABLE, BF), jnp.asarray(ROW_TABLE, BF), jnp.asarray(BACK_TABLE, BF),
    )


def solution(mesh):
    placed = (
        P("gx", "gy", None),
        P("gx", "gy", None),
        P(),
        P("gx", "gy", None),
        P("gx", "gy", None),
        P(),
        P(),
    )
    return jax.shard_map(
        body, mesh=mesh, in_specs=placed, out_specs=P("gx", "gy", None), check_vma=False
    )
```

```python
import math

import jax
import jax.numpy as jnp
import numpy as np
from jax import lax
from jax.experimental import pallas as pl
from jax.experimental.pallas import tpu as pltpu
from jax.sharding import PartitionSpec as P

F32 = jnp.float32
BF = jnp.bfloat16
MESH = pl.DeviceIdType.MESH
GX, GY = 16, 8
ROWS, COLS, CH = 48, 32, 256
KH, KW = 64, 32
H, W = 768, 256
EXPERTS, SLOTS, TILES = 10, 6, 6
OPEN = ROWS + 4
CHUNKS = ((0, 4, 0), (4, 4, 144), (8, 5, 288))

DIRS = ((1, 0), (-1, 0), (0, 1), (0, -1), (1, 1), (1, -1), (-1, 1), (-1, -1))


def mod(value, count):
    return lax.rem(value + count, count)


def tables():
    n = (4 * np.arange(8)[None, :] + np.arange(4)[:, None]).reshape(-1)

    def wave(columns):
        theta = 2 * np.pi * ((n[:, None] * columns[None, :]) % W) / W
        return np.concatenate([np.cos(theta), np.sin(theta)])

    opened = np.zeros((64, 2, GY, 16))
    edge = np.zeros((5, 64, GY, 16))
    for j in range(GY):
        for part in range(2):
            columns = COLS * j + 16 * part - 1 + np.arange(16)
            opened[:, part, j] = wave(columns) * (columns >= 0)
        for side, column in enumerate((COLS * j + COLS - 1, COLS * j + COLS)):
            if column < W:
                for g in range(5):
                    edge[g, :, j, side * 8 + g] = wave(np.array([column]))[:, 0]
    m = np.arange(KH)
    freq = np.where(m < KH // 2, m, H - KH + m)
    row = np.zeros((GX, 2, 2, 32, 2, OPEN))
    for gx in range(GX):
        h = ROWS * gx - 1 + np.arange(OPEN)
        phase = 2 * np.pi * ((freq[:, None] * h[None, :]) % H) / H
        keep = (h >= 0) & (h < H) & (np.arange(OPEN) < ROWS + 2)
        rc = (np.cos(phase) * keep).reshape(2, 32, OPEN)
        rs = (np.sin(phase) * keep).reshape(2, 32, OPEN)
        row[gx, :, 0, :, 0], row[gx, :, 0, :, 1] = rc, -rs
        row[gx, :, 1, :, 0], row[gx, :, 1, :, 1] = rs, rc
    back = row[..., 1 : ROWS + 1].reshape(GX, 128, 2 * ROWS).transpose(0, 2, 1)
    row = row.reshape(GX, 128, 2 * OPEN)
    return opened.reshape(64, 256), wave(np.arange(W)).T, edge.reshape(320, 128), row, back


OPEN_TABLE, COL_TABLE, EDGE_TABLE, ROW_TABLE, BACK_TABLE = tables()


def gelu_slope_twice(values):
    density = jnp.exp2((values * values) * (-0.5 * math.log2(math.e)))
    return (1.0 + lax.erf(values * math.sqrt(0.5))) + (values * math.sqrt(2.0 / math.pi)) * density


def transpose_blocks(parts):
    lane = lax.broadcasted_iota(jnp.int32, parts[0].shape, parts[0].ndim - 1)
    axis = parts[0].ndim - 1
    low = lane < 64
    a, b, c, d = parts
    a, c = (
        jnp.where(low, a, pltpu.roll(c, 64, axis)),
        jnp.where(low, pltpu.roll(a, 64, axis), c),
    )
    b, d = (
        jnp.where(low, b, pltpu.roll(d, 64, axis)),
        jnp.where(low, pltpu.roll(b, 64, axis), d),
    )
    even = (lane & 32) == 0
    a, b = (
        jnp.where(even, a, pltpu.roll(b, 32, axis)),
        jnp.where(even, pltpu.roll(a, 96, axis), b),
    )
    c, d = (
        jnp.where(even, c, pltpu.roll(d, 32, axis)),
        jnp.where(even, pltpu.roll(c, 96, axis), d),
    )
    return a, b, c, d


def border_copies(gx, gy, sources, targets, send_sem, recv_sem):
    copies = []
    for k, (dr, dc) in enumerate(DIRS):
        copies.append(
            pltpu.make_async_remote_copy(
                src_ref=sources[k],
                dst_ref=targets[k],
                send_sem=send_sem.at[k],
                recv_sem=recv_sem.at[k],
                device_id=(mod(gx + dr, GX), mod(gy + dc, GY)),
                device_id_type=MESH,
            )
        )
    return copies


def fused_body(
    mid_hbm, grad_hbm, w_hbm, routes, gates, band_hbm, band_ids,
    col_hbm, col_t_hbm, edge_hbm, row_hbm, back_hbm,
    out,
    mid, grad, w, row, back, band, col, col_t, edge_table, ext, shifted, side, deltas, spread, total, edge, edges, left_edge,
    erow, ecol, ecor, rrow, rcol, rcor, brow, bcol, bcor, hrow, hcol, hcor,
    xs, xr, half, cs, cr, cg, sp, zs, fs, fr,
    w_sem, in_sem, halo_s, halo_r, border_s, border_r,
    x_s, x_r, c_s, c_r, g_s, g_r, p_s, p_r, f_s, f_r,
):
    gx, gy = lax.axis_index("gx"), lax.axis_index("gy")
    w_copies = [pltpu.make_async_copy(w_hbm.at[e], w.at[e], w_sem.at[e]) for e in range(EXPERTS)]
    sources = [
        mid_hbm, grad_hbm, row_hbm.at[gx], back_hbm.at[gx],
        band_hbm.at[:, pl.ds(pl.multiple_of(gy * 32, 32), 32), :],
        col_hbm, col_t_hbm, edge_hbm,
    ]
    targets = [mid, grad, row, back, band, col, col_t, edge_table]
    in_copies = [
        pltpu.make_async_copy(source, target, in_sem.at[k])
        for k, (source, target) in enumerate(zip(sources, targets))
    ]
    for copy in in_copies[:1] + w_copies[:1] + in_copies[1:2] + w_copies[1:] + in_copies[2:]:
        copy.start()
    barrier = pltpu.get_barrier_semaphore()
    partners = [(gx, mod(gy + d, GY)) for d in range(1, GY)]
    partners += [(mod(gx + d, GX), gy) for d in range(1, GX)]
    partners += [(mod(gx + dr, GX), mod(gy + dc, GY)) for dr, dc in DIRS[4:]]
    for device in partners:
        pl.semaphore_signal(barrier, inc=1, device_id=device, device_id_type=MESH)

    above = jnp.where(gx > 0, 1.0, 0.0)
    below = jnp.where(gx < GX - 1, 1.0, 0.0)
    left = jnp.where(gy > 0, 1.0, 0.0)
    right = jnp.where(gy < GY - 1, 1.0, 0.0)

    in_copies[0].wait()
    ext[1 : ROWS + 1] = mid[...].astype(F32)
    hcol[0] = ext[1 : ROWS + 1, COLS - 1, :].astype(BF)
    hcol[1] = ext[1 : ROWS + 1, 0, :].astype(BF)
    for k, (r, c) in enumerate(((ROWS, COLS - 1), (ROWS, 0), (1, COLS - 1), (1, 0))):
        hcor[k] = jnp.broadcast_to(ext[r, c : c + 1, :], (16, CH)).astype(BF)
    pl.semaphore_wait(barrier, len(partners))
    halo = border_copies(
        gx, gy,
        [mid.at[ROWS - 1], mid.at[0], hcol.at[0], hcol.at[1]] + [hcor.at[k] for k in range(4)],
        [rrow.at[0], rrow.at[1], rcol.at[0], rcol.at[1]] + [rcor.at[k] for k in range(4)],
        halo_s, halo_r,
    )
    for copy in halo:
        copy.start()
    in_copies[1].wait()
    for b in (0, 2):
        spread[b] = jnp.zeros((OPEN, COLS, CH), F32)
    spread[1, 0] = jnp.zeros((COLS, CH), F32)
    spread[1, 1 : ROWS + 1] = grad[...].astype(F32)
    spread[1, ROWS + 1 :] = jnp.zeros((OPEN - ROWS - 1, COLS, CH), F32)
    edges[...] = jnp.zeros_like(edges)
    for copy in halo:
        copy.wait()
    ext[0] = rrow[0].astype(F32) * above
    ext[ROWS + 1] = rrow[1].astype(F32) * below
    side[0, 8 : 8 + ROWS] = rcol[0].astype(F32) * left
    side[1, 8 : 8 + ROWS] = rcol[1].astype(F32) * right
    side[0, 7:8] = rcor[0][0:1].astype(F32) * (above * left)
    side[1, 7:8] = rcor[1][0:1].astype(F32) * (above * right)
    side[0, 8 + ROWS : 9 + ROWS] = rcor[2][0:1].astype(F32) * (below * left)
    side[1, 8 + ROWS : 9 + ROWS] = rcor[3][0:1].astype(F32) * (below * right)
    place = lax.broadcasted_iota(jnp.int32, (COLS, CH), 0)

    def shift_row(r, _):
        line = ext[r]
        before = side[0, pl.ds(r + 7, 1), :]
        after = side[1, pl.ds(r + 7, 1), :]
        shifted[1, r] = line.astype(BF)
        shifted[0, r] = jnp.where(place == 0, before, pltpu.roll(line, 1, 0)).astype(BF)
        shifted[2, r] = jnp.where(place == COLS - 1, after, pltpu.roll(line, COLS - 1, 0)).astype(BF)
        return 0

    lax.fori_loop(0, ROWS + 2, shift_row, 0, unroll=5)

    def expert(t, s):
        return routes[t // 2, t % 2, s - 2] + 2

    def forward(s, kernel_of):
        for t in range(TILES):
            rt, cols = t // 2, slice((t % 2) * 16, (t % 2) * 16 + 16)
            pieces = [
                shifted[b, rt * 16 + a : rt * 16 + a + 16, cols, :].reshape(256, CH)
                for a in range(3)
                for b in range(3)
            ]
            pre = jnp.dot(
                jnp.concatenate(pieces, axis=1), w[kernel_of(t, s)], preferred_element_type=F32
            )
            g = grad[rt * 16 : rt * 16 + 16, cols, :].reshape(256, CH).astype(F32)
            gate = gates[rt, t % 2, s] * 0.5
            deltas[t, s] = (gelu_slope_twice(pre) * (g * gate)).astype(BF)

    def forward_shared(s, _):
        forward(s, lambda t, s: s)
        return 0

    def forward_routed(s, _):
        forward(s, expert)
        return 0

    w_copies[0].wait()
    w_copies[1].wait()
    lax.fori_loop(0, 2, forward_shared, 0)
    for copy in w_copies[2:]:
        copy.wait()
    lax.fori_loop(2, SLOTS, forward_routed, 0)

    def along_y(source, target, d, send, recv):
        return pltpu.make_async_remote_copy(
            src_ref=source, dst_ref=target, send_sem=send, recv_sem=recv,
            device_id=(gx, mod(gy + d, GY)), device_id_type=MESH,
        )

    def along_x(source, target, d, send, recv):
        return pltpu.make_async_remote_copy(
            src_ref=source, dst_ref=target, send_sem=send, recv_sem=recv,
            device_id=(mod(gx + d, GX), gy), device_id_type=MESH,
        )

    def backward(t):
        rt, cols = t // 2, slice((t % 2) * 16, (t % 2) * 16 + 16)
        d = jnp.concatenate([deltas[t, s] for s in range(SLOTS)], axis=1)
        chosen = [0, 1] + [expert(t, s) for s in range(2, SLOTS)]
        for a in range(3):
            for b in range(3):
                tap = 3 * a + b
                kernels = jnp.concatenate(
                    [w[e, tap * CH : (tap + 1) * CH, :] for e in chosen], axis=1
                )
                r = lax.dot_general(
                    d, kernels, (((1,), (1,)), ((), ())), preferred_element_type=F32
                )
                spread[b, rt * 16 + a : rt * 16 + a + 16, cols, :] += r.reshape(16, 16, CH)

    def x_copies(t, target):
        _, groups, start = CHUNKS[t // 2]
        rows = slice(start, start + groups * 16)
        if t % 2:
            rows = slice(start + groups * 16, start + groups * 32 + 16)
        return [
            along_y(
                xs.at[mod(gy + d, GY), rows], xr.at[target(d), rows], d,
                x_s.at[t, d], x_r.at[t, d],
            )
            for d in range(1, GY)
        ]

    place16 = lax.broadcasted_iota(jnp.int32, (16, CH), 0)
    for t in range(TILES):
        backward(t)
        first, groups, start = CHUNKS[t // 2]
        base = start + (t % 2) * groups * 16

        def opened(r):
            if t % 2 == 0:
                middle = jnp.where(place16 >= 1, pltpu.roll(spread[1, r, 0:16, :], 1, 0), 0.0)
                ahead = jnp.where(place16 >= 2, pltpu.roll(spread[2, r, 0:16, :], 2, 0), 0.0)
                return spread[0, r, 0:16, :] + middle + ahead
            middle = pltpu.roll(spread[1, r, 8:32, :], 1, 0)[8:24]
            ahead = pltpu.roll(spread[2, r, 8:32, :], 2, 0)[8:24]
            return spread[0, r, 16:32, :] + middle + ahead

        def split_group(k, _):
            lines = [opened(4 * (first + k) + q) for q in range(4)]
            for jt in range(2):
                lanes = slice(jt * 128, jt * 128 + 128)
                for s, part in enumerate(transpose_blocks([line[:, lanes] for line in lines])):
                    xs[jt * 4 + s, pl.ds(pl.multiple_of(base + 16 * k, 16), 16), :] = part.astype(BF)
            return 0

        lax.fori_loop(0, groups, split_group, 0, unroll=groups)
        if t % 2:
            rows = slice(4 * first, 4 * first + 4 * groups)
            last = start + groups * 32
            for jt in range(2):
                lanes = slice(jt * 128, jt * 128 + 128)
                edge[0, jt, rows] = (
                    spread[1, rows, COLS - 1, lanes] + spread[2, rows, COLS - 2, lanes]
                )
                edge[1, jt, rows] = spread[2, rows, COLS - 1, lanes]
                for q in range(4):
                    for s in range(2):
                        edges[q, jt, s * 8 : s * 8 + groups] = edge[
                            s, jt, pl.ds(4 * first + q, groups, stride=4), :
                        ]
                for s, part in enumerate(transpose_blocks([edges[q, jt] for q in range(4)])):
                    xs[jt * 4 + s, last : last + 16, :] = part.astype(BF)
        for copy in x_copies(t, lambda d: gy):
            copy.start()

    def own_row(r, _):
        ahead = jnp.where(place > 0, pltpu.roll(spread[2, r], 1, 0), 0.0)
        behind = jnp.where(place < COLS - 1, pltpu.roll(spread[0, r], COLS - 1, 0), 0.0)
        total[r] = spread[1, r] + ahead + behind
        return 0

    lax.fori_loop(0, ROWS + 2, own_row, 0, unroll=5)
    erow[0] = total[ROWS + 1].astype(BF)
    erow[1] = total[0].astype(BF)
    for jt in range(2):
        lanes = slice(jt * 128, jt * 128 + 128)
        left_edge[jt, 0 : ROWS + 2] = spread[0, 0 : ROWS + 2, 0, lanes]
        ecol[0, :, lanes] = edge[1, jt, 1 : ROWS + 1].astype(BF)
        ecol[1, :, lanes] = left_edge[jt, 1 : ROWS + 1].astype(BF)
        for k, r in enumerate((ROWS + 1, ROWS + 1, 0, 0)):
            corner = left_edge[jt, r : r + 1, :] if k % 2 else edge[1, jt, r : r + 1, :]
            ecor[k, :, lanes] = jnp.broadcast_to(corner, (16, 128)).astype(BF)
    border = border_copies(
        gx, gy,
        [erow.at[0], erow.at[1], ecol.at[0], ecol.at[1]] + [ecor.at[k] for k in range(4)],
        [brow.at[0], brow.at[1], bcol.at[0], bcol.at[1]] + [bcor.at[k] for k in range(4)],
        border_s, border_r,
    )
    for copy in border:
        copy.start()
    xr[gy] = xs[gy]

    for copy in in_copies[2:]:
        copy.wait()
    for chunk, (first, groups, start) in enumerate(CHUNKS):
        for copy in x_copies(2 * chunk, lambda d: mod(gy - d, GY)):
            copy.wait()
        for copy in x_copies(2 * chunk + 1, lambda d: mod(gy - d, GY)):
            copy.wait()
        last = start + groups * 32
        rim = jnp.dot(
            edge_table[0 : groups * 64],
            xr[:, last : last + 16].reshape(128, 128),
            preferred_element_type=F32,
        )
        for pair in range(0, groups, 2):
            width = min(2, groups - pair)
            data = []
            for k in range(pair, pair + width):
                halves = [start + 16 * (groups * part + k) for part in range(2)]
                halves = [xr[:, at : at + 16].reshape(128, 128) for at in halves]
                data.append(jnp.concatenate(halves, axis=0))
            c = jnp.dot(col[...], jnp.concatenate(data, axis=1), preferred_element_type=F32)
            for k in range(width):
                one = c[:, k * 128 : k * 128 + 128] + rim[(pair + k) * 64 : (pair + k) * 64 + 64]
                for part in range(2):
                    parts = [one[part * 32 + 8 * p : part * 32 + 8 * p + 8] for p in range(4)]
                    for q, block in enumerate(transpose_blocks(parts)):
                        r = part * OPEN + 4 * (first + pair + k) + q
                        half[pl.ds(r, 8, stride=2 * OPEN), :] = block
    forward_scale = 1.0 / math.sqrt(H * W)
    for pair in range(4):
        data = [
            half[(2 * pair + k) * 2 * OPEN : (2 * pair + k + 1) * 2 * OPEN].astype(BF)
            for k in range(2)
        ]
        c = jnp.dot(row[...], jnp.concatenate(data, axis=1), preferred_element_type=F32)
        c = (c * forward_scale).astype(BF)
        for k in range(2):
            for mh in range(2):
                cs[mh * 8 + 2 * pair + k] = c[mh * 64 : mh * 64 + 64, k * 128 : k * 128 + 128]
    parts_of = [slice(0, 32), slice(32, 64)]

    def c_copy(part, d, target):
        rows = parts_of[part]
        return along_x(
            cs.at[mod(gx + d, GX), rows], cr.at[target, rows], d, c_s.at[part, d], c_r.at[part, d]
        )

    def g_copy(part, d, target):
        rows = parts_of[part]
        return along_y(cg.at[gy, rows], cg.at[target, rows], d, g_s.at[part, d], g_r.at[part, d])

    def p_copy(part, d, target):
        rows = parts_of[part]
        return along_x(sp.at[gx, rows], sp.at[target, rows], d, p_s.at[part, d], p_r.at[part, d])

    for part in range(2):
        for d in range(1, GX):
            c_copy(part, d, gx).start()
    cr[gx] = cs[gx]

    for copy in border:
        copy.wait()
    total[1] += brow[0].astype(F32) * above
    total[ROWS] += brow[1].astype(F32) * below
    own = slice(1, ROWS + 1)
    total[own, 0, :] += bcol[0].astype(F32) * left
    total[own, COLS - 1, :] += bcol[1].astype(F32) * right
    total[1, 0:1, :] += bcor[0][0:1].astype(F32) * (above * left)
    total[1, COLS - 1 : COLS, :] += bcor[1][0:1].astype(F32) * (above * right)
    total[ROWS, 0:1, :] += bcor[2][0:1].astype(F32) * (below * left)
    total[ROWS, COLS - 1 : COLS, :] += bcor[3][0:1].astype(F32) * (below * right)

    n8 = lax.rem(gx, 8)
    mh = gx // 8
    lane64 = lax.broadcasted_iota(jnp.int32, (32, KH), 1)
    row64 = lax.broadcasted_iota(jnp.int32, (32, KH), 0)
    block_of_lane = lax.broadcasted_iota(jnp.int32, (32, 512), 1) >> 5
    lane_block = lax.broadcasted_iota(jnp.int32, (32, 128), 1) >> 5
    band_of = []
    for n4 in range(4):
        ids = jnp.broadcast_to(band_ids[pl.ds(4 * n8 + n4, 1), :], (32, KH))
        band_of.append(jnp.sum(jnp.where(lane64 == row64 + 32 * mh, ids, 0), axis=1, keepdims=True))

    for part in range(2):
        rows = parts_of[part]
        for d in range(1, GX):
            c_copy(part, d, mod(gx - d, GX)).wait()
        coef = cr[0, rows].astype(F32)
        for k in range(1, GX):
            coef = coef + cr[k, rows].astype(F32)
        cg[gy, rows] = coef.astype(BF)
        for d in range(1, GY):
            g_copy(part, d, gy).start()

    mixer = band[...].reshape(512, CH)
    for part in range(2):
        rows = parts_of[part]
        for d in range(1, GY):
            g_copy(part, d, mod(gy - d, GY)).wait()
        inputs = [
            transpose_blocks([cg[jt * 4 + p, rows].astype(F32) for p in range(4)])
            for jt in range(2)
        ]
        spec = jnp.zeros((32, 128), F32)
        modes = [
            jnp.concatenate([inputs[0][n4], inputs[1][n4]], axis=1).astype(BF) for n4 in range(4)
        ]
        mixed = lax.dot_general(
            jnp.concatenate(modes, axis=0), mixer, (((1,), (1,)), ((), ())),
            preferred_element_type=F32,
        )
        for n4 in range(4):
            z = jnp.where(block_of_lane == band_of[n4], mixed[n4 * 32 : n4 * 32 + 32], 0.0)
            y = z[:, 0:128] + z[:, 128:256] + z[:, 256:384] + z[:, 384:512]
            y = y + pltpu.roll(y, 64, 1)
            y = y + pltpu.roll(y, 32, 1)
            spec = jnp.where(lane_block == n4, y, spec)
        sp[gx, rows] = spec.astype(BF)
        for d in range(1, GX):
            p_copy(part, d, gx).start()
    for part in range(2):
        for d in range(1, GX):
            p_copy(part, d, mod(gx - d, GX)).wait()

    inverse_scale = 1.0 / math.sqrt(2 * KH * KW)
    for pair in range(4):
        data = [
            jnp.concatenate([sp[2 * pair + k], sp[8 + 2 * pair + k]], axis=0) for k in range(2)
        ]
        z = jnp.dot(back[...], jnp.concatenate(data, axis=1), preferred_element_type=F32)
        z = z * inverse_scale
        for k in range(2):
            zs[(2 * pair + k) * 96 : (2 * pair + k + 1) * 96, :] = z[:, k * 128 : k * 128 + 128]

    def f_copies(third, target):
        rows = slice(4 * third, 4 * third + 4)
        return [
            along_y(
                fs.at[mod(gy + d, GY), rows], fr.at[target(d), rows], d,
                f_s.at[third, d], f_r.at[third, d],
            )
            for d in range(1, GY)
        ]

    for third in range(3):
        for pair in range(2 * third, 2 * third + 2):
            columns = []
            for k in range(2):
                pieces = []
                for part in range(2):
                    r = part * ROWS + 4 * (2 * pair + k)
                    parts = [zs[pl.ds(r + q, 8, stride=2 * ROWS), :] for q in range(4)]
                    pieces += list(transpose_blocks(parts))
                columns.append(jnp.concatenate(pieces, axis=0))
            data = jnp.concatenate(columns, axis=1).astype(BF)
            f = jnp.dot(col_t[...], data, preferred_element_type=F32).astype(BF)
            for k in range(2):
                for j in range(GY):
                    fs[j, 2 * pair + k] = f[j * 32 : j * 32 + 32, k * 128 : k * 128 + 128]
        for copy in f_copies(third, lambda d: gy):
            copy.start()
    fr[gy] = fs[gy]

    def join_group(g, _):
        for jt in range(2):
            lanes = slice(jt * 128, jt * 128 + 128)
            parts = [fr[jt * 4 + s, g].astype(F32) for s in range(4)]
            for q, part in enumerate(transpose_blocks(parts)):
                out[4 * g + q, :, lanes] = (total[4 * g + q + 1, :, lanes] + part).astype(BF)
        return 0

    for third in range(3):
        for copy in f_copies(third, lambda d: mod(gy - d, GY)):
            copy.wait()
        lax.fori_loop(4 * third, 4 * third + 4, join_group, 0, unroll=2)


VMEM = pl.BlockSpec(memory_space=pltpu.VMEM)
SMEM = pl.BlockSpec(memory_space=pltpu.SMEM)
ANY = pl.BlockSpec(memory_space=pl.ANY)


def dma(*shape):
    return pltpu.SemaphoreType.DMA(shape)


def border(count=1):
    one = [
        pltpu.VMEM((2, COLS, CH), BF),
        pltpu.VMEM((2, ROWS, CH), BF),
        pltpu.VMEM((4, 16, CH), BF),
    ]
    return one * count


def body(saved_mid, out_grad, expert_weight, routes, gates, band_matrix, band_ids):
    return pl.pallas_call(
        fused_body,
        name="fused",
        out_shape=pltpu.VMEM((ROWS, COLS, CH), BF),
        in_specs=[ANY, ANY, ANY, SMEM, SMEM, ANY, VMEM, ANY, ANY, ANY, ANY, ANY],
        out_specs=VMEM,
        scratch_shapes=[
            pltpu.VMEM((ROWS, COLS, CH), BF),
            pltpu.VMEM((ROWS, COLS, CH), BF),
            pltpu.VMEM((EXPERTS, 9 * CH, CH), BF),
            pltpu.VMEM((128, 2 * OPEN), BF),
            pltpu.VMEM((2 * ROWS, 128), BF),
            pltpu.VMEM((16, 32, CH), BF),
            pltpu.VMEM((64, 256), BF),
            pltpu.VMEM((256, 64), BF),
            pltpu.VMEM((320, 128), BF),
            pltpu.VMEM((ROWS + 2, COLS, CH), F32),
            pltpu.VMEM((3, ROWS + 2, COLS, CH), BF),
            pltpu.VMEM((2, 64, CH), F32),
            pltpu.VMEM((TILES, SLOTS, 256, CH), BF),
            pltpu.VMEM((3, OPEN, COLS, CH), F32),
            pltpu.VMEM((OPEN, COLS, CH), F32),
            pltpu.VMEM((2, 2, OPEN + 4, 128), F32),
            pltpu.VMEM((4, 2, 16, 128), F32),
            pltpu.VMEM((2, OPEN + 4, 128), F32),
            *border(4),
            pltpu.VMEM((GY, 464, 128), BF),
            pltpu.VMEM((GY, 464, 128), BF),
            pltpu.VMEM((8 * 2 * OPEN, 128), F32),
            pltpu.VMEM((GX, 64, 128), BF),
            pltpu.VMEM((GX, 64, 128), BF),
            pltpu.VMEM((GY, 64, 128), BF),
            pltpu.VMEM((GX, 64, 128), BF),
            pltpu.VMEM((8 * 2 * ROWS, 128), F32),
            pltpu.VMEM((GY, 12, 32, 128), BF),
            pltpu.VMEM((GY, 12, 32, 128), BF),
            dma(EXPERTS), dma(8), dma(8), dma(8), dma(8), dma(8),
            dma(6, GY), dma(6, GY), dma(2, GX), dma(2, GX), dma(2, GY), dma(2, GY),
            dma(2, GX), dma(2, GX), dma(3, GY), dma(3, GY),
        ],
        compiler_params=pltpu.CompilerParams(
            collective_id=0, has_side_effects=True, vmem_limit_bytes=66_000_000
        ),
    )(
        saved_mid, out_grad, expert_weight.reshape(EXPERTS, 9 * CH, CH), routes, gates,
        band_matrix, band_ids.T, jnp.asarray(OPEN_TABLE, BF), jnp.asarray(COL_TABLE, BF),
        jnp.asarray(EDGE_TABLE, BF), jnp.asarray(ROW_TABLE, BF), jnp.asarray(BACK_TABLE, BF),
    )


def solution(mesh):
    placed = (
        P("gx", "gy", None),
        P("gx", "gy", None),
        P(),
        P("gx", "gy", None),
        P("gx", "gy", None),
        P(),
        P(),
    )
    return jax.shard_map(
        body, mesh=mesh, in_specs=placed, out_specs=P("gx", "gy", None), check_vma=False
    )
```

```python
import math

import jax
import jax.numpy as jnp
import numpy as np
from jax import lax
from jax.experimental import pallas as pl
from jax.experimental.pallas import tpu as pltpu
from jax.sharding import PartitionSpec as P

F32 = jnp.float32
BF = jnp.bfloat16
MESH = pl.DeviceIdType.MESH
GX, GY = 16, 8
ROWS, COLS, CH = 48, 32, 256
KH, KW = 64, 32
H, W = 768, 256
EXPERTS, SLOTS, TILES = 10, 6, 6
OPEN = ROWS + 4
CHUNKS = ((0, 4, 0), (4, 4, 144), (8, 5, 288))

DIRS = ((1, 0), (-1, 0), (0, 1), (0, -1), (1, 1), (1, -1), (-1, 1), (-1, -1))
PARTS = ((0, 32), (32, 64), (64, 112), (112, 160), (160, 176), (176, 192), (192, 208), (208, 224))


def mod(value, count):
    return lax.rem(value + count, count)


def tables():
    n = (4 * np.arange(8)[None, :] + np.arange(4)[:, None]).reshape(-1)

    def wave(columns):
        theta = 2 * np.pi * ((n[:, None] * columns[None, :]) % W) / W
        return np.concatenate([np.cos(theta), np.sin(theta)])

    opened = np.zeros((64, 2, GY, 16))
    edge = np.zeros((5, 64, GY, 16))
    for j in range(GY):
        for part in range(2):
            columns = COLS * j + 16 * part - 1 + np.arange(16)
            opened[:, part, j] = wave(columns) * (columns >= 0)
        for side, column in enumerate((COLS * j + COLS - 1, COLS * j + COLS)):
            if column < W:
                for g in range(5):
                    edge[g, :, j, side * 8 + g] = wave(np.array([column]))[:, 0]
    m = np.arange(KH)
    freq = np.where(m < KH // 2, m, H - KH + m)
    row = np.zeros((GX, 2, 2, 32, 2, OPEN))
    for gx in range(GX):
        h = ROWS * gx - 1 + np.arange(OPEN)
        phase = 2 * np.pi * ((freq[:, None] * h[None, :]) % H) / H
        keep = (h >= 0) & (h < H) & (np.arange(OPEN) < ROWS + 2)
        rc = (np.cos(phase) * keep).reshape(2, 32, OPEN)
        rs = (np.sin(phase) * keep).reshape(2, 32, OPEN)
        row[gx, :, 0, :, 0], row[gx, :, 0, :, 1] = rc, -rs
        row[gx, :, 1, :, 0], row[gx, :, 1, :, 1] = rs, rc
    back = row[..., 1 : ROWS + 1].reshape(GX, 128, 2 * ROWS).transpose(0, 2, 1)
    row = row.reshape(GX, 128, 2 * OPEN)
    return opened.reshape(64, 256), wave(np.arange(W)).T, edge.reshape(320, 128), row, back


OPEN_TABLE, COL_TABLE, EDGE_TABLE, ROW_TABLE, BACK_TABLE = tables()


def gelu_slope_twice(values):
    density = jnp.exp2((values * values) * (-0.5 * math.log2(math.e)))
    return (1.0 + lax.erf(values * math.sqrt(0.5))) + (values * math.sqrt(2.0 / math.pi)) * density


def transpose_blocks(parts):
    lane = lax.broadcasted_iota(jnp.int32, parts[0].shape, parts[0].ndim - 1)
    axis = parts[0].ndim - 1
    low = lane < 64
    a, b, c, d = parts
    a, c = (
        jnp.where(low, a, pltpu.roll(c, 64, axis)),
        jnp.where(low, pltpu.roll(a, 64, axis), c),
    )
    b, d = (
        jnp.where(low, b, pltpu.roll(d, 64, axis)),
        jnp.where(low, pltpu.roll(b, 64, axis), d),
    )
    even = (lane & 32) == 0
    a, b = (
        jnp.where(even, a, pltpu.roll(b, 32, axis)),
        jnp.where(even, pltpu.roll(a, 96, axis), b),
    )
    c, d = (
        jnp.where(even, c, pltpu.roll(d, 32, axis)),
        jnp.where(even, pltpu.roll(c, 96, axis), d),
    )
    return a, b, c, d


def border_copies(gx, gy, source, target, send_sem, recv_sem):
    copies = [
        pltpu.make_async_remote_copy(
            src_ref=source.at[first:last],
            dst_ref=target.at[first:last],
            send_sem=send_sem,
            recv_sem=recv_sem,
            device_id=(mod(gx + dr, GX), mod(gy + dc, GY)),
            device_id_type=MESH,
        )
        for (dr, dc), (first, last) in zip(DIRS, PARTS)
    ]
    whole = pltpu.make_async_remote_copy(
        src_ref=source,
        dst_ref=target,
        send_sem=send_sem,
        recv_sem=recv_sem,
        device_id=(mod(gx + 1, GX), gy),
        device_id_type=MESH,
    )
    return copies, whole


def fused_body(
    mid_hbm, grad_hbm, w_hbm, routes, gates, band_hbm, band_ids,
    col_hbm, col_t_hbm, edge_hbm, row_hbm, back_hbm,
    out,
    mid, grad, w, row, back, band, col, col_t, edge_table, ext, shifted, side, deltas, spread, total, edge, edges, left_edge,
    border_out, border_in, halo_out, halo_in,
    xs, xr, half, cs, cr, cg, sp, zs, fs, fr,
    w_sem, in_sem, halo_s, halo_r, border_s, border_r,
    x_s, x_r, c_s, c_r, g_s, g_r, p_s, p_r, f_s, f_r,
):
    gx, gy = lax.axis_index("gx"), lax.axis_index("gy")
    w_copies = [
        pltpu.make_async_copy(w_hbm.at[first:last], w.at[first:last], w_sem.at[k])
        for k, (first, last) in enumerate(((0, 1), (1, 2), (2, EXPERTS)))
    ]
    sources = [
        mid_hbm, grad_hbm, row_hbm.at[gx], back_hbm.at[gx],
        band_hbm.at[:, pl.ds(pl.multiple_of(gy * 32, 32), 32), :],
        col_hbm, col_t_hbm, edge_hbm,
    ]
    targets = [mid, grad, row, back, band, col, col_t, edge_table]
    in_copies = [
        pltpu.make_async_copy(source, target, in_sem.at[k])
        for k, (source, target) in enumerate(zip(sources, targets))
    ]
    for copy in in_copies[:1] + w_copies[:1] + in_copies[1:2] + w_copies[1:] + in_copies[2:]:
        copy.start()
    barrier = pltpu.get_barrier_semaphore()
    partners = [(gx, mod(gy + d, GY)) for d in range(1, GY)]
    partners += [(mod(gx + d, GX), gy) for d in range(1, GX)]
    partners += [(mod(gx + dr, GX), mod(gy + dc, GY)) for dr, dc in DIRS[4:]]
    for device in partners:
        pl.semaphore_signal(barrier, inc=1, device_id=device, device_id_type=MESH)

    above = jnp.where(gx > 0, 1.0, 0.0)
    below = jnp.where(gx < GX - 1, 1.0, 0.0)
    left = jnp.where(gy > 0, 1.0, 0.0)
    right = jnp.where(gy < GY - 1, 1.0, 0.0)

    in_copies[0].wait()
    ext[1 : ROWS + 1] = mid[...].astype(F32)
    halo_out[0:32] = mid[ROWS - 1]
    halo_out[32:64] = mid[0]
    halo_out[64:112] = ext[1 : ROWS + 1, COLS - 1, :].astype(BF)
    halo_out[112:160] = ext[1 : ROWS + 1, 0, :].astype(BF)
    for k, (r, c) in enumerate(((ROWS, COLS - 1), (ROWS, 0), (1, COLS - 1), (1, 0))):
        corner = jnp.broadcast_to(ext[r, c : c + 1, :], (16, CH)).astype(BF)
        halo_out[160 + 16 * k : 176 + 16 * k] = corner
    pl.semaphore_wait(barrier, len(partners))
    halo, halo_all = border_copies(gx, gy, halo_out, halo_in, halo_s.at[0], halo_r.at[0])
    for copy in halo:
        copy.start()
    in_copies[1].wait()
    for b in (0, 2):
        spread[b] = jnp.zeros((OPEN, COLS, CH), F32)
    spread[1, 0] = jnp.zeros((COLS, CH), F32)
    spread[1, 1 : ROWS + 1] = grad[...].astype(F32)
    spread[1, ROWS + 1 :] = jnp.zeros((OPEN - ROWS - 1, COLS, CH), F32)
    edges[...] = jnp.zeros_like(edges)
    halo_all.wait()
    ext[0] = halo_in[0:32].astype(F32) * above
    ext[ROWS + 1] = halo_in[32:64].astype(F32) * below
    side[0, 8 : 8 + ROWS] = halo_in[64:112].astype(F32) * left
    side[1, 8 : 8 + ROWS] = halo_in[112:160].astype(F32) * right
    side[0, 7:8] = halo_in[160:176].astype(F32)[0:1] * (above * left)
    side[1, 7:8] = halo_in[176:192].astype(F32)[0:1] * (above * right)
    side[0, 8 + ROWS : 9 + ROWS] = halo_in[192:208].astype(F32)[0:1] * (below * left)
    side[1, 8 + ROWS : 9 + ROWS] = halo_in[208:224].astype(F32)[0:1] * (below * right)
    place = lax.broadcasted_iota(jnp.int32, (COLS, CH), 0)

    def shift_row(r, _):
        line = ext[r]
        before = side[0, pl.ds(r + 7, 1), :]
        after = side[1, pl.ds(r + 7, 1), :]
        shifted[1, r] = line.astype(BF)
        shifted[0, r] = jnp.where(place == 0, before, pltpu.roll(line, 1, 0)).astype(BF)
        shifted[2, r] = jnp.where(place == COLS - 1, after, pltpu.roll(line, COLS - 1, 0)).astype(BF)
        return 0

    lax.fori_loop(0, ROWS + 2, shift_row, 0, unroll=5)

    def expert(t, s):
        return routes[t // 2, t % 2, s - 2] + 2

    def forward(s, kernel_of):
        for t in range(TILES):
            rt, cols = t // 2, slice((t % 2) * 16, (t % 2) * 16 + 16)
            pieces = [
                shifted[b, rt * 16 + a : rt * 16 + a + 16, cols, :].reshape(256, CH)
                for a in range(3)
                for b in range(3)
            ]
            pre = jnp.dot(
                jnp.concatenate(pieces, axis=1), w[kernel_of(t, s)], preferred_element_type=F32
            )
            g = grad[rt * 16 : rt * 16 + 16, cols, :].reshape(256, CH).astype(F32)
            gate = gates[rt, t % 2, s] * 0.5
            deltas[t, s] = (gelu_slope_twice(pre) * (g * gate)).astype(BF)

    def forward_shared(s, _):
        forward(s, lambda t, s: s)
        return 0

    def forward_routed(s, _):
        forward(s, expert)
        return 0

    w_copies[0].wait()
    w_copies[1].wait()
    lax.fori_loop(0, 2, forward_shared, 0)
    w_copies[2].wait()
    lax.fori_loop(2, SLOTS, forward_routed, 0)

    def along_y(source, target, d, send, recv):
        return pltpu.make_async_remote_copy(
            src_ref=source, dst_ref=target, send_sem=send, recv_sem=recv,
            device_id=(gx, mod(gy + d, GY)), device_id_type=MESH,
        )

    def along_x(source, target, d, send, recv):
        return pltpu.make_async_remote_copy(
            src_ref=source, dst_ref=target, send_sem=send, recv_sem=recv,
            device_id=(mod(gx + d, GX), gy), device_id_type=MESH,
        )

    place16 = lax.broadcasted_iota(jnp.int32, (16, CH), 0)

    def x_rows(rt, half):
        _, groups, start = CHUNKS[rt]
        at = start + groups * 16
        return slice(at, start + groups * 32 + 16) if half else slice(start, at)

    def opened(r, half):
        if half == 0:
            middle = jnp.where(place16 >= 1, pltpu.roll(spread[1, r, 0:16, :], 1, 0), 0.0)
            ahead = jnp.where(place16 >= 2, pltpu.roll(spread[2, r, 0:16, :], 2, 0), 0.0)
            return spread[0, r, 0:16, :] + middle + ahead
        middle = pltpu.roll(spread[1, r, 8:32, :], 1, 0)[8:24]
        ahead = pltpu.roll(spread[2, r, 8:32, :], 2, 0)[8:24]
        return spread[0, r, 16:32, :] + middle + ahead

    def leave(rt, half):
        first, groups, start = CHUNKS[rt]
        base = start + half * groups * 16

        def split_group(k, _):
            lines = [opened(4 * (first + k) + q, half) for q in range(4)]
            for jt in range(2):
                lanes = slice(jt * 128, jt * 128 + 128)
                for s, part in enumerate(transpose_blocks([line[:, lanes] for line in lines])):
                    xs[jt * 4 + s, pl.ds(pl.multiple_of(base + 16 * k, 16), 16), :] = part.astype(BF)
            return 0

        lax.fori_loop(0, groups, split_group, 0, unroll=groups)
        if half:
            rows = slice(4 * first, 4 * first + 4 * groups)
            last = start + groups * 32
            for jt in range(2):
                lanes = slice(jt * 128, jt * 128 + 128)
                edge[0, jt, rows] = (
                    spread[1, rows, COLS - 1, lanes] + spread[2, rows, COLS - 2, lanes]
                )
                edge[1, jt, rows] = spread[2, rows, COLS - 1, lanes]
                for q in range(4):
                    for s in range(2):
                        edges[q, jt, s * 8 : s * 8 + groups] = edge[
                            s, jt, pl.ds(4 * first + q, groups, stride=4), :
                        ]
                for s, part in enumerate(transpose_blocks([edges[q, jt] for q in range(4)])):
                    xs[jt * 4 + s, last : last + 16, :] = part.astype(BF)
        rows = x_rows(rt, half)
        for d in range(1, GY):
            along_y(
                xs.at[mod(gy + d, GY), rows], xr.at[gy, rows], d,
                x_s.at[2 * rt + half], x_r.at[2 * rt + half],
            ).start()

    for rt in range(3):

        def backward(ct, _):
            cols = pl.ds(pl.multiple_of(ct * 16, 16), 16)
            d = jnp.concatenate([deltas[2 * rt + ct, s] for s in range(SLOTS)], axis=1)
            chosen = [0, 1] + [routes[rt, ct, s - 2] + 2 for s in range(2, SLOTS)]
            for a in range(3):
                for b in range(3):
                    tap = 3 * a + b
                    kernels = jnp.concatenate(
                        [w[e, tap * CH : (tap + 1) * CH, :] for e in chosen], axis=1
                    )
                    r = lax.dot_general(
                        d, kernels, (((1,), (1,)), ((), ())), preferred_element_type=F32
                    )
                    spread[b, rt * 16 + a : rt * 16 + a + 16, cols, :] += r.reshape(16, 16, CH)

            @pl.when(ct == 0)
            def _():
                leave(rt, 0)

            @pl.when(ct == 1)
            def _():
                leave(rt, 1)

            return 0

        lax.fori_loop(0, 2, backward, 0)

    def own_row(r, _):
        ahead = jnp.where(place > 0, pltpu.roll(spread[2, r], 1, 0), 0.0)
        behind = jnp.where(place < COLS - 1, pltpu.roll(spread[0, r], COLS - 1, 0), 0.0)
        total[r] = spread[1, r] + ahead + behind
        return 0

    lax.fori_loop(0, ROWS + 2, own_row, 0, unroll=5)
    border_out[0:32] = total[ROWS + 1].astype(BF)
    border_out[32:64] = total[0].astype(BF)
    for jt in range(2):
        lanes = slice(jt * 128, jt * 128 + 128)
        left_edge[jt, 0 : ROWS + 2] = spread[0, 0 : ROWS + 2, 0, lanes]
        border_out[64:112, lanes] = edge[1, jt, 1 : ROWS + 1].astype(BF)
        border_out[112:160, lanes] = left_edge[jt, 1 : ROWS + 1].astype(BF)
        for k, r in enumerate((ROWS + 1, ROWS + 1, 0, 0)):
            corner = left_edge[jt, r : r + 1, :] if k % 2 else edge[1, jt, r : r + 1, :]
            border_out[160 + 16 * k : 176 + 16 * k, lanes] = jnp.broadcast_to(
                corner, (16, 128)
            ).astype(BF)
    border, border_all = border_copies(
        gx, gy, border_out, border_in, border_s.at[0], border_r.at[0]
    )
    for copy in border:
        copy.start()
    xr[gy] = xs[gy]

    for copy in in_copies[2:]:
        copy.wait()
    for chunk, (first, groups, start) in enumerate(CHUNKS):
        for part in range(2):
            rows = x_rows(chunk, part)
            t = 2 * chunk + part
            along_y(xs.at[1:GY, rows], xr.at[1:GY, rows], 1, x_s.at[t], x_r.at[t]).wait()
        last = start + groups * 32
        rim = jnp.dot(
            edge_table[0 : groups * 64],
            xr[:, last : last + 16].reshape(128, 128),
            preferred_element_type=F32,
        )
        for pair in range(0, groups, 2):
            width = min(2, groups - pair)
            data = []
            for k in range(pair, pair + width):
                halves = [start + 16 * (groups * part + k) for part in range(2)]
                halves = [xr[:, at : at + 16].reshape(128, 128) for at in halves]
                data.append(jnp.concatenate(halves, axis=0))
            c = jnp.dot(col[...], jnp.concatenate(data, axis=1), preferred_element_type=F32)
            for k in range(width):
                one = c[:, k * 128 : k * 128 + 128] + rim[(pair + k) * 64 : (pair + k) * 64 + 64]
                for part in range(2):
                    parts = [one[part * 32 + 8 * p : part * 32 + 8 * p + 8] for p in range(4)]
                    for q, block in enumerate(transpose_blocks(parts)):
                        r = part * OPEN + 4 * (first + pair + k) + q
                        half[pl.ds(r, 8, stride=2 * OPEN), :] = block
    forward_scale = 1.0 / math.sqrt(H * W)
    for pair in range(4):
        data = [
            half[(2 * pair + k) * 2 * OPEN : (2 * pair + k + 1) * 2 * OPEN].astype(BF)
            for k in range(2)
        ]
        c = jnp.dot(row[...], jnp.concatenate(data, axis=1), preferred_element_type=F32)
        c = (c * forward_scale).astype(BF)
        for k in range(2):
            for mh in range(2):
                cs[mh * 8 + 2 * pair + k] = c[mh * 64 : mh * 64 + 64, k * 128 : k * 128 + 128]
    parts_of = [slice(0, 32), slice(32, 64)]

    def c_copy(part, source, target, d=1):
        rows = parts_of[part]
        return along_x(cs.at[source, rows], cr.at[target, rows], d, c_s.at[part], c_r.at[part])

    def g_copy(part, source, target, d=1):
        rows = parts_of[part]
        return along_y(cg.at[source, rows], cg.at[target, rows], d, g_s.at[part], g_r.at[part])

    def p_copy(part, source, target, d=1):
        rows = parts_of[part]
        return along_x(sp.at[source, rows], sp.at[target, rows], d, p_s.at[part], p_r.at[part])

    others_x, others_y = slice(1, GX), slice(1, GY)
    for part in range(2):
        for d in range(1, GX):
            c_copy(part, mod(gx + d, GX), gx, d).start()
    cr[gx] = cs[gx]

    border_all.wait()
    total[1] += border_in[0:32].astype(F32) * above
    total[ROWS] += border_in[32:64].astype(F32) * below
    own = slice(1, ROWS + 1)
    total[own, 0, :] += border_in[64:112].astype(F32) * left
    total[own, COLS - 1, :] += border_in[112:160].astype(F32) * right
    total[1, 0:1, :] += border_in[160:176].astype(F32)[0:1] * (above * left)
    total[1, COLS - 1 : COLS, :] += border_in[176:192].astype(F32)[0:1] * (above * right)
    total[ROWS, 0:1, :] += border_in[192:208].astype(F32)[0:1] * (below * left)
    total[ROWS, COLS - 1 : COLS, :] += border_in[208:224].astype(F32)[0:1] * (below * right)

    n8 = lax.rem(gx, 8)
    mh = gx // 8
    lane64 = lax.broadcasted_iota(jnp.int32, (32, KH), 1)
    row64 = lax.broadcasted_iota(jnp.int32, (32, KH), 0)
    block_of_lane = lax.broadcasted_iota(jnp.int32, (32, 512), 1) >> 5
    lane_block = lax.broadcasted_iota(jnp.int32, (32, 128), 1) >> 5
    band_of = []
    for n4 in range(4):
        ids = jnp.broadcast_to(band_ids[pl.ds(4 * n8 + n4, 1), :], (32, KH))
        band_of.append(jnp.sum(jnp.where(lane64 == row64 + 32 * mh, ids, 0), axis=1, keepdims=True))

    for part in range(2):
        rows = parts_of[part]
        c_copy(part, others_x, others_x).wait()
        coef = cr[0, rows].astype(F32)
        for k in range(1, GX):
            coef = coef + cr[k, rows].astype(F32)
        cg[gy, rows] = coef.astype(BF)
        for d in range(1, GY):
            g_copy(part, gy, gy, d).start()

    mixer = band[...].reshape(512, CH)
    for part in range(2):
        rows = parts_of[part]
        g_copy(part, others_y, others_y).wait()
        inputs = [
            transpose_blocks([cg[jt * 4 + p, rows].astype(F32) for p in range(4)])
            for jt in range(2)
        ]
        spec = jnp.zeros((32, 128), F32)
        modes = [
            jnp.concatenate([inputs[0][n4], inputs[1][n4]], axis=1).astype(BF) for n4 in range(4)
        ]
        mixed = lax.dot_general(
            jnp.concatenate(modes, axis=0), mixer, (((1,), (1,)), ((), ())),
            preferred_element_type=F32,
        )
        for n4 in range(4):
            z = jnp.where(block_of_lane == band_of[n4], mixed[n4 * 32 : n4 * 32 + 32], 0.0)
            y = z[:, 0:128] + z[:, 128:256] + z[:, 256:384] + z[:, 384:512]
            y = y + pltpu.roll(y, 64, 1)
            y = y + pltpu.roll(y, 32, 1)
            spec = jnp.where(lane_block == n4, y, spec)
        sp[gx, rows] = spec.astype(BF)
        for d in range(1, GX):
            p_copy(part, gx, gx, d).start()
    for part in range(2):
        p_copy(part, others_x, others_x).wait()

    inverse_scale = 1.0 / math.sqrt(2 * KH * KW)
    for pair in range(4):
        data = [
            jnp.concatenate([sp[2 * pair + k], sp[8 + 2 * pair + k]], axis=0) for k in range(2)
        ]
        z = jnp.dot(back[...], jnp.concatenate(data, axis=1), preferred_element_type=F32)
        z = z * inverse_scale
        for k in range(2):
            zs[(2 * pair + k) * 96 : (2 * pair + k + 1) * 96, :] = z[:, k * 128 : k * 128 + 128]

    def f_copy(third, source, target, d=1):
        rows = slice(4 * third, 4 * third + 4)
        return along_y(fs.at[source, rows], fr.at[target, rows], d, f_s.at[third], f_r.at[third])

    for third in range(3):
        for pair in range(2 * third, 2 * third + 2):
            columns = []
            for k in range(2):
                pieces = []
                for part in range(2):
                    r = part * ROWS + 4 * (2 * pair + k)
                    parts = [zs[pl.ds(r + q, 8, stride=2 * ROWS), :] for q in range(4)]
                    pieces += list(transpose_blocks(parts))
                columns.append(jnp.concatenate(pieces, axis=0))
            data = jnp.concatenate(columns, axis=1).astype(BF)
            f = jnp.dot(col_t[...], data, preferred_element_type=F32).astype(BF)
            for k in range(2):
                for j in range(GY):
                    fs[j, 2 * pair + k] = f[j * 32 : j * 32 + 32, k * 128 : k * 128 + 128]
        for d in range(1, GY):
            f_copy(third, mod(gy + d, GY), gy, d).start()
    fr[gy] = fs[gy]

    def join_group(g, _):
        for jt in range(2):
            lanes = slice(jt * 128, jt * 128 + 128)
            parts = [fr[jt * 4 + s, g].astype(F32) for s in range(4)]
            for q, part in enumerate(transpose_blocks(parts)):
                out[4 * g + q, :, lanes] = (total[4 * g + q + 1, :, lanes] + part).astype(BF)
        return 0

    for third in range(3):
        f_copy(third, others_y, others_y).wait()
        lax.fori_loop(4 * third, 4 * third + 4, join_group, 0, unroll=2)


VMEM = pl.BlockSpec(memory_space=pltpu.VMEM)
SMEM = pl.BlockSpec(memory_space=pltpu.SMEM)
ANY = pl.BlockSpec(memory_space=pl.ANY)


def dma(*shape):
    return pltpu.SemaphoreType.DMA(shape)


def body(saved_mid, out_grad, expert_weight, routes, gates, band_matrix, band_ids):
    return pl.pallas_call(
        fused_body,
        name="fused",
        out_shape=pltpu.VMEM((ROWS, COLS, CH), BF),
        in_specs=[ANY, ANY, ANY, SMEM, SMEM, ANY, VMEM, ANY, ANY, ANY, ANY, ANY],
        out_specs=VMEM,
        scratch_shapes=[
            pltpu.VMEM((ROWS, COLS, CH), BF),
            pltpu.VMEM((ROWS, COLS, CH), BF),
            pltpu.VMEM((EXPERTS, 9 * CH, CH), BF),
            pltpu.VMEM((128, 2 * OPEN), BF),
            pltpu.VMEM((2 * ROWS, 128), BF),
            pltpu.VMEM((16, 32, CH), BF),
            pltpu.VMEM((64, 256), BF),
            pltpu.VMEM((256, 64), BF),
            pltpu.VMEM((320, 128), BF),
            pltpu.VMEM((ROWS + 2, COLS, CH), F32),
            pltpu.VMEM((3, ROWS + 2, COLS, CH), BF),
            pltpu.VMEM((2, 64, CH), F32),
            pltpu.VMEM((TILES, SLOTS, 256, CH), BF),
            pltpu.VMEM((3, OPEN, COLS, CH), F32),
            pltpu.VMEM((OPEN, COLS, CH), F32),
            pltpu.VMEM((2, 2, OPEN + 4, 128), F32),
            pltpu.VMEM((4, 2, 16, 128), F32),
            pltpu.VMEM((2, OPEN + 4, 128), F32),
            *[pltpu.VMEM((224, CH), BF)] * 4,
            pltpu.VMEM((GY, 464, 128), BF),
            pltpu.VMEM((GY, 464, 128), BF),
            pltpu.VMEM((8 * 2 * OPEN, 128), F32),
            pltpu.VMEM((GX, 64, 128), BF),
            pltpu.VMEM((GX, 64, 128), BF),
            pltpu.VMEM((GY, 64, 128), BF),
            pltpu.VMEM((GX, 64, 128), BF),
            pltpu.VMEM((8 * 2 * ROWS, 128), F32),
            pltpu.VMEM((GY, 12, 32, 128), BF),
            pltpu.VMEM((GY, 12, 32, 128), BF),
            dma(3), dma(8), dma(1), dma(1), dma(1), dma(1),
            dma(6), dma(6), dma(2), dma(2), dma(2), dma(2), dma(2), dma(2), dma(3), dma(3),
        ],
        compiler_params=pltpu.CompilerParams(
            collective_id=0, has_side_effects=True, vmem_limit_bytes=66_000_000
        ),
    )(
        saved_mid, out_grad, expert_weight.reshape(EXPERTS, 9 * CH, CH), routes, gates,
        band_matrix, band_ids.T, jnp.asarray(OPEN_TABLE, BF), jnp.asarray(COL_TABLE, BF),
        jnp.asarray(EDGE_TABLE, BF), jnp.asarray(ROW_TABLE, BF), jnp.asarray(BACK_TABLE, BF),
    )


def solution(mesh):
    placed = (
        P("gx", "gy", None),
        P("gx", "gy", None),
        P(),
        P("gx", "gy", None),
        P("gx", "gy", None),
        P(),
        P(),
    )
    return jax.shard_map(
        body, mesh=mesh, in_specs=placed, out_specs=P("gx", "gy", None), check_vma=False
    )
```

```python
import math

import jax
import jax.numpy as jnp
import numpy as np
from jax import lax
from jax.experimental import pallas as pl
from jax.experimental.pallas import tpu as pltpu
from jax.sharding import PartitionSpec as P

F32 = jnp.float32
BF = jnp.bfloat16
MESH = pl.DeviceIdType.MESH
GX, GY = 16, 8
ROWS, COLS, CH = 48, 32, 256
KH, KW = 64, 32
H, W = 768, 256
EXPERTS, SLOTS, TILES = 10, 6, 6
OPEN = ROWS + 4
CHUNKS = ((0, 4, 0), (4, 4, 144), (8, 5, 288))

DIRS = ((1, 0), (-1, 0), (0, 1), (0, -1), (1, 1), (1, -1), (-1, 1), (-1, -1))
AHEAD_X = (8, 10, 6, 9, 7, 11, 5, 12, 4, 13, 3, 14, 2, 15, 1)
AHEAD_Y = (4, 5, 3, 6, 2, 7, 1)
PARTS = ((0, 32), (32, 64), (64, 112), (112, 160), (160, 176), (176, 192), (192, 208), (208, 224))


def mod(value, count):
    return lax.rem(value + count, count)


def tables():
    n = (4 * np.arange(8)[None, :] + np.arange(4)[:, None]).reshape(-1)

    def wave(columns):
        theta = 2 * np.pi * ((n[:, None] * columns[None, :]) % W) / W
        return np.concatenate([np.cos(theta), np.sin(theta)])

    opened = np.zeros((64, 2, GY, 16))
    edge = np.zeros((5, 64, GY, 16))
    for j in range(GY):
        for part in range(2):
            columns = COLS * j + 16 * part - 1 + np.arange(16)
            opened[:, part, j] = wave(columns) * (columns >= 0)
        for side, column in enumerate((COLS * j + COLS - 1, COLS * j + COLS)):
            if column < W:
                for g in range(5):
                    edge[g, :, j, side * 8 + g] = wave(np.array([column]))[:, 0]
    m = np.arange(KH)
    freq = np.where(m < KH // 2, m, H - KH + m)
    row = np.zeros((GX, 2, 2, 32, 2, OPEN))
    for gx in range(GX):
        h = ROWS * gx - 1 + np.arange(OPEN)
        phase = 2 * np.pi * ((freq[:, None] * h[None, :]) % H) / H
        keep = (h >= 0) & (h < H) & (np.arange(OPEN) < ROWS + 2)
        rc = (np.cos(phase) * keep).reshape(2, 32, OPEN)
        rs = (np.sin(phase) * keep).reshape(2, 32, OPEN)
        row[gx, :, 0, :, 0], row[gx, :, 0, :, 1] = rc, -rs
        row[gx, :, 1, :, 0], row[gx, :, 1, :, 1] = rs, rc
    back = row[..., 1 : ROWS + 1].reshape(GX, 128, 2 * ROWS).transpose(0, 2, 1)
    row = row.reshape(GX, 128, 2 * OPEN)
    return opened.reshape(64, 256), wave(np.arange(W)).T, edge.reshape(320, 128), row, back


OPEN_TABLE, COL_TABLE, EDGE_TABLE, ROW_TABLE, BACK_TABLE = tables()


def gelu_slope_twice(values):
    density = jnp.exp2((values * values) * (-0.5 * math.log2(math.e)))
    return (1.0 + lax.erf(values * math.sqrt(0.5))) + (values * math.sqrt(2.0 / math.pi)) * density


def transpose_blocks(parts):
    lane = lax.broadcasted_iota(jnp.int32, parts[0].shape, parts[0].ndim - 1)
    axis = parts[0].ndim - 1
    low = lane < 64
    a, b, c, d = parts
    a, c = (
        jnp.where(low, a, pltpu.roll(c, 64, axis)),
        jnp.where(low, pltpu.roll(a, 64, axis), c),
    )
    b, d = (
        jnp.where(low, b, pltpu.roll(d, 64, axis)),
        jnp.where(low, pltpu.roll(b, 64, axis), d),
    )
    even = (lane & 32) == 0
    a, b = (
        jnp.where(even, a, pltpu.roll(b, 32, axis)),
        jnp.where(even, pltpu.roll(a, 96, axis), b),
    )
    c, d = (
        jnp.where(even, c, pltpu.roll(d, 32, axis)),
        jnp.where(even, pltpu.roll(c, 96, axis), d),
    )
    return a, b, c, d


def border_copies(gx, gy, source, target, send_sem, recv_sem):
    copies = [
        pltpu.make_async_remote_copy(
            src_ref=source.at[first:last],
            dst_ref=target.at[first:last],
            send_sem=send_sem,
            recv_sem=recv_sem,
            device_id=(mod(gx + dr, GX), mod(gy + dc, GY)),
            device_id_type=MESH,
        )
        for (dr, dc), (first, last) in zip(DIRS, PARTS)
    ]
    whole = pltpu.make_async_remote_copy(
        src_ref=source,
        dst_ref=target,
        send_sem=send_sem,
        recv_sem=recv_sem,
        device_id=(mod(gx + 1, GX), gy),
        device_id_type=MESH,
    )
    return copies, whole


def fused_body(
    mid_hbm, grad_hbm, w_hbm, routes_hbm, gates_hbm, band_hbm, ids_hbm,
    col_hbm, col_t_hbm, edge_hbm, row_hbm, back_hbm,
    out,
    routes, gates, band_ids, mid, grad, w, row, back, band, col, col_t, edge_table, shifted, side, deltas, last_pre, spread, total, edge, edges, left_edge,
    border_out, border_in, halo_out, halo_in,
    xs, xr, half, cs, cr, cg, sp, zs, fs, fr,
    w_sem, in_sem, halo_s, halo_r, border_s, border_r,
    x_s, x_r, c_s, c_r, g_s, g_r, p_s, p_r, f_s, f_r,
):
    gx, gy = lax.axis_index("gx"), lax.axis_index("gy")
    w_copies = [
        pltpu.make_async_copy(w_hbm.at[first:last], w.at[first:last], w_sem.at[k])
        for k, (first, last) in enumerate(((0, 1), (1, 2), (2, EXPERTS)))
    ]
    sources = [
        mid_hbm, grad_hbm, row_hbm.at[gx], back_hbm.at[gx],
        band_hbm.at[:, pl.ds(pl.multiple_of(gy * 32, 32), 32), :],
        col_hbm, col_t_hbm, edge_hbm, ids_hbm, routes_hbm, gates_hbm,
    ]
    targets = [mid, grad, row, back, band, col, col_t, edge_table, band_ids, routes, gates]
    in_copies = [
        pltpu.make_async_copy(source, target, in_sem.at[k])
        for k, (source, target) in enumerate(zip(sources, targets))
    ]
    for copy in in_copies[:1] + w_copies[:1] + in_copies[9:] + in_copies[1:2] + w_copies[1:] + in_copies[2:9]:
        copy.start()
    barrier = pltpu.get_barrier_semaphore()
    partners = [(gx, mod(gy + d, GY)) for d in range(1, GY)]
    partners += [(mod(gx + d, GX), gy) for d in range(1, GX)]
    partners += [(mod(gx + dr, GX), mod(gy + dc, GY)) for dr, dc in DIRS[4:]]
    for device in partners:
        pl.semaphore_signal(barrier, inc=1, device_id=device, device_id_type=MESH)

    above = jnp.where(gx > 0, 1.0, 0.0)
    below = jnp.where(gx < GX - 1, 1.0, 0.0)
    left = jnp.where(gy > 0, 1.0, 0.0)
    right = jnp.where(gy < GY - 1, 1.0, 0.0)

    in_copies[0].wait()
    halo_out[0:32] = mid[ROWS - 1]
    halo_out[32:64] = mid[0]
    rim = [mid[:, 16:32, :].astype(F32)[:, 15, :], mid[:, 0:16, :].astype(F32)[:, 0, :]]
    halo_out[64:112] = rim[0].astype(BF)
    halo_out[112:160] = rim[1].astype(BF)
    for k, r in enumerate((ROWS - 1, ROWS - 1, 0, 0)):
        corner = jnp.broadcast_to(rim[k % 2][r : r + 1], (16, CH)).astype(BF)
        halo_out[160 + 16 * k : 176 + 16 * k] = corner
    pl.semaphore_wait(barrier, len(partners))
    halo, halo_all = border_copies(gx, gy, halo_out, halo_in, halo_s.at[0], halo_r.at[0])
    for copy in halo:
        copy.start()
    in_copies[1].wait()
    for b in (0, 2):
        spread[b] = jnp.zeros((OPEN, COLS, CH), F32)
    spread[1, 0] = jnp.zeros((COLS, CH), F32)
    spread[1, 1 : ROWS + 1] = grad[...].astype(F32)
    spread[1, ROWS + 1 :] = jnp.zeros((OPEN - ROWS - 1, COLS, CH), F32)
    edges[...] = jnp.zeros_like(edges)
    last_pre[...] = jnp.zeros_like(last_pre)
    place = lax.broadcasted_iota(jnp.int32, (COLS, CH), 0)

    def shift_row(r, line):
        shifted[1, r] = line.astype(BF)
        shifted[0, r] = pltpu.roll(line, 1, 0).astype(BF)
        shifted[2, r] = pltpu.roll(line, COLS - 1, 0).astype(BF)

    def own_shift(r, _):
        shift_row(r + 1, mid[r].astype(F32))
        return 0

    lax.fori_loop(0, ROWS, own_shift, 0, unroll=4)
    halo_all.wait()
    shift_row(0, halo_in[0:32].astype(F32) * above)
    shift_row(ROWS + 1, halo_in[32:64].astype(F32) * below)
    side[0, 8 : 8 + ROWS] = halo_in[64:112].astype(F32) * left
    side[1, 8 : 8 + ROWS] = halo_in[112:160].astype(F32) * right
    side[0, 7:8] = halo_in[160:176].astype(F32)[0:1] * (above * left)
    side[1, 7:8] = halo_in[176:192].astype(F32)[0:1] * (above * right)
    side[0, 8 + ROWS : 9 + ROWS] = halo_in[192:208].astype(F32)[0:1] * (below * left)
    side[1, 8 + ROWS : 9 + ROWS] = halo_in[208:224].astype(F32)[0:1] * (below * right)
    place16 = lax.broadcasted_iota(jnp.int32, (16, CH), 0)

    def fix_row(r, _):
        before = side[0, pl.ds(r + 7, 1), :]
        after = side[1, pl.ds(r + 7, 1), :]
        first = shifted[0, r, 0:16, :].astype(F32)
        shifted[0, r, 0:16, :] = jnp.where(place16 == 0, before, first).astype(BF)
        last = shifted[2, r, 16:32, :].astype(F32)
        shifted[2, r, 16:32, :] = jnp.where(place16 == 15, after, last).astype(BF)
        return 0

    lax.fori_loop(0, ROWS + 2, fix_row, 0, unroll=5)

    def expert(t, s):
        return routes[t // 2, t % 2, s - 2] + 2

    def slope(t, s, pre):
        rt, cols = t // 2, slice((t % 2) * 16, (t % 2) * 16 + 16)
        g = grad[rt * 16 : rt * 16 + 16, cols, :].reshape(256, CH).astype(F32)
        gate = gates[rt, t % 2, s] * 0.5
        deltas[t, s] = (gelu_slope_twice(pre) * (g * gate)).astype(BF)

    def forward(s, kernel_of):
        for t in range(TILES):
            rt, cols = t // 2, slice((t % 2) * 16, (t % 2) * 16 + 16)
            pieces = [
                shifted[b, rt * 16 + a : rt * 16 + a + 16, cols, :].reshape(256, CH)
                for a in range(3)
                for b in range(3)
            ]
            pre = jnp.dot(
                jnp.concatenate(pieces, axis=1), w[kernel_of(t, s)], preferred_element_type=F32
            )
            if t == 0:
                slope(TILES - 1, jnp.maximum(s - 1, 0), last_pre[...])
            if t < TILES - 1:
                slope(t, s, pre)
            else:
                last_pre[...] = pre

    def forward_shared(s, _):
        forward(s, lambda t, s: s)
        return 0

    def forward_routed(s, _):
        forward(s, expert)
        return 0

    w_copies[0].wait()
    w_copies[1].wait()
    in_copies[9].wait()
    in_copies[10].wait()
    lax.fori_loop(0, 2, forward_shared, 0)
    w_copies[2].wait()
    lax.fori_loop(2, SLOTS, forward_routed, 0)
    slope(TILES - 1, SLOTS - 1, last_pre[...])

    def along_y(source, target, d, send, recv):
        return pltpu.make_async_remote_copy(
            src_ref=source, dst_ref=target, send_sem=send, recv_sem=recv,
            device_id=(gx, mod(gy + d, GY)), device_id_type=MESH,
        )

    def along_x(source, target, d, send, recv):
        return pltpu.make_async_remote_copy(
            src_ref=source, dst_ref=target, send_sem=send, recv_sem=recv,
            device_id=(mod(gx + d, GX), gy), device_id_type=MESH,
        )

    def x_rows(rt, half):
        _, groups, start = CHUNKS[rt]
        at = start + groups * 16
        return slice(at, start + groups * 32 + 16) if half else slice(start, at)

    def opened(r, half):
        if half == 0:
            middle = jnp.where(place16 >= 1, pltpu.roll(spread[1, r, 0:16, :], 1, 0), 0.0)
            ahead = jnp.where(place16 >= 2, pltpu.roll(spread[2, r, 0:16, :], 2, 0), 0.0)
            return spread[0, r, 0:16, :] + middle + ahead
        middle = pltpu.roll(spread[1, r, 8:32, :], 1, 0)[8:24]
        ahead = pltpu.roll(spread[2, r, 8:32, :], 2, 0)[8:24]
        return spread[0, r, 16:32, :] + middle + ahead

    def leave(rt, half):
        first, groups, start = CHUNKS[rt]
        base = start + half * groups * 16

        def split_group(k, _):
            lines = [opened(4 * (first + k) + q, half) for q in range(4)]
            for jt in range(2):
                lanes = slice(jt * 128, jt * 128 + 128)
                for s, part in enumerate(transpose_blocks([line[:, lanes] for line in lines])):
                    xs[jt * 4 + s, pl.ds(pl.multiple_of(base + 16 * k, 16), 16), :] = part.astype(BF)
            return 0

        lax.fori_loop(0, groups, split_group, 0, unroll=groups)
        if half:
            rows = slice(4 * first, 4 * first + 4 * groups)
            last = start + groups * 32
            for jt in range(2):
                lanes = slice(jt * 128, jt * 128 + 128)
                edge[0, jt, rows] = (
                    spread[1, rows, COLS - 1, lanes] + spread[2, rows, COLS - 2, lanes]
                )
                edge[1, jt, rows] = spread[2, rows, COLS - 1, lanes]
                for q in range(4):
                    for s in range(2):
                        edges[q, jt, s * 8 : s * 8 + groups] = edge[
                            s, jt, pl.ds(4 * first + q, groups, stride=4), :
                        ]
                for s, part in enumerate(transpose_blocks([edges[q, jt] for q in range(4)])):
                    xs[jt * 4 + s, last : last + 16, :] = part.astype(BF)
        rows = x_rows(rt, half)
        for d in AHEAD_Y:
            along_y(
                xs.at[mod(gy + d, GY), rows], xr.at[gy, rows], d,
                x_s.at[2 * rt + half], x_r.at[2 * rt + half],
            ).start()

    for rt in range(3):

        def backward(ct, _):
            cols = pl.ds(pl.multiple_of(ct * 16, 16), 16)
            d = jnp.concatenate([deltas[2 * rt + ct, s] for s in range(SLOTS)], axis=1)
            chosen = [0, 1] + [routes[rt, ct, s - 2] + 2 for s in range(2, SLOTS)]
            for a in range(3):
                for b in range(3):
                    tap = 3 * a + b
                    kernels = jnp.concatenate(
                        [w[e, tap * CH : (tap + 1) * CH, :] for e in chosen], axis=1
                    )
                    r = lax.dot_general(
                        d, kernels, (((1,), (1,)), ((), ())), preferred_element_type=F32
                    )
                    spread[b, rt * 16 + a : rt * 16 + a + 16, cols, :] += r.reshape(16, 16, CH)

            @pl.when(ct == 0)
            def _():
                leave(rt, 0)

            @pl.when(ct == 1)
            def _():
                leave(rt, 1)

            return 0

        lax.fori_loop(0, 2, backward, 0)

    def own_row(r, _):
        ahead = jnp.where(place > 0, pltpu.roll(spread[2, r], 1, 0), 0.0)
        behind = jnp.where(place < COLS - 1, pltpu.roll(spread[0, r], COLS - 1, 0), 0.0)
        total[r] = spread[1, r] + ahead + behind
        return 0

    lax.fori_loop(0, ROWS + 2, own_row, 0, unroll=5)
    border_out[0:32] = total[ROWS + 1].astype(BF)
    border_out[32:64] = total[0].astype(BF)
    for jt in range(2):
        lanes = slice(jt * 128, jt * 128 + 128)
        left_edge[jt, 0 : ROWS + 2] = spread[0, 0 : ROWS + 2, 0, lanes]
        border_out[64:112, lanes] = edge[1, jt, 1 : ROWS + 1].astype(BF)
        border_out[112:160, lanes] = left_edge[jt, 1 : ROWS + 1].astype(BF)
        for k, r in enumerate((ROWS + 1, ROWS + 1, 0, 0)):
            corner = left_edge[jt, r : r + 1, :] if k % 2 else edge[1, jt, r : r + 1, :]
            border_out[160 + 16 * k : 176 + 16 * k, lanes] = jnp.broadcast_to(
                corner, (16, 128)
            ).astype(BF)
    border, border_all = border_copies(
        gx, gy, border_out, border_in, border_s.at[0], border_r.at[0]
    )
    for copy in border:
        copy.start()
    xr[gy] = xs[gy]

    for copy in in_copies[2:9]:
        copy.wait()
    for chunk, (first, groups, start) in enumerate(CHUNKS):
        for part in range(2):
            rows = x_rows(chunk, part)
            t = 2 * chunk + part
            along_y(xs.at[1:GY, rows], xr.at[1:GY, rows], 1, x_s.at[t], x_r.at[t]).wait()
        last = start + groups * 32
        rim = jnp.dot(
            edge_table[0 : groups * 64],
            xr[:, last : last + 16].reshape(128, 128),
            preferred_element_type=F32,
        )
        for pair in range(0, groups, 2):
            width = min(2, groups - pair)
            data = []
            for k in range(pair, pair + width):
                halves = [start + 16 * (groups * part + k) for part in range(2)]
                halves = [xr[:, at : at + 16].reshape(128, 128) for at in halves]
                data.append(jnp.concatenate(halves, axis=0))
            c = jnp.dot(col[...], jnp.concatenate(data, axis=1), preferred_element_type=F32)
            for k in range(width):
                one = c[:, k * 128 : k * 128 + 128] + rim[(pair + k) * 64 : (pair + k) * 64 + 64]
                for part in range(2):
                    parts = [one[part * 32 + 8 * p : part * 32 + 8 * p + 8] for p in range(4)]
                    for q, block in enumerate(transpose_blocks(parts)):
                        r = part * OPEN + 4 * (first + pair + k) + q
                        half[pl.ds(r, 8, stride=2 * OPEN), :] = block
    forward_scale = 1.0 / math.sqrt(H * W)
    for pair in range(4):
        data = [
            half[(2 * pair + k) * 2 * OPEN : (2 * pair + k + 1) * 2 * OPEN].astype(BF)
            for k in range(2)
        ]
        c = jnp.dot(row[...], jnp.concatenate(data, axis=1), preferred_element_type=F32)
        c = (c * forward_scale).astype(BF)
        for k in range(2):
            for mh in range(2):
                cs[mh * 8 + 2 * pair + k] = c[mh * 64 : mh * 64 + 64, k * 128 : k * 128 + 128]
    parts_of = [slice(0, 32), slice(32, 64)]

    def c_copy(part, source, target, d=1):
        rows = parts_of[part]
        return along_x(cs.at[source, rows], cr.at[target, rows], d, c_s.at[part], c_r.at[part])

    def g_copy(part, source, target, d=1):
        rows = parts_of[part]
        return along_y(cg.at[source, rows], cg.at[target, rows], d, g_s.at[part], g_r.at[part])

    def p_copy(part, source, target, d=1):
        rows = parts_of[part]
        return along_x(sp.at[source, rows], sp.at[target, rows], d, p_s.at[part], p_r.at[part])

    others_x, others_y = slice(1, GX), slice(1, GY)
    for part in range(2):
        for d in AHEAD_X:
            c_copy(part, mod(gx + d, GX), gx, d).start()
    cr[gx] = cs[gx]

    border_all.wait()
    total[1] += border_in[0:32].astype(F32) * above
    total[ROWS] += border_in[32:64].astype(F32) * below
    own = slice(1, ROWS + 1)
    total[own, 0, :] += border_in[64:112].astype(F32) * left
    total[own, COLS - 1, :] += border_in[112:160].astype(F32) * right
    total[1, 0:1, :] += border_in[160:176].astype(F32)[0:1] * (above * left)
    total[1, COLS - 1 : COLS, :] += border_in[176:192].astype(F32)[0:1] * (above * right)
    total[ROWS, 0:1, :] += border_in[192:208].astype(F32)[0:1] * (below * left)
    total[ROWS, COLS - 1 : COLS, :] += border_in[208:224].astype(F32)[0:1] * (below * right)

    n8 = lax.rem(gx, 8)
    mh = gx // 8
    lane64 = lax.broadcasted_iota(jnp.int32, (32, KH), 1)
    row64 = lax.broadcasted_iota(jnp.int32, (32, KH), 0)
    block_of_lane = lax.broadcasted_iota(jnp.int32, (32, 512), 1) >> 5
    lane_block = lax.broadcasted_iota(jnp.int32, (32, 128), 1) >> 5
    band_of = []
    for n4 in range(4):
        ids = jnp.broadcast_to(band_ids[pl.ds(4 * n8 + n4, 1), :], (32, KH))
        band_of.append(jnp.sum(jnp.where(lane64 == row64 + 32 * mh, ids, 0), axis=1, keepdims=True))

    for part in range(2):
        rows = parts_of[part]
        c_copy(part, others_x, others_x).wait()
        coef = cr[0, rows].astype(F32)
        for k in range(1, GX):
            coef = coef + cr[k, rows].astype(F32)
        cg[gy, rows] = coef.astype(BF)
        for d in AHEAD_Y:
            g_copy(part, gy, gy, d).start()

    mixer = band[...].reshape(512, CH)
    for part in range(2):
        rows = parts_of[part]
        g_copy(part, others_y, others_y).wait()
        inputs = [
            transpose_blocks([cg[jt * 4 + p, rows].astype(F32) for p in range(4)])
            for jt in range(2)
        ]
        spec = jnp.zeros((32, 128), F32)
        modes = [
            jnp.concatenate([inputs[0][n4], inputs[1][n4]], axis=1).astype(BF) for n4 in range(4)
        ]
        mixed = lax.dot_general(
            jnp.concatenate(modes, axis=0), mixer, (((1,), (1,)), ((), ())),
            preferred_element_type=F32,
        )
        for n4 in range(4):
            z = jnp.where(block_of_lane == band_of[n4], mixed[n4 * 32 : n4 * 32 + 32], 0.0)
            y = z[:, 0:128] + z[:, 128:256] + z[:, 256:384] + z[:, 384:512]
            y = y + pltpu.roll(y, 64, 1)
            y = y + pltpu.roll(y, 32, 1)
            spec = jnp.where(lane_block == n4, y, spec)
        sp[gx, rows] = spec.astype(BF)
        for d in AHEAD_X:
            p_copy(part, gx, gx, d).start()
    for part in range(2):
        p_copy(part, others_x, others_x).wait()

    inverse_scale = 1.0 / math.sqrt(2 * KH * KW)
    for pair in range(4):
        data = [
            jnp.concatenate([sp[2 * pair + k], sp[8 + 2 * pair + k]], axis=0) for k in range(2)
        ]
        z = jnp.dot(back[...], jnp.concatenate(data, axis=1), preferred_element_type=F32)
        z = z * inverse_scale
        for k in range(2):
            zs[(2 * pair + k) * 96 : (2 * pair + k + 1) * 96, :] = z[:, k * 128 : k * 128 + 128]

    def f_copy(sixth, source, target, d=1):
        rows = slice(2 * sixth, 2 * sixth + 2)
        return along_y(fs.at[source, rows], fr.at[target, rows], d, f_s.at[sixth], f_r.at[sixth])

    for sixth in range(6):
        for pair in (sixth,):
            columns = []
            for k in range(2):
                pieces = []
                for part in range(2):
                    r = part * ROWS + 4 * (2 * pair + k)
                    parts = [zs[pl.ds(r + q, 8, stride=2 * ROWS), :] for q in range(4)]
                    pieces += list(transpose_blocks(parts))
                columns.append(jnp.concatenate(pieces, axis=0))
            data = jnp.concatenate(columns, axis=1).astype(BF)
            f = jnp.dot(col_t[...], data, preferred_element_type=F32).astype(BF)
            for k in range(2):
                for j in range(GY):
                    fs[j, 2 * pair + k] = f[j * 32 : j * 32 + 32, k * 128 : k * 128 + 128]
        for d in AHEAD_Y:
            f_copy(sixth, mod(gy + d, GY), gy, d).start()
    fr[gy] = fs[gy]

    def join_group(g, _):
        for jt in range(2):
            lanes = slice(jt * 128, jt * 128 + 128)
            parts = [fr[jt * 4 + s, g].astype(F32) for s in range(4)]
            for q, part in enumerate(transpose_blocks(parts)):
                out[4 * g + q, :, lanes] = (total[4 * g + q + 1, :, lanes] + part).astype(BF)
        return 0

    for sixth in range(6):
        f_copy(sixth, others_y, others_y).wait()
        lax.fori_loop(2 * sixth, 2 * sixth + 2, join_group, 0, unroll=2)


ANY = pl.BlockSpec(memory_space=pl.ANY)


def dma(*shape):
    return pltpu.SemaphoreType.DMA(shape)


def body(saved_mid, out_grad, expert_weight, routes, gates, band_matrix, band_ids):
    return pl.pallas_call(
        fused_body,
        name="fused",
        out_shape=pltpu.VMEM((ROWS, COLS, CH), BF),
        in_specs=[ANY, ANY, ANY, ANY, ANY, ANY, ANY, ANY, ANY, ANY, ANY, ANY],
        out_specs=pl.BlockSpec(memory_space=pltpu.VMEM),
        scratch_shapes=[
            pltpu.SMEM((3, 2, 4), jnp.int32),
            pltpu.SMEM((3, 2, SLOTS), F32),
            pltpu.VMEM((KW, KH), jnp.int32),
            pltpu.VMEM((ROWS, COLS, CH), BF),
            pltpu.VMEM((ROWS, COLS, CH), BF),
            pltpu.VMEM((EXPERTS, 9 * CH, CH), BF),
            pltpu.VMEM((128, 2 * OPEN), BF),
            pltpu.VMEM((2 * ROWS, 128), BF),
            pltpu.VMEM((16, 32, CH), BF),
            pltpu.VMEM((64, 256), BF),
            pltpu.VMEM((256, 64), BF),
            pltpu.VMEM((320, 128), BF),
            pltpu.VMEM((3, ROWS + 2, COLS, CH), BF),
            pltpu.VMEM((2, 64, CH), F32),
            pltpu.VMEM((TILES, SLOTS, 256, CH), BF),
            pltpu.VMEM((256, CH), F32),
            pltpu.VMEM((3, OPEN, COLS, CH), F32),
            pltpu.VMEM((OPEN, COLS, CH), F32),
            pltpu.VMEM((2, 2, OPEN + 4, 128), F32),
            pltpu.VMEM((4, 2, 16, 128), F32),
            pltpu.VMEM((2, OPEN + 4, 128), F32),
            *[pltpu.VMEM((224, CH), BF)] * 4,
            pltpu.VMEM((GY, 464, 128), BF),
            pltpu.VMEM((GY, 464, 128), BF),
            pltpu.VMEM((8 * 2 * OPEN, 128), F32),
            pltpu.VMEM((GX, 64, 128), BF),
            pltpu.VMEM((GX, 64, 128), BF),
            pltpu.VMEM((GY, 64, 128), BF),
            pltpu.VMEM((GX, 64, 128), BF),
            pltpu.VMEM((8 * 2 * ROWS, 128), F32),
            pltpu.VMEM((GY, 12, 32, 128), BF),
            pltpu.VMEM((GY, 12, 32, 128), BF),
            dma(3), dma(11), dma(1), dma(1), dma(1), dma(1),
            dma(6), dma(6), dma(2), dma(2), dma(2), dma(2), dma(2), dma(2), dma(6), dma(6),
        ],
        compiler_params=pltpu.CompilerParams(
            collective_id=0, has_side_effects=True, vmem_limit_bytes=66_000_000
        ),
    )(
        saved_mid, out_grad, expert_weight.reshape(EXPERTS, 9 * CH, CH), routes, gates,
        band_matrix, band_ids.T, jnp.asarray(OPEN_TABLE, BF), jnp.asarray(COL_TABLE, BF),
        jnp.asarray(EDGE_TABLE, BF), jnp.asarray(ROW_TABLE, BF), jnp.asarray(BACK_TABLE, BF),
    )


def solution(mesh):
    placed = (
        P("gx", "gy", None),
        P("gx", "gy", None),
        P(),
        P("gx", "gy", None),
        P("gx", "gy", None),
        P(),
        P(),
    )
    return jax.shard_map(
        body, mesh=mesh, in_specs=placed, out_specs=P("gx", "gy", None), check_vma=False
    )
```

```python
import math

import jax
import jax.numpy as jnp
import numpy as np
from jax import lax
from jax.experimental import pallas as pl
from jax.experimental.pallas import tpu as pltpu
from jax.sharding import PartitionSpec as P

F32 = jnp.float32
BF = jnp.bfloat16
MESH = pl.DeviceIdType.MESH
GX, GY = 16, 8
ROWS, COLS, CH = 48, 32, 256
KH, KW = 64, 32
H, W = 768, 256
EXPERTS, SLOTS, TILES = 10, 6, 6
OPEN = ROWS + 4
PIECES = 4
CHUNKS = ((0, 4, 0), (4, 4, 144), (8, 5, 288))

DIRS = ((1, 0), (-1, 0), (0, 1), (0, -1), (1, 1), (1, -1), (-1, 1), (-1, -1))
AHEAD_X = (8, 10, 6, 9, 7, 11, 5, 12, 4, 13, 3, 14, 2, 15, 1)
AHEAD_Y = (4, 5, 3, 6, 2, 7, 1)
PARTS = ((0, 32), (32, 64), (64, 112), (112, 160), (160, 176), (176, 192), (192, 208), (208, 224))


def mod(value, count):
    return lax.rem(value + count, count)


def tables():
    n = (4 * np.arange(8)[None, :] + np.arange(4)[:, None]).reshape(-1)

    def wave(columns):
        theta = 2 * np.pi * ((n[:, None] * columns[None, :]) % W) / W
        return np.concatenate([np.cos(theta), np.sin(theta)])

    opened = np.zeros((64, 2, GY, 16))
    edge = np.zeros((5, 64, GY, 16))
    for j in range(GY):
        for part in range(2):
            columns = COLS * j + 16 * part - 1 + np.arange(16)
            opened[:, part, j] = wave(columns) * (columns >= 0)
        for side, column in enumerate((COLS * j + COLS - 1, COLS * j + COLS)):
            if column < W:
                for g in range(5):
                    edge[g, :, j, side * 8 + g] = wave(np.array([column]))[:, 0]
    m = np.arange(KH)
    freq = np.where(m < KH // 2, m, H - KH + m)
    row = np.zeros((GX, 2, 2, 32, 2, OPEN))
    for gx in range(GX):
        h = ROWS * gx - 1 + np.arange(OPEN)
        phase = 2 * np.pi * ((freq[:, None] * h[None, :]) % H) / H
        keep = (h >= 0) & (h < H) & (np.arange(OPEN) < ROWS + 2)
        rc = (np.cos(phase) * keep).reshape(2, 32, OPEN)
        rs = (np.sin(phase) * keep).reshape(2, 32, OPEN)
        row[gx, :, 0, :, 0], row[gx, :, 0, :, 1] = rc, -rs
        row[gx, :, 1, :, 0], row[gx, :, 1, :, 1] = rs, rc
    back = row[..., 1 : ROWS + 1].reshape(GX, 128, 2 * ROWS).transpose(0, 2, 1)
    row = row.reshape(GX, 128, 2 * OPEN)
    return opened.reshape(64, 256), wave(np.arange(W)).T, edge.reshape(320, 128), row, back


OPEN_TABLE, COL_TABLE, EDGE_TABLE, ROW_TABLE, BACK_TABLE = tables()


def gelu_slope_twice(values):
    density = jnp.exp2((values * values) * (-0.5 * math.log2(math.e)))
    return (1.0 + lax.erf(values * math.sqrt(0.5))) + (values * math.sqrt(2.0 / math.pi)) * density


def transpose_blocks(parts):
    lane = lax.broadcasted_iota(jnp.int32, parts[0].shape, parts[0].ndim - 1)
    axis = parts[0].ndim - 1
    low = lane < 64
    a, b, c, d = parts
    a, c = (
        jnp.where(low, a, pltpu.roll(c, 64, axis)),
        jnp.where(low, pltpu.roll(a, 64, axis), c),
    )
    b, d = (
        jnp.where(low, b, pltpu.roll(d, 64, axis)),
        jnp.where(low, pltpu.roll(b, 64, axis), d),
    )
    even = (lane & 32) == 0
    a, b = (
        jnp.where(even, a, pltpu.roll(b, 32, axis)),
        jnp.where(even, pltpu.roll(a, 96, axis), b),
    )
    c, d = (
        jnp.where(even, c, pltpu.roll(d, 32, axis)),
        jnp.where(even, pltpu.roll(c, 96, axis), d),
    )
    return a, b, c, d


def border_copies(gx, gy, source, target, send_sem, recv_sem):
    copies = [
        pltpu.make_async_remote_copy(
            src_ref=source.at[first:last],
            dst_ref=target.at[first:last],
            send_sem=send_sem,
            recv_sem=recv_sem,
            device_id=(mod(gx + dr, GX), mod(gy + dc, GY)),
            device_id_type=MESH,
        )
        for (dr, dc), (first, last) in zip(DIRS, PARTS)
    ]
    whole = pltpu.make_async_remote_copy(
        src_ref=source,
        dst_ref=target,
        send_sem=send_sem,
        recv_sem=recv_sem,
        device_id=(mod(gx + 1, GX), gy),
        device_id_type=MESH,
    )
    return copies, whole


def fused_body(
    mid_hbm, grad_hbm, w_hbm, routes_hbm, gates_hbm, band_hbm, ids_hbm,
    col_hbm, col_t_hbm, edge_hbm, row_hbm, back_hbm,
    out,
    routes, gates, band_ids, mid, grad, w, row, back, band, col, col_t, edge_table, shifted, side, deltas, last_pre, spread, total, edge, edges, left_edge,
    border_out, border_in, halo_out, halo_in,
    xs, xr, half, cs, cr, cg, sp, zs, fs, fr,
    w_sem, in_sem, halo_s, halo_r, border_s, border_r,
    x_s, x_r, c_s, c_r, g_s, g_r, p_s, p_r, f_s, f_r,
):
    gx, gy = lax.axis_index("gx"), lax.axis_index("gy")
    w_copies = [
        pltpu.make_async_copy(w_hbm.at[first:last], w.at[first:last], w_sem.at[k])
        for k, (first, last) in enumerate(((0, 1), (1, 2), (2, EXPERTS)))
    ]
    sources = [
        mid_hbm, grad_hbm, row_hbm.at[gx], back_hbm.at[gx],
        band_hbm.at[:, pl.ds(pl.multiple_of(gy * 32, 32), 32), :],
        col_hbm, col_t_hbm, edge_hbm, ids_hbm, routes_hbm, gates_hbm,
    ]
    targets = [mid, grad, row, back, band, col, col_t, edge_table, band_ids, routes, gates]
    in_copies = [
        pltpu.make_async_copy(source, target, in_sem.at[k])
        for k, (source, target) in enumerate(zip(sources, targets))
    ]
    in_copies[0].start()
    barrier = pltpu.get_barrier_semaphore()
    partners = [(mod(gx + dr, GX), mod(gy + dc, GY)) for dr, dc in DIRS]
    partners += [(mod(gx + d, GX), gy) for d in range(2, GX - 1)]
    partners += [(gx, mod(gy + d, GY)) for d in range(2, GY - 1)]
    for device in partners:
        pl.semaphore_signal(barrier, inc=1, device_id=device, device_id_type=MESH)
    for copy in w_copies[:1] + in_copies[9:] + in_copies[1:2] + w_copies[1:] + in_copies[2:9]:
        copy.start()

    above = jnp.where(gx > 0, 1.0, 0.0)
    below = jnp.where(gx < GX - 1, 1.0, 0.0)
    left = jnp.where(gy > 0, 1.0, 0.0)
    right = jnp.where(gy < GY - 1, 1.0, 0.0)

    in_copies[0].wait()
    halo_out[0:32] = mid[ROWS - 1]
    halo_out[32:64] = mid[0]
    rim = [mid[:, 16:32, :].astype(F32)[:, 15, :], mid[:, 0:16, :].astype(F32)[:, 0, :]]
    halo_out[64:112] = rim[0].astype(BF)
    halo_out[112:160] = rim[1].astype(BF)
    for k, r in enumerate((ROWS - 1, ROWS - 1, 0, 0)):
        corner = jnp.broadcast_to(rim[k % 2][r : r + 1], (16, CH)).astype(BF)
        halo_out[160 + 16 * k : 176 + 16 * k] = corner
    pl.semaphore_wait(barrier, len(partners))
    halo, halo_all = border_copies(gx, gy, halo_out, halo_in, halo_s.at[0], halo_r.at[0])
    for copy in halo:
        copy.start()
    in_copies[1].wait()
    for b in (0, 2):
        spread[b] = jnp.zeros((OPEN, COLS, CH), F32)
    spread[1, 0] = jnp.zeros((COLS, CH), F32)
    spread[1, 1 : ROWS + 1] = grad[...].astype(F32)
    spread[1, ROWS + 1 :] = jnp.zeros((OPEN - ROWS - 1, COLS, CH), F32)
    edges[...] = jnp.zeros_like(edges)
    last_pre[...] = jnp.zeros_like(last_pre)
    place = lax.broadcasted_iota(jnp.int32, (COLS, CH), 0)

    def shift_row(r, line):
        shifted[1, r] = line.astype(BF)
        shifted[0, r] = pltpu.roll(line, 1, 0).astype(BF)
        shifted[2, r] = pltpu.roll(line, COLS - 1, 0).astype(BF)

    def own_shift(r, _):
        shift_row(r + 1, mid[r].astype(F32))
        return 0

    lax.fori_loop(0, ROWS, own_shift, 0, unroll=4)
    halo_all.wait()
    shift_row(0, halo_in[0:32].astype(F32) * above)
    shift_row(ROWS + 1, halo_in[32:64].astype(F32) * below)
    side[0, 8 : 8 + ROWS] = halo_in[64:112].astype(F32) * left
    side[1, 8 : 8 + ROWS] = halo_in[112:160].astype(F32) * right
    side[0, 7:8] = halo_in[160:176].astype(F32)[0:1] * (above * left)
    side[1, 7:8] = halo_in[176:192].astype(F32)[0:1] * (above * right)
    side[0, 8 + ROWS : 9 + ROWS] = halo_in[192:208].astype(F32)[0:1] * (below * left)
    side[1, 8 + ROWS : 9 + ROWS] = halo_in[208:224].astype(F32)[0:1] * (below * right)
    place16 = lax.broadcasted_iota(jnp.int32, (16, CH), 0)

    def fix_row(r, _):
        before = side[0, pl.ds(r + 7, 1), :]
        after = side[1, pl.ds(r + 7, 1), :]
        first = shifted[0, r, 0:16, :].astype(F32)
        shifted[0, r, 0:16, :] = jnp.where(place16 == 0, before, first).astype(BF)
        last = shifted[2, r, 16:32, :].astype(F32)
        shifted[2, r, 16:32, :] = jnp.where(place16 == 15, after, last).astype(BF)
        return 0

    lax.fori_loop(0, ROWS + 2, fix_row, 0, unroll=5)

    def expert(t, s):
        return routes[t // 2, t % 2, s - 2] + 2

    def slope(t, s, pre, low=0, high=16):
        top = (t // 2) * 16
        cols = slice((t % 2) * 16, (t % 2) * 16 + 16)
        g = grad[top + low : top + high, cols, :].reshape(-1, CH).astype(F32)
        gate = gates[t // 2, t % 2, s] * 0.5
        values = (gelu_slope_twice(pre) * (g * gate)).astype(BF)
        deltas[t, s, low * 16 : high * 16] = values

    def forward(s, kernel_of):
        for t in range(TILES):
            top = (t // 2) * 16
            cols = slice((t % 2) * 16, (t % 2) * 16 + 16)
            for low in (0, 8):
                pieces = [
                    shifted[b, top + low + a : top + low + a + 8, cols, :].reshape(128, CH)
                    for a in range(3)
                    for b in range(3)
                ]
                pre = jnp.dot(
                    jnp.concatenate(pieces, axis=1), w[kernel_of(t, s)], preferred_element_type=F32
                )
                if t == 0 and low == 0:
                    slope(TILES - 1, jnp.maximum(s - 1, 0), last_pre[...], 8)
                if t < TILES - 1 or low == 0:
                    slope(t, s, pre, low, low + 8)
                else:
                    last_pre[...] = pre

    def forward_shared(s, _):
        forward(s, lambda t, s: s)
        return 0

    def forward_routed(s, _):
        forward(s, expert)
        return 0

    w_copies[0].wait()
    w_copies[1].wait()
    in_copies[9].wait()
    in_copies[10].wait()
    lax.fori_loop(0, 2, forward_shared, 0)
    w_copies[2].wait()
    lax.fori_loop(2, SLOTS, forward_routed, 0)
    slope(TILES - 1, SLOTS - 1, last_pre[...], 8)

    def along_y(source, target, d, send, recv):
        return pltpu.make_async_remote_copy(
            src_ref=source, dst_ref=target, send_sem=send, recv_sem=recv,
            device_id=(gx, mod(gy + d, GY)), device_id_type=MESH,
        )

    def along_x(source, target, d, send, recv):
        return pltpu.make_async_remote_copy(
            src_ref=source, dst_ref=target, send_sem=send, recv_sem=recv,
            device_id=(mod(gx + d, GX), gy), device_id_type=MESH,
        )

    def x_rows(rt, half):
        _, groups, start = CHUNKS[rt]
        at = start + groups * 16
        return slice(at, start + groups * 32 + 16) if half else slice(start, at)

    def opened(r, half):
        if half == 0:
            middle = jnp.where(place16 >= 1, pltpu.roll(spread[1, r, 0:16, :], 1, 0), 0.0)
            ahead = jnp.where(place16 >= 2, pltpu.roll(spread[2, r, 0:16, :], 2, 0), 0.0)
            return spread[0, r, 0:16, :] + middle + ahead
        middle = pltpu.roll(spread[1, r, 8:32, :], 1, 0)[8:24]
        ahead = pltpu.roll(spread[2, r, 8:32, :], 2, 0)[8:24]
        return spread[0, r, 16:32, :] + middle + ahead

    def leave(rt, half):
        first, groups, start = CHUNKS[rt]
        base = start + half * groups * 16

        def split_group(k, _):
            lines = [opened(4 * (first + k) + q, half) for q in range(4)]
            for jt in range(2):
                lanes = slice(jt * 128, jt * 128 + 128)
                for s, part in enumerate(transpose_blocks([line[:, lanes] for line in lines])):
                    xs[jt * 4 + s, pl.ds(pl.multiple_of(base + 16 * k, 16), 16), :] = part.astype(BF)
            return 0

        lax.fori_loop(0, groups, split_group, 0, unroll=groups)
        if half:
            rows = slice(4 * first, 4 * first + 4 * groups)
            last = start + groups * 32
            for jt in range(2):
                lanes = slice(jt * 128, jt * 128 + 128)
                edge[0, jt, rows] = (
                    spread[1, rows, COLS - 1, lanes] + spread[2, rows, COLS - 2, lanes]
                )
                edge[1, jt, rows] = spread[2, rows, COLS - 1, lanes]
                for q in range(4):
                    for s in range(2):
                        edges[q, jt, s * 8 : s * 8 + groups] = edge[
                            s, jt, pl.ds(4 * first + q, groups, stride=4), :
                        ]
                for s, part in enumerate(transpose_blocks([edges[q, jt] for q in range(4)])):
                    xs[jt * 4 + s, last : last + 16, :] = part.astype(BF)
        rows = x_rows(rt, half)
        for d in AHEAD_Y:
            along_y(
                xs.at[mod(gy + d, GY), rows], xr.at[gy, rows], d,
                x_s.at[2 * rt + half], x_r.at[2 * rt + half],
            ).start()

    for rt in range(3):

        def backward(ct, _):
            cols = pl.ds(pl.multiple_of(ct * 16, 16), 16)
            d = jnp.concatenate([deltas[2 * rt + ct, s] for s in range(SLOTS)], axis=1)
            chosen = [0, 1] + [routes[rt, ct, s - 2] + 2 for s in range(2, SLOTS)]
            for a in range(3):
                for b in range(3):
                    tap = 3 * a + b
                    kernels = jnp.concatenate(
                        [w[e, tap * CH : (tap + 1) * CH, :] for e in chosen], axis=1
                    )
                    r = lax.dot_general(
                        d, kernels, (((1,), (1,)), ((), ())), preferred_element_type=F32
                    )
                    spread[b, rt * 16 + a : rt * 16 + a + 16, cols, :] += r.reshape(16, 16, CH)

            @pl.when(ct == 0)
            def _():
                leave(rt, 0)

            @pl.when(ct == 1)
            def _():
                leave(rt, 1)

            return 0

        lax.fori_loop(0, 2, backward, 0)

    def own_row(r, _):
        ahead = jnp.where(place > 0, pltpu.roll(spread[2, r], 1, 0), 0.0)
        behind = jnp.where(place < COLS - 1, pltpu.roll(spread[0, r], COLS - 1, 0), 0.0)
        total[r] = spread[1, r] + ahead + behind
        return 0

    lax.fori_loop(0, ROWS + 2, own_row, 0, unroll=5)
    border_out[0:32] = total[ROWS + 1].astype(BF)
    border_out[32:64] = total[0].astype(BF)
    for jt in range(2):
        lanes = slice(jt * 128, jt * 128 + 128)
        left_edge[jt, 0 : ROWS + 2] = spread[0, 0 : ROWS + 2, 0, lanes]
        border_out[64:112, lanes] = edge[1, jt, 1 : ROWS + 1].astype(BF)
        border_out[112:160, lanes] = left_edge[jt, 1 : ROWS + 1].astype(BF)
        for k, r in enumerate((ROWS + 1, ROWS + 1, 0, 0)):
            corner = left_edge[jt, r : r + 1, :] if k % 2 else edge[1, jt, r : r + 1, :]
            border_out[160 + 16 * k : 176 + 16 * k, lanes] = jnp.broadcast_to(
                corner, (16, 128)
            ).astype(BF)
    border, border_all = border_copies(
        gx, gy, border_out, border_in, border_s.at[0], border_r.at[0]
    )
    for copy in border:
        copy.start()
    xr[gy] = xs[gy]

    for copy in in_copies[2:9]:
        copy.wait()
    for chunk, (first, groups, start) in enumerate(CHUNKS):
        for part in range(2):
            rows = x_rows(chunk, part)
            t = 2 * chunk + part
            along_y(xs.at[1:GY, rows], xr.at[1:GY, rows], 1, x_s.at[t], x_r.at[t]).wait()
        last = start + groups * 32
        rim = jnp.dot(
            edge_table[0 : groups * 64],
            xr[:, last : last + 16].reshape(128, 128),
            preferred_element_type=F32,
        )
        for pair in range(0, groups, 2):
            width = min(2, groups - pair)
            data = []
            for k in range(pair, pair + width):
                halves = [start + 16 * (groups * part + k) for part in range(2)]
                halves = [xr[:, at : at + 16].reshape(128, 128) for at in halves]
                data.append(jnp.concatenate(halves, axis=0))
            c = jnp.dot(col[...], jnp.concatenate(data, axis=1), preferred_element_type=F32)
            for k in range(width):
                one = c[:, k * 128 : k * 128 + 128] + rim[(pair + k) * 64 : (pair + k) * 64 + 64]
                for part in range(2):
                    parts = [one[part * 32 + 8 * p : part * 32 + 8 * p + 8] for p in range(4)]
                    for q, block in enumerate(transpose_blocks(parts)):
                        r = part * OPEN + 4 * (first + pair + k) + q
                        half[pl.ds(r, 8, stride=2 * OPEN), :] = block
    forward_scale = 1.0 / math.sqrt(H * W)
    for pair in range(4):
        data = [
            half[(2 * pair + k) * 2 * OPEN : (2 * pair + k + 1) * 2 * OPEN].astype(BF)
            for k in range(2)
        ]
        c = jnp.dot(row[...], jnp.concatenate(data, axis=1), preferred_element_type=F32)
        c = (c * forward_scale).astype(BF)
        for k in range(2):
            for mh in range(2):
                cs[mh * 8 + 2 * pair + k] = c[mh * 64 : mh * 64 + 64, k * 128 : k * 128 + 128]
    halves_of = [slice(0, 32), slice(32, 64)]
    parts_of = [slice(16 * k, 16 * k + 16) for k in range(PIECES)]

    def c_copy(part, source, target, d=1):
        rows = parts_of[part]
        return along_x(cs.at[source, rows], cr.at[target, rows], d, c_s.at[part], c_r.at[part])

    def g_copy(part, source, target, d=1):
        rows = parts_of[part]
        return along_y(cg.at[source, rows], cg.at[target, rows], d, g_s.at[part], g_r.at[part])

    def p_copy(part, source, target, d=1):
        rows = halves_of[part]
        return along_x(sp.at[source, rows], sp.at[target, rows], d, p_s.at[part], p_r.at[part])

    others_x, others_y = slice(1, GX), slice(1, GY)
    for part in range(PIECES):
        for d in AHEAD_X:
            c_copy(part, mod(gx + d, GX), gx, d).start()
    cr[gx] = cs[gx]

    border_all.wait()
    total[1] += border_in[0:32].astype(F32) * above
    total[ROWS] += border_in[32:64].astype(F32) * below
    own = slice(1, ROWS + 1)
    total[own, 0, :] += border_in[64:112].astype(F32) * left
    total[own, COLS - 1, :] += border_in[112:160].astype(F32) * right
    total[1, 0:1, :] += border_in[160:176].astype(F32)[0:1] * (above * left)
    total[1, COLS - 1 : COLS, :] += border_in[176:192].astype(F32)[0:1] * (above * right)
    total[ROWS, 0:1, :] += border_in[192:208].astype(F32)[0:1] * (below * left)
    total[ROWS, COLS - 1 : COLS, :] += border_in[208:224].astype(F32)[0:1] * (below * right)

    n8 = lax.rem(gx, 8)
    mh = gx // 8
    lane64 = lax.broadcasted_iota(jnp.int32, (32, KH), 1)
    row64 = lax.broadcasted_iota(jnp.int32, (32, KH), 0)
    block_of_lane = lax.broadcasted_iota(jnp.int32, (32, 512), 1) >> 5
    lane_block = lax.broadcasted_iota(jnp.int32, (32, 128), 1) >> 5
    band_of = []
    for n4 in range(4):
        ids = jnp.broadcast_to(band_ids[pl.ds(4 * n8 + n4, 1), :], (32, KH))
        band_of.append(jnp.sum(jnp.where(lane64 == row64 + 32 * mh, ids, 0), axis=1, keepdims=True))

    for part in range(PIECES):
        rows = parts_of[part]
        c_copy(part, others_x, others_x).wait()
        coef = cr[0, rows].astype(F32)
        for k in range(1, GX):
            coef = coef + cr[k, rows].astype(F32)
        cg[gy, rows] = coef.astype(BF)
        for d in AHEAD_Y:
            g_copy(part, gy, gy, d).start()

    mixer = band[...].reshape(512, CH)
    for part in range(2):
        rows = halves_of[part]
        for piece in range(part * PIECES // 2, (part + 1) * PIECES // 2):
            g_copy(piece, others_y, others_y).wait()
        inputs = [
            transpose_blocks([cg[jt * 4 + p, rows].astype(F32) for p in range(4)])
            for jt in range(2)
        ]
        spec = jnp.zeros((32, 128), F32)
        modes = [
            jnp.concatenate([inputs[0][n4], inputs[1][n4]], axis=1).astype(BF) for n4 in range(4)
        ]
        mixed = lax.dot_general(
            jnp.concatenate(modes, axis=0), mixer, (((1,), (1,)), ((), ())),
            preferred_element_type=F32,
        )
        for n4 in range(4):
            z = jnp.where(block_of_lane == band_of[n4], mixed[n4 * 32 : n4 * 32 + 32], 0.0)
            y = z[:, 0:128] + z[:, 128:256] + z[:, 256:384] + z[:, 384:512]
            y = y + pltpu.roll(y, 64, 1)
            y = y + pltpu.roll(y, 32, 1)
            spec = jnp.where(lane_block == n4, y, spec)
        sp[gx, rows] = spec.astype(BF)
        for d in AHEAD_X:
            p_copy(part, gx, gx, d).start()
    for part in range(2):
        p_copy(part, others_x, others_x).wait()

    inverse_scale = 1.0 / math.sqrt(2 * KH * KW)
    for pair in range(4):
        data = [
            jnp.concatenate([sp[2 * pair + k], sp[8 + 2 * pair + k]], axis=0) for k in range(2)
        ]
        z = jnp.dot(back[...], jnp.concatenate(data, axis=1), preferred_element_type=F32)
        z = z * inverse_scale
        for k in range(2):
            zs[(2 * pair + k) * 96 : (2 * pair + k + 1) * 96, :] = z[:, k * 128 : k * 128 + 128]

    def f_copy(sixth, source, target, d=1):
        rows = slice(2 * sixth, 2 * sixth + 2)
        return along_y(fs.at[source, rows], fr.at[target, rows], d, f_s.at[sixth], f_r.at[sixth])

    for sixth in range(6):
        for pair in (sixth,):
            columns = []
            for k in range(2):
                pieces = []
                for part in range(2):
                    r = part * ROWS + 4 * (2 * pair + k)
                    parts = [zs[pl.ds(r + q, 8, stride=2 * ROWS), :] for q in range(4)]
                    pieces += list(transpose_blocks(parts))
                columns.append(jnp.concatenate(pieces, axis=0))
            data = jnp.concatenate(columns, axis=1).astype(BF)
            f = jnp.dot(col_t[...], data, preferred_element_type=F32).astype(BF)
            for k in range(2):
                for j in range(GY):
                    fs[j, 2 * pair + k] = f[j * 32 : j * 32 + 32, k * 128 : k * 128 + 128]
        for d in AHEAD_Y:
            f_copy(sixth, mod(gy + d, GY), gy, d).start()
    fr[gy] = fs[gy]

    def join_group(g, _):
        for jt in range(2):
            lanes = slice(jt * 128, jt * 128 + 128)
            parts = [fr[jt * 4 + s, g].astype(F32) for s in range(4)]
            for q, part in enumerate(transpose_blocks(parts)):
                out[4 * g + q, :, lanes] = (total[4 * g + q + 1, :, lanes] + part).astype(BF)
        return 0

    for sixth in range(6):
        f_copy(sixth, others_y, others_y).wait()
        lax.fori_loop(2 * sixth, 2 * sixth + 2, join_group, 0, unroll=2)


ANY = pl.BlockSpec(memory_space=pl.ANY)


def dma(*shape):
    return pltpu.SemaphoreType.DMA(shape)


def body(saved_mid, out_grad, expert_weight, routes, gates, band_matrix, band_ids):
    return pl.pallas_call(
        fused_body,
        name="fused",
        out_shape=pltpu.VMEM((ROWS, COLS, CH), BF),
        in_specs=[ANY, ANY, ANY, ANY, ANY, ANY, ANY, ANY, ANY, ANY, ANY, ANY],
        out_specs=pl.BlockSpec(memory_space=pltpu.VMEM),
        scratch_shapes=[
            pltpu.SMEM((3, 2, 4), jnp.int32),
            pltpu.SMEM((3, 2, SLOTS), F32),
            pltpu.VMEM((KW, KH), jnp.int32),
            pltpu.VMEM((ROWS, COLS, CH), BF),
            pltpu.VMEM((ROWS, COLS, CH), BF),
            pltpu.VMEM((EXPERTS, 9 * CH, CH), BF),
            pltpu.VMEM((128, 2 * OPEN), BF),
            pltpu.VMEM((2 * ROWS, 128), BF),
            pltpu.VMEM((16, 32, CH), BF),
            pltpu.VMEM((64, 256), BF),
            pltpu.VMEM((256, 64), BF),
            pltpu.VMEM((320, 128), BF),
            pltpu.VMEM((3, ROWS + 2, COLS, CH), BF),
            pltpu.VMEM((2, 64, CH), F32),
            pltpu.VMEM((TILES, SLOTS, 256, CH), BF),
            pltpu.VMEM((128, CH), F32),
            pltpu.VMEM((3, OPEN, COLS, CH), F32),
            pltpu.VMEM((OPEN, COLS, CH), F32),
            pltpu.VMEM((2, 2, OPEN + 4, 128), F32),
            pltpu.VMEM((4, 2, 16, 128), F32),
            pltpu.VMEM((2, OPEN + 4, 128), F32),
            *[pltpu.VMEM((224, CH), BF)] * 4,
            pltpu.VMEM((GY, 464, 128), BF),
            pltpu.VMEM((GY, 464, 128), BF),
            pltpu.VMEM((8 * 2 * OPEN, 128), F32),
            pltpu.VMEM((GX, 64, 128), BF),
            pltpu.VMEM((GX, 64, 128), BF),
            pltpu.VMEM((GY, 64, 128), BF),
            pltpu.VMEM((GX, 64, 128), BF),
            pltpu.VMEM((8 * 2 * ROWS, 128), F32),
            pltpu.VMEM((GY, 12, 32, 128), BF),
            pltpu.VMEM((GY, 12, 32, 128), BF),
            dma(3), dma(11), dma(1), dma(1), dma(1), dma(1),
            dma(6), dma(6), *[dma(PIECES)] * 4, dma(2), dma(2), dma(6), dma(6),
        ],
        compiler_params=pltpu.CompilerParams(
            collective_id=0, has_side_effects=True, vmem_limit_bytes=66_000_000
        ),
    )(
        saved_mid, out_grad, expert_weight.reshape(EXPERTS, 9 * CH, CH), routes, gates,
        band_matrix, band_ids.T, jnp.asarray(OPEN_TABLE, BF), jnp.asarray(COL_TABLE, BF),
        jnp.asarray(EDGE_TABLE, BF), jnp.asarray(ROW_TABLE, BF), jnp.asarray(BACK_TABLE, BF),
    )


def solution(mesh):
    placed = (
        P("gx", "gy", None),
        P("gx", "gy", None),
        P(),
        P("gx", "gy", None),
        P("gx", "gy", None),
        P(),
        P(),
    )
    return jax.shard_map(
        body, mesh=mesh, in_specs=placed, out_specs=P("gx", "gy", None), check_vma=False
    )
```

```python
import math

import jax
import jax.numpy as jnp
import numpy as np
from jax import lax
from jax.experimental import pallas as pl
from jax.experimental.pallas import tpu as pltpu
from jax.sharding import PartitionSpec as P

F32 = jnp.float32
BF = jnp.bfloat16
MESH = pl.DeviceIdType.MESH
GX, GY = 16, 8
ROWS, COLS, CH = 48, 32, 256
KH, KW = 64, 32
H, W = 768, 256
EXPERTS, SLOTS, TILES = 10, 6, 6
OPEN = ROWS + 4
PIECES = 4
CHUNKS = ((0, 4, 0), (4, 4, 144), (8, 5, 288))

DIRS = ((1, 0), (-1, 0), (0, 1), (0, -1), (1, 1), (1, -1), (-1, 1), (-1, -1))
AHEAD_X = (8, 10, 6, 9, 7, 11, 5, 12, 4, 13, 3, 14, 2, 15, 1)
AHEAD_Y = (4, 5, 3, 6, 2, 7, 1)
PARTS = ((0, 32), (32, 64), (64, 112), (112, 160), (160, 176), (176, 192), (192, 208), (208, 224))


def mod(value, count):
    return lax.rem(value + count, count)


def tables():
    n = (4 * np.arange(8)[None, :] + np.arange(4)[:, None]).reshape(-1)

    def wave(columns):
        theta = 2 * np.pi * ((n[:, None] * columns[None, :]) % W) / W
        return np.concatenate([np.cos(theta), np.sin(theta)])

    opened = np.zeros((64, 2, GY, 16))
    edge = np.zeros((5, 64, GY, 16))
    for j in range(GY):
        for part in range(2):
            columns = COLS * j + 16 * part - 1 + np.arange(16)
            opened[:, part, j] = wave(columns) * (columns >= 0)
        for side, column in enumerate((COLS * j + COLS - 1, COLS * j + COLS)):
            if column < W:
                for g in range(5):
                    edge[g, :, j, side * 8 + g] = wave(np.array([column]))[:, 0]
    m = np.arange(KH)
    freq = np.where(m < KH // 2, m, H - KH + m)
    row = np.zeros((GX, 2, 2, 32, 2, OPEN))
    for gx in range(GX):
        h = ROWS * gx - 1 + np.arange(OPEN)
        phase = 2 * np.pi * ((freq[:, None] * h[None, :]) % H) / H
        keep = (h >= 0) & (h < H) & (np.arange(OPEN) < ROWS + 2)
        rc = (np.cos(phase) * keep).reshape(2, 32, OPEN)
        rs = (np.sin(phase) * keep).reshape(2, 32, OPEN)
        row[gx, :, 0, :, 0], row[gx, :, 0, :, 1] = rc, -rs
        row[gx, :, 1, :, 0], row[gx, :, 1, :, 1] = rs, rc
    back = row[..., 1 : ROWS + 1].reshape(GX, 128, 2 * ROWS).transpose(0, 2, 1)
    row = row.reshape(GX, 128, 2 * OPEN)
    return opened.reshape(64, 256), wave(np.arange(W)).T, edge.reshape(320, 128), row, back


OPEN_TABLE, COL_TABLE, EDGE_TABLE, ROW_TABLE, BACK_TABLE = tables()


def gelu_slope_twice(values):
    density = jnp.exp2((values * values) * (-0.5 * math.log2(math.e)))
    return (1.0 + lax.erf(values * math.sqrt(0.5))) + (values * math.sqrt(2.0 / math.pi)) * density


def transpose_blocks(parts):
    lane = lax.broadcasted_iota(jnp.int32, parts[0].shape, parts[0].ndim - 1)
    axis = parts[0].ndim - 1
    low = lane < 64
    a, b, c, d = parts
    a, c = (
        jnp.where(low, a, pltpu.roll(c, 64, axis)),
        jnp.where(low, pltpu.roll(a, 64, axis), c),
    )
    b, d = (
        jnp.where(low, b, pltpu.roll(d, 64, axis)),
        jnp.where(low, pltpu.roll(b, 64, axis), d),
    )
    even = (lane & 32) == 0
    a, b = (
        jnp.where(even, a, pltpu.roll(b, 32, axis)),
        jnp.where(even, pltpu.roll(a, 96, axis), b),
    )
    c, d = (
        jnp.where(even, c, pltpu.roll(d, 32, axis)),
        jnp.where(even, pltpu.roll(c, 96, axis), d),
    )
    return a, b, c, d


def border_copies(gx, gy, source, target, send_sem, recv_sem):
    copies = [
        pltpu.make_async_remote_copy(
            src_ref=source.at[first:last],
            dst_ref=target.at[first:last],
            send_sem=send_sem,
            recv_sem=recv_sem,
            device_id=(mod(gx + dr, GX), mod(gy + dc, GY)),
            device_id_type=MESH,
        )
        for (dr, dc), (first, last) in zip(DIRS, PARTS)
    ]
    whole = pltpu.make_async_remote_copy(
        src_ref=source,
        dst_ref=target,
        send_sem=send_sem,
        recv_sem=recv_sem,
        device_id=(mod(gx + 1, GX), gy),
        device_id_type=MESH,
    )
    return copies, whole


def fused_body(
    mid_hbm, grad_hbm, w_hbm, routes_hbm, gates_hbm, band_hbm, ids_hbm,
    col_hbm, col_t_hbm, edge_hbm, row_hbm, back_hbm,
    out,
    routes, gates, band_ids, mid, grad, w, row, back, band, col, col_t, edge_table, shifted, side, deltas, last_pre, spread, total, edge, edges, left_edge,
    border_out, border_in, halo_out, halo_in,
    xs, xr, half, cs, cr, cg, sp, zs, fs, fr,
    w_sem, in_sem, halo_s, halo_r, border_s, border_r,
    x_s, x_r, c_s, c_r, g_s, g_r, p_s, p_r, f_s, f_r,
):
    gx, gy = lax.axis_index("gx"), lax.axis_index("gy")
    w_copies = [
        pltpu.make_async_copy(w_hbm.at[first:last], w.at[first:last], w_sem.at[k])
        for k, (first, last) in enumerate(((0, 1), (1, 2), (2, EXPERTS)))
    ]
    sources = [
        mid_hbm, grad_hbm, row_hbm.at[gx], back_hbm.at[gx],
        band_hbm.at[:, pl.ds(pl.multiple_of(gy * 32, 32), 32), :],
        col_hbm, col_t_hbm, edge_hbm, ids_hbm, routes_hbm, gates_hbm,
    ]
    targets = [mid, grad, row, back, band, col, col_t, edge_table, band_ids, routes, gates]
    in_copies = [
        pltpu.make_async_copy(source, target, in_sem.at[k])
        for k, (source, target) in enumerate(zip(sources, targets))
    ]
    in_copies[0].start()
    barrier = pltpu.get_barrier_semaphore()
    partners = [(mod(gx + dr, GX), mod(gy + dc, GY)) for dr, dc in DIRS]
    partners += [(mod(gx + d, GX), gy) for d in range(2, GX - 1)]
    partners += [(gx, mod(gy + d, GY)) for d in range(2, GY - 1)]
    for device in partners:
        pl.semaphore_signal(barrier, inc=1, device_id=device, device_id_type=MESH)

    above = jnp.where(gx > 0, 1.0, 0.0)
    below = jnp.where(gx < GX - 1, 1.0, 0.0)
    left = jnp.where(gy > 0, 1.0, 0.0)
    right = jnp.where(gy < GY - 1, 1.0, 0.0)

    in_copies[0].wait()
    halo_out[0:32] = mid[ROWS - 1]
    halo_out[32:64] = mid[0]
    rim = [mid[:, 16:32, :].astype(F32)[:, 15, :], mid[:, 0:16, :].astype(F32)[:, 0, :]]
    halo_out[64:112] = rim[0].astype(BF)
    halo_out[112:160] = rim[1].astype(BF)
    for k, r in enumerate((ROWS - 1, ROWS - 1, 0, 0)):
        corner = jnp.broadcast_to(rim[k % 2][r : r + 1], (16, CH)).astype(BF)
        halo_out[160 + 16 * k : 176 + 16 * k] = corner
    pl.semaphore_wait(barrier, len(partners))
    halo, halo_all = border_copies(gx, gy, halo_out, halo_in, halo_s.at[0], halo_r.at[0])
    for copy in halo:
        copy.start()
    for copy in in_copies[1:2] + w_copies[:1] + in_copies[9:] + w_copies[1:] + in_copies[2:9]:
        copy.start()
    in_copies[1].wait()
    for b in (0, 2):
        spread[b] = jnp.zeros((OPEN, COLS, CH), F32)
    spread[1, 0] = jnp.zeros((COLS, CH), F32)
    spread[1, 1 : ROWS + 1] = grad[...].astype(F32)
    spread[1, ROWS + 1 :] = jnp.zeros((OPEN - ROWS - 1, COLS, CH), F32)
    edges[...] = jnp.zeros_like(edges)
    last_pre[...] = jnp.zeros_like(last_pre)
    place = lax.broadcasted_iota(jnp.int32, (COLS, CH), 0)

    def shift_row(r, line):
        shifted[1, r] = line.astype(BF)
        shifted[0, r] = pltpu.roll(line, 1, 0).astype(BF)
        shifted[2, r] = pltpu.roll(line, COLS - 1, 0).astype(BF)

    def own_shift(r, _):
        shift_row(r + 1, mid[r].astype(F32))
        return 0

    lax.fori_loop(0, ROWS, own_shift, 0, unroll=4)
    halo_all.wait()
    shift_row(0, halo_in[0:32].astype(F32) * above)
    shift_row(ROWS + 1, halo_in[32:64].astype(F32) * below)
    side[0, 8 : 8 + ROWS] = halo_in[64:112].astype(F32) * left
    side[1, 8 : 8 + ROWS] = halo_in[112:160].astype(F32) * right
    side[0, 7:8] = halo_in[160:176].astype(F32)[0:1] * (above * left)
    side[1, 7:8] = halo_in[176:192].astype(F32)[0:1] * (above * right)
    side[0, 8 + ROWS : 9 + ROWS] = halo_in[192:208].astype(F32)[0:1] * (below * left)
    side[1, 8 + ROWS : 9 + ROWS] = halo_in[208:224].astype(F32)[0:1] * (below * right)
    place16 = lax.broadcasted_iota(jnp.int32, (16, CH), 0)

    def fix_row(r, _):
        before = side[0, pl.ds(r + 7, 1), :]
        after = side[1, pl.ds(r + 7, 1), :]
        first = shifted[0, r, 0:16, :].astype(F32)
        shifted[0, r, 0:16, :] = jnp.where(place16 == 0, before, first).astype(BF)
        last = shifted[2, r, 16:32, :].astype(F32)
        shifted[2, r, 16:32, :] = jnp.where(place16 == 15, after, last).astype(BF)
        return 0

    lax.fori_loop(0, ROWS + 2, fix_row, 0, unroll=5)

    def expert(t, s):
        return routes[t // 2, t % 2, s - 2] + 2

    def slope(t, s, pre, low=0, high=16):
        top = (t // 2) * 16
        cols = slice((t % 2) * 16, (t % 2) * 16 + 16)
        g = grad[top + low : top + high, cols, :].reshape(-1, CH).astype(F32)
        gate = gates[t // 2, t % 2, s] * 0.5
        values = (gelu_slope_twice(pre) * (g * gate)).astype(BF)
        deltas[t, s, low * 16 : high * 16] = values

    def forward(s, kernel_of):
        for t in range(TILES):
            top = (t // 2) * 16
            cols = slice((t % 2) * 16, (t % 2) * 16 + 16)
            for low in (0, 8):
                pieces = [
                    shifted[b, top + low + a : top + low + a + 8, cols, :].reshape(128, CH)
                    for a in range(3)
                    for b in range(3)
                ]
                pre = jnp.dot(
                    jnp.concatenate(pieces, axis=1), w[kernel_of(t, s)], preferred_element_type=F32
                )
                if t == 0 and low == 0:
                    slope(TILES - 1, jnp.maximum(s - 1, 0), last_pre[...], 8)
                if t < TILES - 1 or low == 0:
                    slope(t, s, pre, low, low + 8)
                else:
                    last_pre[...] = pre

    def forward_shared(s, _):
        forward(s, lambda t, s: s)
        return 0

    def forward_routed(s, _):
        forward(s, expert)
        return 0

    w_copies[0].wait()
    w_copies[1].wait()
    in_copies[9].wait()
    in_copies[10].wait()
    lax.fori_loop(0, 2, forward_shared, 0)
    w_copies[2].wait()
    lax.fori_loop(2, SLOTS, forward_routed, 0)
    slope(TILES - 1, SLOTS - 1, last_pre[...], 8)

    def along_y(source, target, d, send, recv):
        return pltpu.make_async_remote_copy(
            src_ref=source, dst_ref=target, send_sem=send, recv_sem=recv,
            device_id=(gx, mod(gy + d, GY)), device_id_type=MESH,
        )

    def along_x(source, target, d, send, recv):
        return pltpu.make_async_remote_copy(
            src_ref=source, dst_ref=target, send_sem=send, recv_sem=recv,
            device_id=(mod(gx + d, GX), gy), device_id_type=MESH,
        )

    def x_rows(rt, half):
        _, groups, start = CHUNKS[rt]
        at = start + groups * 16
        return slice(at, start + groups * 32 + 16) if half else slice(start, at)

    def opened(r, half):
        if half == 0:
            middle = jnp.where(place16 >= 1, pltpu.roll(spread[1, r, 0:16, :], 1, 0), 0.0)
            ahead = jnp.where(place16 >= 2, pltpu.roll(spread[2, r, 0:16, :], 2, 0), 0.0)
            return spread[0, r, 0:16, :] + middle + ahead
        middle = pltpu.roll(spread[1, r, 8:32, :], 1, 0)[8:24]
        ahead = pltpu.roll(spread[2, r, 8:32, :], 2, 0)[8:24]
        return spread[0, r, 16:32, :] + middle + ahead

    def leave(rt, half):
        first, groups, start = CHUNKS[rt]
        base = start + half * groups * 16

        def split_group(k, _):
            lines = [opened(4 * (first + k) + q, half) for q in range(4)]
            for jt in range(2):
                lanes = slice(jt * 128, jt * 128 + 128)
                for s, part in enumerate(transpose_blocks([line[:, lanes] for line in lines])):
                    xs[jt * 4 + s, pl.ds(pl.multiple_of(base + 16 * k, 16), 16), :] = part.astype(BF)
            return 0

        lax.fori_loop(0, groups, split_group, 0, unroll=groups)
        if half:
            rows = slice(4 * first, 4 * first + 4 * groups)
            last = start + groups * 32
            for jt in range(2):
                lanes = slice(jt * 128, jt * 128 + 128)
                edge[0, jt, rows] = (
                    spread[1, rows, COLS - 1, lanes] + spread[2, rows, COLS - 2, lanes]
                )
                edge[1, jt, rows] = spread[2, rows, COLS - 1, lanes]
                for q in range(4):
                    for s in range(2):
                        edges[q, jt, s * 8 : s * 8 + groups] = edge[
                            s, jt, pl.ds(4 * first + q, groups, stride=4), :
                        ]
                for s, part in enumerate(transpose_blocks([edges[q, jt] for q in range(4)])):
                    xs[jt * 4 + s, last : last + 16, :] = part.astype(BF)
        rows = x_rows(rt, half)
        for d in AHEAD_Y:
            along_y(
                xs.at[mod(gy + d, GY), rows], xr.at[gy, rows], d,
                x_s.at[2 * rt + half], x_r.at[2 * rt + half],
            ).start()

    for rt in range(3):

        def backward(ct, _):
            cols = pl.ds(pl.multiple_of(ct * 16, 16), 16)
            d = jnp.concatenate([deltas[2 * rt + ct, s] for s in range(SLOTS)], axis=1)
            chosen = [0, 1] + [routes[rt, ct, s - 2] + 2 for s in range(2, SLOTS)]
            for a in range(3):
                for b in range(3):
                    tap = 3 * a + b
                    kernels = jnp.concatenate(
                        [w[e, tap * CH : (tap + 1) * CH, :] for e in chosen], axis=1
                    )
                    r = lax.dot_general(
                        d, kernels, (((1,), (1,)), ((), ())), preferred_element_type=F32
                    )
                    spread[b, rt * 16 + a : rt * 16 + a + 16, cols, :] += r.reshape(16, 16, CH)

            @pl.when(ct == 0)
            def _():
                leave(rt, 0)

            @pl.when(ct == 1)
            def _():
                leave(rt, 1)

            return 0

        lax.fori_loop(0, 2, backward, 0)

    def own_row(r, _):
        ahead = jnp.where(place > 0, pltpu.roll(spread[2, r], 1, 0), 0.0)
        behind = jnp.where(place < COLS - 1, pltpu.roll(spread[0, r], COLS - 1, 0), 0.0)
        total[r] = spread[1, r] + ahead + behind
        return 0

    lax.fori_loop(0, ROWS + 2, own_row, 0, unroll=5)
    border_out[0:32] = total[ROWS + 1].astype(BF)
    border_out[32:64] = total[0].astype(BF)
    for jt in range(2):
        lanes = slice(jt * 128, jt * 128 + 128)
        left_edge[jt, 0 : ROWS + 2] = spread[0, 0 : ROWS + 2, 0, lanes]
        border_out[64:112, lanes] = edge[1, jt, 1 : ROWS + 1].astype(BF)
        border_out[112:160, lanes] = left_edge[jt, 1 : ROWS + 1].astype(BF)
        for k, r in enumerate((ROWS + 1, ROWS + 1, 0, 0)):
            corner = left_edge[jt, r : r + 1, :] if k % 2 else edge[1, jt, r : r + 1, :]
            border_out[160 + 16 * k : 176 + 16 * k, lanes] = jnp.broadcast_to(
                corner, (16, 128)
            ).astype(BF)
    border, border_all = border_copies(
        gx, gy, border_out, border_in, border_s.at[0], border_r.at[0]
    )
    for copy in border:
        copy.start()
    xr[gy] = xs[gy]

    for copy in in_copies[2:9]:
        copy.wait()
    for chunk, (first, groups, start) in enumerate(CHUNKS):
        for part in range(2):
            rows = x_rows(chunk, part)
            t = 2 * chunk + part
            along_y(xs.at[1:GY, rows], xr.at[1:GY, rows], 1, x_s.at[t], x_r.at[t]).wait()
        last = start + groups * 32
        rim = jnp.dot(
            edge_table[0 : groups * 64],
            xr[:, last : last + 16].reshape(128, 128),
            preferred_element_type=F32,
        )
        for pair in range(0, groups, 2):
            width = min(2, groups - pair)
            data = []
            for k in range(pair, pair + width):
                halves = [start + 16 * (groups * part + k) for part in range(2)]
                halves = [xr[:, at : at + 16].reshape(128, 128) for at in halves]
                data.append(jnp.concatenate(halves, axis=0))
            c = jnp.dot(col[...], jnp.concatenate(data, axis=1), preferred_element_type=F32)
            for k in range(width):
                one = c[:, k * 128 : k * 128 + 128] + rim[(pair + k) * 64 : (pair + k) * 64 + 64]
                for part in range(2):
                    parts = [one[part * 32 + 8 * p : part * 32 + 8 * p + 8] for p in range(4)]
                    for q, block in enumerate(transpose_blocks(parts)):
                        r = part * OPEN + 4 * (first + pair + k) + q
                        half[pl.ds(r, 8, stride=2 * OPEN), :] = block
    forward_scale = 1.0 / math.sqrt(H * W)
    for pair in range(4):
        data = [
            half[(2 * pair + k) * 2 * OPEN : (2 * pair + k + 1) * 2 * OPEN].astype(BF)
            for k in range(2)
        ]
        c = jnp.dot(row[...], jnp.concatenate(data, axis=1), preferred_element_type=F32)
        c = (c * forward_scale).astype(BF)
        for k in range(2):
            for mh in range(2):
                cs[mh * 8 + 2 * pair + k] = c[mh * 64 : mh * 64 + 64, k * 128 : k * 128 + 128]
    halves_of = [slice(0, 32), slice(32, 64)]
    parts_of = [slice(16 * k, 16 * k + 16) for k in range(PIECES)]

    def c_copy(part, source, target, d=1):
        rows = parts_of[part]
        return along_x(cs.at[source, rows], cr.at[target, rows], d, c_s.at[part], c_r.at[part])

    def g_copy(part, source, target, d=1):
        rows = parts_of[part]
        return along_y(cg.at[source, rows], cg.at[target, rows], d, g_s.at[part], g_r.at[part])

    def p_copy(part, source, target, d=1):
        rows = halves_of[part]
        return along_x(sp.at[source, rows], sp.at[target, rows], d, p_s.at[part], p_r.at[part])

    others_x, others_y = slice(1, GX), slice(1, GY)
    for part in range(PIECES):
        for d in AHEAD_X:
            c_copy(part, mod(gx + d, GX), gx, d).start()
    cr[gx] = cs[gx]

    border_all.wait()
    total[1] += border_in[0:32].astype(F32) * above
    total[ROWS] += border_in[32:64].astype(F32) * below
    own = slice(1, ROWS + 1)
    total[own, 0, :] += border_in[64:112].astype(F32) * left
    total[own, COLS - 1, :] += border_in[112:160].astype(F32) * right
    total[1, 0:1, :] += border_in[160:176].astype(F32)[0:1] * (above * left)
    total[1, COLS - 1 : COLS, :] += border_in[176:192].astype(F32)[0:1] * (above * right)
    total[ROWS, 0:1, :] += border_in[192:208].astype(F32)[0:1] * (below * left)
    total[ROWS, COLS - 1 : COLS, :] += border_in[208:224].astype(F32)[0:1] * (below * right)

    n8 = lax.rem(gx, 8)
    mh = gx // 8
    lane64 = lax.broadcasted_iota(jnp.int32, (32, KH), 1)
    row64 = lax.broadcasted_iota(jnp.int32, (32, KH), 0)
    block_of_lane = lax.broadcasted_iota(jnp.int32, (32, 512), 1) >> 5
    lane_block = lax.broadcasted_iota(jnp.int32, (32, 128), 1) >> 5
    band_of = []
    for n4 in range(4):
        ids = jnp.broadcast_to(band_ids[pl.ds(4 * n8 + n4, 1), :], (32, KH))
        band_of.append(jnp.sum(jnp.where(lane64 == row64 + 32 * mh, ids, 0), axis=1, keepdims=True))

    for part in range(PIECES):
        rows = parts_of[part]
        c_copy(part, others_x, others_x).wait()
        coef = cr[0, rows].astype(F32)
        for k in range(1, GX):
            coef = coef + cr[k, rows].astype(F32)
        cg[gy, rows] = coef.astype(BF)
        for d in AHEAD_Y:
            g_copy(part, gy, gy, d).start()

    mixer = band[...].reshape(512, CH)
    for part in range(2):
        rows = halves_of[part]
        for piece in range(part * PIECES // 2, (part + 1) * PIECES // 2):
            g_copy(piece, others_y, others_y).wait()
        inputs = [
            transpose_blocks([cg[jt * 4 + p, rows].astype(F32) for p in range(4)])
            for jt in range(2)
        ]
        spec = jnp.zeros((32, 128), F32)
        modes = [
            jnp.concatenate([inputs[0][n4], inputs[1][n4]], axis=1).astype(BF) for n4 in range(4)
        ]
        mixed = lax.dot_general(
            jnp.concatenate(modes, axis=0), mixer, (((1,), (1,)), ((), ())),
            preferred_element_type=F32,
        )
        for n4 in range(4):
            z = jnp.where(block_of_lane == band_of[n4], mixed[n4 * 32 : n4 * 32 + 32], 0.0)
            y = z[:, 0:128] + z[:, 128:256] + z[:, 256:384] + z[:, 384:512]
            y = y + pltpu.roll(y, 64, 1)
            y = y + pltpu.roll(y, 32, 1)
            spec = jnp.where(lane_block == n4, y, spec)
        sp[gx, rows] = spec.astype(BF)
        for d in AHEAD_X:
            p_copy(part, gx, gx, d).start()
    for part in range(2):
        p_copy(part, others_x, others_x).wait()

    inverse_scale = 1.0 / math.sqrt(2 * KH * KW)
    for pair in range(4):
        data = [
            jnp.concatenate([sp[2 * pair + k], sp[8 + 2 * pair + k]], axis=0) for k in range(2)
        ]
        z = jnp.dot(back[...], jnp.concatenate(data, axis=1), preferred_element_type=F32)
        z = z * inverse_scale
        for k in range(2):
            zs[(2 * pair + k) * 96 : (2 * pair + k + 1) * 96, :] = z[:, k * 128 : k * 128 + 128]

    def f_copy(sixth, source, target, d=1):
        rows = slice(2 * sixth, 2 * sixth + 2)
        return along_y(fs.at[source, rows], fr.at[target, rows], d, f_s.at[sixth], f_r.at[sixth])

    for sixth in range(6):
        for pair in (sixth,):
            columns = []
            for k in range(2):
                pieces = []
                for part in range(2):
                    r = part * ROWS + 4 * (2 * pair + k)
                    parts = [zs[pl.ds(r + q, 8, stride=2 * ROWS), :] for q in range(4)]
                    pieces += list(transpose_blocks(parts))
                columns.append(jnp.concatenate(pieces, axis=0))
            data = jnp.concatenate(columns, axis=1).astype(BF)
            f = jnp.dot(col_t[...], data, preferred_element_type=F32).astype(BF)
            for k in range(2):
                for j in range(GY):
                    fs[j, 2 * pair + k] = f[j * 32 : j * 32 + 32, k * 128 : k * 128 + 128]
        for d in AHEAD_Y:
            f_copy(sixth, mod(gy + d, GY), gy, d).start()
    fr[gy] = fs[gy]

    def join_group(g, _):
        for jt in range(2):
            lanes = slice(jt * 128, jt * 128 + 128)
            parts = [fr[jt * 4 + s, g].astype(F32) for s in range(4)]
            for q, part in enumerate(transpose_blocks(parts)):
                out[4 * g + q, :, lanes] = (total[4 * g + q + 1, :, lanes] + part).astype(BF)
        return 0

    for sixth in range(6):
        f_copy(sixth, others_y, others_y).wait()
        lax.fori_loop(2 * sixth, 2 * sixth + 2, join_group, 0, unroll=2)


ANY = pl.BlockSpec(memory_space=pl.ANY)


def dma(*shape):
    return pltpu.SemaphoreType.DMA(shape)


def body(saved_mid, out_grad, expert_weight, routes, gates, band_matrix, band_ids):
    return pl.pallas_call(
        fused_body,
        name="fused",
        out_shape=pltpu.VMEM((ROWS, COLS, CH), BF),
        in_specs=[ANY, ANY, ANY, ANY, ANY, ANY, ANY, ANY, ANY, ANY, ANY, ANY],
        out_specs=pl.BlockSpec(memory_space=pltpu.VMEM),
        scratch_shapes=[
            pltpu.SMEM((3, 2, 4), jnp.int32),
            pltpu.SMEM((3, 2, SLOTS), F32),
            pltpu.VMEM((KW, KH), jnp.int32),
            pltpu.VMEM((ROWS, COLS, CH), BF),
            pltpu.VMEM((ROWS, COLS, CH), BF),
            pltpu.VMEM((EXPERTS, 9 * CH, CH), BF),
            pltpu.VMEM((128, 2 * OPEN), BF),
            pltpu.VMEM((2 * ROWS, 128), BF),
            pltpu.VMEM((16, 32, CH), BF),
            pltpu.VMEM((64, 256), BF),
            pltpu.VMEM((256, 64), BF),
            pltpu.VMEM((320, 128), BF),
            pltpu.VMEM((3, ROWS + 2, COLS, CH), BF),
            pltpu.VMEM((2, 64, CH), F32),
            pltpu.VMEM((TILES, SLOTS, 256, CH), BF),
            pltpu.VMEM((128, CH), F32),
            pltpu.VMEM((3, OPEN, COLS, CH), F32),
            pltpu.VMEM((OPEN, COLS, CH), F32),
            pltpu.VMEM((2, 2, OPEN + 4, 128), F32),
            pltpu.VMEM((4, 2, 16, 128), F32),
            pltpu.VMEM((2, OPEN + 4, 128), F32),
            *[pltpu.VMEM((224, CH), BF)] * 4,
            pltpu.VMEM((GY, 464, 128), BF),
            pltpu.VMEM((GY, 464, 128), BF),
            pltpu.VMEM((8 * 2 * OPEN, 128), F32),
            pltpu.VMEM((GX, 64, 128), BF),
            pltpu.VMEM((GX, 64, 128), BF),
            pltpu.VMEM((GY, 64, 128), BF),
            pltpu.VMEM((GX, 64, 128), BF),
            pltpu.VMEM((8 * 2 * ROWS, 128), F32),
            pltpu.VMEM((GY, 12, 32, 128), BF),
            pltpu.VMEM((GY, 12, 32, 128), BF),
            dma(3), dma(11), dma(1), dma(1), dma(1), dma(1),
            dma(6), dma(6), *[dma(PIECES)] * 4, dma(2), dma(2), dma(6), dma(6),
        ],
        compiler_params=pltpu.CompilerParams(
            collective_id=0, has_side_effects=True, vmem_limit_bytes=66_000_000
        ),
    )(
        saved_mid, out_grad, expert_weight.reshape(EXPERTS, 9 * CH, CH), routes, gates,
        band_matrix, band_ids.T, jnp.asarray(OPEN_TABLE, BF), jnp.asarray(COL_TABLE, BF),
        jnp.asarray(EDGE_TABLE, BF), jnp.asarray(ROW_TABLE, BF), jnp.asarray(BACK_TABLE, BF),
    )


def solution(mesh):
    placed = (
        P("gx", "gy", None),
        P("gx", "gy", None),
        P(),
        P("gx", "gy", None),
        P("gx", "gy", None),
        P(),
        P(),
    )
    return jax.shard_map(
        body, mesh=mesh, in_specs=placed, out_specs=P("gx", "gy", None), check_vma=False
    )
```
